32 devices in a mesh: dp: 8 (over z, y), seq: 4 (over x, core).
Axes of the slice: x: 2, y: 2, z: 4, core: 2. Of those that a mesh axis runs over, the one named last changes fastest.
Arguments:
- hidden: bfloat16 [2, 8, 1024, 1536], P(None, 'dp', 'seq'), may hold values from -6 to 6
- in_weight: bfloat16 [1536, 6448], P(('dp', 'seq')), may hold values from -0.15625 to 0.15625
- out_weight: bfloat16 [3072, 1536], P(('dp', 'seq')), may hold values from -0.109375 to 0.109375
- conv_weight: bfloat16 [3328, 4], P(('dp', 'seq')), may hold values from -3 to 3
- conv_bias: bfloat16 [3328], P(('dp', 'seq')), may hold values from -3 to 3
- norm_gain: bfloat16 [1536], P(('dp', 'seq')), may hold values from 0.099609375 to 1.8984375
- gate_gain: bfloat16 [3072], P(('dp', 'seq')), may hold values from 0.099609375 to 1.8984375
- step_bias: float32 [48], replicated, may hold values from -4 to -1
- decay_rate: float32 [48], replicated, may hold values from 0.00048828125 to 1
- skip_gain: float32 [48], replicated, may hold values from 0.5 to 2
- cotangent: bfloat16 [2, 8, 1024, 1536], P(None, 'dp', 'seq'), may hold values from -6 to 6
Outputs:
- block_out: bfloat16 [2, 8, 1024, 1536], P(None, 'dp', 'seq')
- grad_hidden: float32 [2, 8, 1024, 1536], P(None, 'dp', 'seq')
- grad_in_weight: float32 [1536, 6448], P(('dp', 'seq'))
- grad_out_weight: float32 [3072, 1536], P(('dp', 'seq'))
- grad_conv_weight: float32 [3328, 4], P(('dp', 'seq'))
- grad_conv_bias: float32 [3328], P(('dp', 'seq'))
- grad_norm_gain: float32 [1536], P(('dp', 'seq'))
- grad_gate_gain: float32 [3072], P(('dp', 'seq'))
- grad_step_bias: float32 [48], replicated
- grad_decay_rate: float32 [48], replicated
- grad_skip_gain: float32 [48], replicated
The draws below stay inside these ranges and needn't reach their ends.
All inputs are finite; a program needn't handle non-finite values.
Results may differ from the reference program's by a relative error of at most 0.008.
The reference program's roundings to bfloat16 on the way count: a program that leaves them out, or rounds other values in their place, can miss the bound.
Values may be sent and summed in bfloat16 or wider, within the bound.
No kernel may reach another device: no remote copies, remote signals or barrier semaphores. Data moves between devices by JAX's collectives and lax.ppermute only.
A program may use at most 320 MiB of HBM per device.

```python
import math
import jax
import jax.numpy as jnp
from jax import lax

D = 1536
DI = 3072
H = 48
P_SIZE = 64
N = 128
KCONV = 4
GROUP = 256
MB = 2
CONV = 3328
NPROJ = 6448
SEQS = 8
LEN = 1024


def steps_of(rng, shape, shards, smallest, largest):
    loudness = 1.0
    for axis_at, shards_of in shards:
        steps = jax.random.uniform(jax.random.fold_in(jax.random.fold_in(rng, 6), axis_at), (shards_of,), jnp.float32, smallest / len(shards), largest / len(shards))
        loudness = loudness * jnp.repeat(jnp.exp(steps), shape[axis_at] // shards_of).reshape((-1,) + (1,) * (len(shape) - 1 - axis_at))
    return loudness


def noise(key, shape, spread, bound, cuts=(), kind=jnp.bfloat16):
    result = jax.random.normal(key, shape, jnp.float32) * spread
    if len(cuts) > 0:
        result = steps_of(key, shape, cuts, -0.22, 0.18) * result
    return jnp.clip(result, min=-bound, max=bound).astype(kind)


def setup_inputs(seed: int = 0) -> dict:
    splits = jax.random.split(jax.random.key(seed), 12)
    return {
        "hidden": noise(splits[0], (MB, SEQS, LEN, D), 1.0, 6.0, ((1, 8), (2, 4))),
        "in_weight": noise(splits[1], (D, NPROJ), D ** -0.5, 0.15625, ((0, 32),)),
        "out_weight": noise(splits[2], (DI, D), DI ** -0.5, 0.109375, ((0, 32),)),
        "conv_weight": noise(splits[3], (CONV, KCONV), KCONV ** -0.5, 3.0, ((0, 32),)),
        "conv_bias": noise(splits[4], (CONV,), 0.5, 3.0, ((0, 32),)),
        "norm_gain": jnp.clip(1.0 + 0.18 * jax.random.normal(splits[5], (D,), jnp.float32), 0.099609375, 1.8984375).astype(jnp.bfloat16),
        "gate_gain": jnp.clip(1.0 + 0.18 * jax.random.normal(splits[6], (DI,), jnp.float32), 0.099609375, 1.8984375).astype(jnp.bfloat16),
        "step_bias": jnp.clip(jax.random.uniform(splits[7], (H,), jnp.float32, -4.0, -1.0), -4.0, -1.0),
        "decay_rate": jnp.clip(jnp.exp(jax.random.uniform(splits[8], (H,), jnp.float32, math.log(0.00048828125), math.log(1.0))), 0.00048828125, 1.0),
        "skip_gain": jnp.clip(jax.random.uniform(splits[9], (H,), jnp.float32, 0.5, 2.0), 0.5, 2.0),
        "cotangent": noise(splits[10], (MB, SEQS, LEN, D), 1.0, 6.0, ((1, 8), (2, 4))),
    }


epsilon = 1e-05
highest = lax.Precision.HIGHEST

@jax.custom_vjp
def low(v):
    return lax.optimization_barrier(v.astype(jnp.bfloat16)).astype(jnp.float32)

@jax.custom_vjp
def low_back(v):
    return v

def low_keep(v):
    return (low(v), None)

def low_pass(kept, grad):
    return (grad,)

def back_keep(v):
    return (v, None)

def back_low(kept, grad):
    return (low(grad),)
low.defvjp(low_keep, low_pass)
low_back.defvjp(back_keep, back_low)

def rms_scale(values, gain_vec):
    return values * lax.rsqrt(lax.optimization_barrier(jnp.mean(values * values, axis=-1, keepdims=True)) + epsilon) * gain_vec

def convolve(padded, conv_taps, conv_shift, block_rows):
    summed = conv_shift
    for tap_index in range(conv_taps.shape[1]):
        summed = summed + conv_taps[:, tap_index] * padded[..., tap_index:tap_index + block_rows, :]
    return summed

def split_parts(act, dt_raw, step_bias, decay_rate):
    x_heads = act[..., :DI].reshape(act.shape[:-1] + (H, P_SIZE))
    b_state = act[..., DI:DI + N]
    c_state = act[..., DI + N:]
    dt_step = jax.nn.softplus(dt_raw + step_bias)
    log_decay = jnp.cumsum(-decay_rate * dt_step, axis=-2)
    return (x_heads, b_state, c_state, dt_step, log_decay)

def group_states(x_heads, b_state, dt_step, log_decay):
    tail_weights = jnp.exp(log_decay[:, -1:, :] - log_decay) * dt_step
    weighted = x_heads * tail_weights[..., None]
    states = jnp.einsum('sun,suhp->shnp', b_state, weighted, precision=highest)
    return (jnp.exp(log_decay[:, -1, :]), states)

def group_outputs(gate_z, x_heads, b_state, c_state, dt_step, log_decay, entering, gate_vec, skip_gain):
    block_count, block_rows = (x_heads.shape[0], x_heads.shape[1])
    scores = jnp.einsum('stn,sun->stu', c_state, b_state, precision=highest)
    decay_heads = jnp.transpose(log_decay, (0, 2, 1))
    log_diff = decay_heads[:, :, :, None] - decay_heads[:, :, None, :]
    causal = lax.broadcasted_iota(jnp.int32, (block_rows, block_rows), 0) >= lax.broadcasted_iota(jnp.int32, (block_rows, block_rows), 1)
    decay_mat = jnp.exp(jnp.where(causal, log_diff, -jnp.inf))
    mixing = decay_mat * scores[:, None, :, :] * jnp.transpose(dt_step, (0, 2, 1))[:, :, None, :]
    inner_sum = jnp.einsum('shtu,suhp->sthp', mixing, x_heads, precision=highest)
    carried = jnp.einsum('stn,shnp->sthp', c_state, entering, precision=highest) * jnp.exp(log_decay)[..., None]
    ssd_sum = inner_sum + carried + skip_gain[:, None] * x_heads
    flat_ssd = ssd_sum.reshape(block_count, block_rows, DI)
    gated = flat_ssd * jax.nn.silu(gate_z)
    return rms_scale(gated, gate_vec)

def one_sequence(sequence, in_w, out_w, conv_taps, conv_shift, norm_vec, gate_vec, step_bias, decay_rate, skip_gain):
    normed = low(rms_scale(sequence, norm_vec))
    projected = low_back(jnp.dot(normed, in_w, precision=highest))
    xbc_part = projected[:, DI:DI + CONV]
    padded = jnp.concatenate([jnp.zeros((KCONV - 1, CONV), jnp.float32), xbc_part], axis=0)
    act = jax.nn.silu(convolve(padded, conv_taps, conv_shift, LEN))
    blocks = LEN // GROUP
    act = act.reshape(blocks, GROUP, CONV)
    dt_raw = projected[:, DI + CONV:].reshape(blocks, GROUP, H)
    x_heads, b_state, c_state, dt_step, log_decay = split_parts(act, dt_raw, step_bias, decay_rate)
    decays, states = group_states(x_heads, b_state, dt_step, log_decay)

    def carry_step(held_state, block_item):
        return (block_item[0][:, None, None] * held_state + block_item[1], held_state)
    _, entering = lax.scan(carry_step, jnp.zeros((H, N, P_SIZE), jnp.float32), (decays, states))
    gate_z = projected[:, :DI].reshape(blocks, GROUP, DI)
    finished = group_outputs(gate_z, x_heads, b_state, c_state, dt_step, log_decay, entering, gate_vec, skip_gain)
    finished = low(finished.reshape(LEN, DI))
    return sequence + jnp.dot(finished, out_w, precision=highest)

def reference(hidden, in_weight, out_weight, conv_weight, conv_bias, norm_gain, gate_gain, step_bias, decay_rate, skip_gain, cotangent):
    params = (in_weight.astype(jnp.float32), out_weight.astype(jnp.float32), conv_weight.astype(jnp.float32), conv_bias.astype(jnp.float32), norm_gain.astype(jnp.float32), gate_gain.astype(jnp.float32), step_bias, decay_rate, skip_gain)
    inputs_f = hidden.astype(jnp.float32).reshape(MB * SEQS, LEN, D)

    def forward(inputs_all, *weights_all):

        def single(sequence):
            return one_sequence(sequence, *weights_all)
        return lax.map(jax.checkpoint(single), inputs_all)
    outputs, pullback = jax.vjp(forward, inputs_f, *params)
    gradients = pullback(cotangent.astype(jnp.float32).reshape(MB * SEQS, LEN, D))
    return (outputs.astype(jnp.bfloat16).reshape(hidden.shape), gradients[0].reshape(hidden.shape), gradients[1], gradients[2], gradients[3], gradients[4], gradients[5], gradients[6], gradients[7], gradients[8], gradients[9])
```

```python
import functools

import jax
import jax.numpy as jnp
import numpy as np
from jax import lax
from jax.experimental import pallas as pl
from jax.experimental.pallas import tpu as pltpu
from jax.sharding import Mesh
from jax.sharding import PartitionSpec as P

DI = 3072
H = 48
PS = 64
N = 128
KC = 4
CONV = 3328
D = 1536
T = 256
HH = H // 2
W = DI // 2
XC = W + 2 * N
XP = XC + 128
EPS = 1e-05
NEG = -1e30
f32 = jnp.float32
bf16 = jnp.bfloat16
HIGH = lax.Precision.HIGHEST
ALL = ("za", "zb", "zl", "s", "c")
Z = ("za", "zb")
MB_ = 1 << 20


def nn(a, b):
    return lax.dot_general(a, b, (((1,), (0,)), ((), ())), preferred_element_type=f32)


def nt(a, b):
    return lax.dot_general(a, b, (((1,), (1,)), ((), ())), preferred_element_type=f32)


def tn(a, b):
    return lax.dot_general(a, b, (((0,), (0,)), ((), ())), preferred_element_type=f32)


def halves(v):
    high = v.astype(bf16)
    return high, (v - high.astype(f32)).astype(bf16)


def fine(dot, a, b):
    (ah, al), (bh, bl) = halves(a), halves(b)
    return dot(ah, bh) + (dot(ah, bl) + dot(al, bh))


def iota(shape, dim):
    return lax.broadcasted_iota(jnp.int32, shape, dim)


def spread(cols, first, heads):
    rows = cols.shape[0]
    head = iota((rows, heads * PS), 1) // PS
    out = jnp.broadcast_to(cols[:, first : first + 1], (rows, heads * PS))
    for i in range(1, heads):
        out = jnp.where(head == i, cols[:, first + i : first + i + 1], out)
    return out


def per_head(values, first):
    lanes = values.shape[1]
    place = (iota((lanes, 128), 0) // PS + first == iota((lanes, 128), 1)).astype(bf16)
    high, low = halves(values)
    return nn(high, place) + nn(low, place)


def row_sum(values):
    return jnp.sum(values, axis=0, keepdims=True)


def conv_taps(pad_ref, cw_ref, lanes):
    total = cw_ref[4:5, lanes]
    for k in range(KC):
        total = total + cw_ref[k : k + 1, lanes] * pad_ref[pl.ds(5 + k, T), lanes]
    return total


def softplus(v):
    return jnp.maximum(v, 0.0) + jnp.log1p(jnp.exp(-jnp.abs(v)))


def params(**kw):
    return pltpu.CompilerParams(vmem_limit_bytes=40 * MB_, **kw)


def cost(flops, nbytes, trans=0):
    return pl.CostEstimate(flops=int(flops), bytes_accessed=int(nbytes), transcendentals=int(trans))


def states_kernel(xbc, halo, cw, hp, x, bc, s, dt, ld, ldt, st0, comb, dec, pad, tail, carry, xw):
    j = pl.program_id(0)
    m, b = j // 2, j % 2
    before = jnp.where(b == 0, halo[pl.ds(8 * m, 8), :XC], tail[...])
    pad[0:8] = before
    pad[8 : 8 + T] = xbc[:, :XC]
    tail[...] = xbc[T - 8 : T, :XC]
    step = softplus(xbc[:, XC:XP] + hp[0:1, :])
    step = jnp.where(iota((T, 128), 1) < HH, step, 0.0)
    tri = (iota((T, T), 0) >= iota((T, T), 1)).astype(f32)
    logd = jnp.dot(tri, -hp[1:2, :] * step, precision=HIGH, preferred_element_type=f32)
    dt[...] = step
    ld[...] = logd
    ldt[0] = logd.T[:32]
    tailw = jnp.exp(logd[T - 1 : T] - logd) * step
    lanes = slice(W, XC)
    a = conv_taps(pad, cw, lanes)
    act = a * lax.logistic(a)
    bc[...] = act
    s[...] = fine(nt, act[:, N:], act[:, :N])
    for i in range(W // 128):
        lanes = slice(128 * i, 128 * i + 128)
        a = conv_taps(pad, cw, lanes)
        act_x = a * lax.logistic(a)
        x[:, lanes] = act_x
        xw[:, lanes] = (act_x * spread(tailw, 2 * i, 2)).astype(bf16)
    st = tn(act[:, :N].astype(bf16), xw[...])
    last = jnp.exp(logd[T - 8 : T])
    decay = jnp.concatenate([spread(last, 4 * i, 4) for i in range(W // 256)], axis=1)[7:8]
    dec[0] = jnp.broadcast_to(decay, (8, W))

    @pl.when(b == 0)
    def _():
        st0[0] = st
        carry[...] = st

    @pl.when(b == 1)
    def _():
        comb[0] = (decay * carry[...] + st).astype(bf16)


def block_states(xbc, cw, hp, micros):
    blocks = 2 * micros
    rows = blocks * T
    blk = lambda j: (j % 2) * micros + j // 2
    out = lambda *sh: jax.ShapeDtypeStruct(sh, f32)
    whole = lambda a: pl.BlockSpec(a.shape, lambda j: (0, 0))
    return pl.pallas_call(
        states_kernel,
        name="block_states",
        grid=(blocks,),
        in_specs=[
            pl.BlockSpec((T, XP), lambda j: (blk(j), 0)),
            pl.BlockSpec((8 * micros, XP), lambda j: (rows // (8 * micros), 0)),
            whole(cw),
            whole(hp),
        ],
        out_specs=[
            pl.BlockSpec((T, W), lambda j: (blk(j), 0)),
            pl.BlockSpec((T, 2 * N), lambda j: (blk(j), 0)),
            pl.BlockSpec((T, T), lambda j: (blk(j), 0)),
            pl.BlockSpec((T, 128), lambda j: (blk(j), 0)),
            pl.BlockSpec((T, 128), lambda j: (blk(j), 0)),
            pl.BlockSpec((1, 32, T), lambda j: (blk(j), 0, 0)),
            pl.BlockSpec((1, N, W), lambda j: (j // 2, 0, 0)),
            pl.BlockSpec((1, N, W), lambda j: (j // 2, 0, 0)),
            pl.BlockSpec((1, 8, W), lambda j: (blk(j), 0, 0)),
        ],
        out_shape=[
            out(rows, W),
            out(rows, 2 * N),
            out(rows, T),
            out(rows, 128),
            out(rows, 128),
            out(blocks, 32, T),
            out(micros, N, W),
            jax.ShapeDtypeStruct((micros, N, W), bf16),
            out(blocks, 8, W),
        ],
        scratch_shapes=[
            pltpu.VMEM((T + 8, XC), f32),
            pltpu.VMEM((8, XC), f32),
            pltpu.VMEM((N, W), f32),
            pltpu.VMEM((T, W), bf16),
        ],
        compiler_params=params(),
        cost_estimate=cost(blocks * 2 * T * N * W, rows * (XP + W + 800) * 4, rows * XC * 2),
    )(xbc, xbc, cw, hp)


def inner_kernel(s, ld, ldt, dt, x, skip, y):
    g = pl.program_id(1)
    causal = iota((T, T), 0) >= iota((T, T), 1)
    head = iota((T, 256), 1) // PS
    shift = lax.rem(128 - 4 * g, 128)
    logd = pltpu.roll(ld[...], shift, 1)
    step = pltpu.roll(dt[...], shift, 1)
    tile = x[...]
    xdt = tile * spread(step, 0, 4)
    scores = s[...]
    total = skip[0:1, :] * tile
    for i in range(4):
        gap = logd[:, i : i + 1] - ldt[0, pl.ds(4 * g + i, 1), :]
        mixing = (jnp.exp(jnp.where(causal, gap, NEG)) * scores).astype(bf16)
        total = total + nn(mixing, jnp.where(head == i, xdt, 0.0).astype(bf16))
    y[...] = total


def inner_part(s, ld, ldt, dt, x, skip_row):
    rows = x.shape[0]
    blocks, groups = rows // T, W // 256
    return pl.pallas_call(
        inner_kernel,
        name="inner_part",
        grid=(blocks, groups),
        in_specs=[
            pl.BlockSpec((T, T), lambda j, g: (j, 0)),
            pl.BlockSpec((T, 128), lambda j, g: (j, 0)),
            pl.BlockSpec((1, 32, T), lambda j, g: (j, 0, 0)),
            pl.BlockSpec((T, 128), lambda j, g: (j, 0)),
            pl.BlockSpec((T, 256), lambda j, g: (j, g)),
            pl.BlockSpec((8, 256), lambda j, g: (0, g)),
        ],
        out_specs=pl.BlockSpec((T, 256), lambda j, g: (j, g)),
        out_shape=jax.ShapeDtypeStruct((rows, W), f32),
        compiler_params=params(),
        cost_estimate=cost(
            blocks * HH * 2 * T * T * 256, rows * (2 * W + 1024) * 4, blocks * HH * T * T
        ),
    )(s, ld, ldt, dt, x, skip_row)


def gate_kernel(yin, bc, e, ld, z, y, sums):
    grow = jnp.exp(ld[...])
    cst = bc[:, N:].astype(bf16)
    squares = jnp.zeros((T, 256), f32)
    for i in range(W // 256):
        lanes = slice(256 * i, 256 * i + 256)
        out = yin[:, lanes] + spread(grow, 4 * i, 4) * nn(cst, e[0, :, lanes])
        y[:, lanes] = out
        zt = z[:, lanes]
        g = out * (zt * lax.logistic(zt))
        squares = squares + g * g
    sums[...] = jnp.broadcast_to(jnp.sum(squares, axis=1, keepdims=True), (T, 128))


def gate_part(yin, bc, e, ld, z):
    rows = yin.shape[0]
    blocks = rows // T
    row = lambda c: pl.BlockSpec((T, c), lambda j: (j, 0))
    return pl.pallas_call(
        gate_kernel,
        name="gate_part",
        grid=(blocks,),
        in_specs=[
            row(W),
            row(2 * N),
            pl.BlockSpec((1, N, W), lambda j: (j, 0, 0)),
            row(128),
            row(W),
        ],
        out_specs=[row(W), row(128)],
        out_shape=[
            jax.ShapeDtypeStruct((rows, W), f32),
            jax.ShapeDtypeStruct((rows, 128), f32),
        ],
        input_output_aliases={0: 0},
        compiler_params=params(),
        cost_estimate=cost(2 * rows * N * W, rows * W * 4 * 3, rows * W * 2),
    )(yin, bc, e, ld, z)


def gate_back_kernel(y, z, gfin, x, sums, dots, bc, e, ld, gain, skip, dz, dy, dc, de, dl, ggain, gskip, dye):
    j = pl.program_id(0)

    @pl.when(j == 0)
    def _():
        ggain[...] = jnp.zeros_like(ggain)
        gskip[...] = jnp.zeros_like(gskip)

    r = lax.rsqrt(sums[:, 0:1] * (1.0 / DI) + EPS)
    coef = r * r * dots[:, 0:1] * (1.0 / DI)
    grow = jnp.exp(ld[...])
    dlog = jnp.zeros((T, 128), f32)
    dcs = jnp.zeros((T, N), f32)
    for i in range(W // 256):
        lanes = slice(256 * i, 256 * i + 256)
        zt, yt, gf = z[:, lanes], y[:, lanes], gfin[:, lanes]
        sg = lax.logistic(zt)
        silu = zt * sg
        g = yt * silu
        gr = g * r
        ggain[0:1, lanes] += row_sum(gf * gr)
        dg = r * (gf * gain[0:1, lanes]) - g * coef
        dyt = dg * silu
        dz[:, lanes] = (dg * yt * (sg * (1.0 + zt * (1.0 - sg)))).astype(bf16)
        dy[:, lanes] = dyt.astype(bf16)
        xt = x[:, lanes]
        gskip[0:1, lanes] += row_sum(dyt * xt)
        dlog = dlog + per_head(dyt * (yt - skip[0:1, lanes] * xt), 4 * i)
        high, low = halves(dyt * spread(grow, 4 * i, 4))
        dye[:, lanes] = high
        dcs = dcs + (nt(high, e[0, :, lanes]) + nt(low, e[0, :, lanes]))
    dl[...] = dlog
    dc[...] = dcs
    de[0] = tn(bc[:, N:].astype(bf16), dye[...])


def gate_back(y, z, gfin, x, sums, dots, bc, e, ld, gain, skip_row):
    rows = y.shape[0]
    blocks = rows // T
    row = lambda c: pl.BlockSpec((T, c), lambda j: (j, 0))
    fixed = pl.BlockSpec((8, W), lambda j: (0, 0))
    state = pl.BlockSpec((1, N, W), lambda j: (j, 0, 0))
    sh = jax.ShapeDtypeStruct
    return pl.pallas_call(
        gate_back_kernel,
        name="gate_back",
        grid=(blocks,),
        in_specs=[row(W), row(W), row(W), row(W), row(128), row(128), row(2 * N), state, row(128), fixed, fixed],
        out_specs=[row(W), row(W), row(N), state, row(128), fixed, fixed],
        out_shape=[
            sh((rows, W), bf16),
            sh((rows, W), bf16),
            sh((rows, N), f32),
            sh((blocks, N, W), f32),
            sh((rows, 128), f32),
            sh((8, W), f32),
            sh((8, W), f32),
        ],
        scratch_shapes=[pltpu.VMEM((T, W), bf16)],
        compiler_params=params(),
        cost_estimate=cost(8 * rows * N * W, rows * W * 24, rows * W * 2),
    )(y, z, gfin, x, sums, dots, bc, e, ld, gain, skip_row)


def inner_back_kernel(s, bc, ld, ldt, dt, x, dy, skip, dx, xv, dbc, st, dst):
    g = pl.program_id(1)

    @pl.when(g == 0)
    def _():
        st[...] = s[...].T
        dst[...] = jnp.zeros_like(dst)
        xv[...] = jnp.zeros_like(xv)

    causal = iota((T, T), 1) >= iota((T, T), 0)
    head = iota((T, 256), 1) // PS
    shift = lax.rem(128 - 4 * g, 128)
    logd = pltpu.roll(ld[...], shift, 1)
    steps = spread(pltpu.roll(dt[...], shift, 1), 0, 4)
    tile = x[...]
    xdt = tile * steps
    dyt = dy[...]
    scores = st[...]
    total = jnp.zeros((T, 256), f32)
    gscore = jnp.zeros((T, T), f32)
    for i in range(4):
        gap = ldt[0, pl.ds(4 * g + i, 1), :] - logd[:, i : i + 1]
        decay = jnp.exp(jnp.where(causal, gap, NEG))
        mine = head == i
        total = total + nn((decay * scores).astype(bf16), jnp.where(mine, dyt, jnp.zeros_like(dyt)))
        gscore = gscore + nt(jnp.where(mine, xdt, 0.0).astype(bf16), dyt) * decay
    dst[...] += gscore
    dx[...] = total * steps + skip[0:1, :] * dyt.astype(f32)
    xv[...] += per_head(tile * total, 4 * g)

    @pl.when(g == pl.num_programs(1) - 1)
    def _():
        dbc[:, :N] = fine(nn, dst[...], bc[:, N:])
        dbc[:, N:] = fine(tn, dst[...], bc[:, :N])


def inner_back(s, bc, ld, ldt, dt, x, dy, skip_row):
    rows = x.shape[0]
    blocks, groups = rows // T, W // 256
    row = lambda c: pl.BlockSpec((T, c), lambda j, g: (j, 0))
    tile = pl.BlockSpec((T, 256), lambda j, g: (j, g))
    sh = jax.ShapeDtypeStruct
    return pl.pallas_call(
        inner_back_kernel,
        name="inner_back",
        grid=(blocks, groups),
        in_specs=[
            row(T),
            row(2 * N),
            row(128),
            pl.BlockSpec((1, 32, T), lambda j, g: (j, 0, 0)),
            row(128),
            tile,
            tile,
            pl.BlockSpec((8, 256), lambda j, g: (0, g)),
        ],
        out_specs=[tile, row(128), row(2 * N)],
        out_shape=[sh((rows, W), f32), sh((rows, 128), f32), sh((rows, 2 * N), f32)],
        scratch_shapes=[pltpu.VMEM((T, T), f32), pltpu.VMEM((T, T), f32)],
        compiler_params=params(),
        cost_estimate=cost(
            2 * blocks * HH * 2 * T * T * 256, rows * (2 * W + 1024) * 4, blocks * HH * T * T
        ),
    )(s, bc, ld, ldt, dt, x, dy, skip_row)


def conv_back_kernel(
    micros, xbc, prev, x, dxi, xv, dbc, bc, dt, ld, later, e, dc, dla, cw, hp,
    gp, gcw, ghp, pad, dpre, nxt, edge,
):
    p = pl.program_id(0)
    b = 1 - p % 2

    @pl.when(p == 0)
    def _():
        gcw[...] = jnp.zeros_like(gcw)
        ghp[...] = jnp.zeros_like(ghp)

    @pl.when(p == 2 * micros)
    def _():
        gp[0 : 8 * micros] = edge[...].astype(bf16)

    @pl.when(p < 2 * micros)
    def _():
        pad[0:8] = prev[:, :XC]
        pad[8 : 8 + T] = xbc[:, :XC]
        dpre[0:8] = jnp.zeros((8, XC), f32)
        dpre[8 + T : 16 + T] = jnp.where(b == 1, 0.0, nxt[...])
        step, logd = dt[...], ld[...]
        fade = jnp.exp(logd[T - 1 : T] - logd)
        tailw = fade * step
        bst = bc[:, :N].astype(bf16)

        def through_conv(grad, lanes):
            a = conv_taps(pad, cw, lanes)
            sg = lax.logistic(a)
            d = grad * (sg * (1.0 + a * (1.0 - sg)))
            dpre[8 : 8 + T, lanes] = d
            gcw[4:5, lanes] += row_sum(d)
            for k in range(KC):
                gcw[k : k + 1, lanes] += row_sum(d * pad[pl.ds(5 + k, T), lanes])
            total = cw[0:1, lanes] * dpre[pl.ds(11, T), lanes]
            rim = cw[0:1, lanes] * dpre[pl.ds(3, 8), lanes]
            for k in range(1, KC):
                total = total + cw[k : k + 1, lanes] * dpre[pl.ds(11 - k, T), lanes]
                rim = rim + cw[k : k + 1, lanes] * dpre[pl.ds(3 - k, 8), lanes]
            gp[:, lanes] = total.astype(bf16)
            nxt[:, lanes] = d[0:8]

            @pl.when(b == 0)
            def _():
                edge[pl.ds(pl.multiple_of(8 * (p // 2), 8), 8), lanes] = rim

        dw = jnp.zeros((T, 128), f32)
        dbs = jnp.zeros((T, N), f32)
        ddec = jnp.zeros((8, 128), f32)
        for i in range(W // 256):
            lanes = slice(256 * i, 256 * i + 256)
            lat = later[0, :, lanes]
            spreadw = spread(tailw, 4 * i, 4)
            xt = x[:, lanes]
            bl = nn(bst, lat)
            dw = dw + per_head(xt * bl, 4 * i)
            high, low = halves(xt * spreadw)
            dbs = dbs + (nt(high, lat) + nt(low, lat))
            both = row_sum(lat.astype(f32) * e[0, :, lanes].astype(f32))
            ddec = ddec + per_head(jnp.broadcast_to(both, (8, 256)), 4 * i)
            through_conv(dxi[:, lanes] + bl * spreadw, lanes)
        through_conv(
            jnp.concatenate([dbc[:, :N] + dbs, dbc[:, N:] + dc[...]], axis=1), slice(W, XC)
        )
        q = dw * tailw
        dlog = dla[...] - step * xv[...] - q
        dlast = row_sum(q) + ddec[0:1] * jnp.exp(logd[T - 1 : T])
        dlog = dlog + jnp.where(iota((T, 128), 0) == T - 1, dlast, 0.0)
        tri = (iota((T, T), 1) >= iota((T, T), 0)).astype(f32)
        dcum = jnp.dot(tri, dlog, precision=HIGH, preferred_element_type=f32)
        dstep = xv[...] + dw * fade - hp[1:2, :] * dcum
        draw = dstep * lax.logistic(xbc[:, XC:XP] + hp[0:1, :])
        draw = jnp.where(iota((T, 128), 1) < HH, draw, 0.0)
        ghp[0:1] += row_sum(draw)
        ghp[1:2] -= row_sum(dcum * step)
        gp[:, XC:XP] = draw.astype(bf16)

        @pl.when(b == 0)
        def _():
            edge[pl.ds(pl.multiple_of(8 * (p // 2), 8), 8), XC:XP] = jnp.zeros((8, 128), f32)


def conv_back(xbc, x, dxi, xv, dbc, bc, dt, ld, later, e, dc, dla, cw, hp, micros):
    blocks = 2 * micros
    rows = blocks * T
    blk = lambda p: jnp.where(p < blocks, (1 - p % 2) * micros + p // 2, micros - 1)
    row = lambda c: pl.BlockSpec((T, c), lambda p: (blk(p), 0))
    whole = lambda a: pl.BlockSpec(a.shape, lambda p: (0, 0))
    state = pl.BlockSpec((1, N, W), lambda p: (blk(p), 0, 0))

    def before(p):
        k = blk(p)
        return (jnp.where(k >= micros, (k - micros + 1) * (T // 8) - 1, rows // 8 + k), 0)

    return pl.pallas_call(
        functools.partial(conv_back_kernel, micros),
        name="conv_back",
        grid=(blocks + 1,),
        in_specs=[
            row(XP),
            pl.BlockSpec((8, XP), before),
            row(W), row(W), row(128), row(2 * N), row(2 * N), row(128), row(128),
            state, state, row(N), row(128), whole(cw), whole(hp),
        ],
        out_specs=[
            pl.BlockSpec((T, XP), lambda p: (jnp.where(p < blocks, blk(p), blocks), 0)),
            pl.BlockSpec((8, XC), lambda p: (0, 0)),
            pl.BlockSpec((8, 128), lambda p: (0, 0)),
        ],
        out_shape=[
            jax.ShapeDtypeStruct((rows + 8 * micros, XP), bf16),
            jax.ShapeDtypeStruct((8, XC), f32),
            jax.ShapeDtypeStruct((8, 128), f32),
        ],
        scratch_shapes=[
            pltpu.VMEM((T + 8, XC), f32),
            pltpu.VMEM((T + 16, XC), f32),
            pltpu.VMEM((8, XC), f32),
            pltpu.VMEM((8 * micros, XP), f32),
        ],
        compiler_params=pltpu.CompilerParams(vmem_limit_bytes=58 * MB_),
        cost_estimate=cost(6 * rows * N * W, rows * W * 18, rows * XC * 2),
    )(xbc, xbc, x, dxi, xv, dbc, bc, dt, ld, later, e, dc, dla, cw, hp)


AXIS = {"z": Z, "l": "zl", "s": "s"}
RING = 4
CHIPS = 16


def hop(value, axis):
    n = RING if axis == "z" else 2
    return lax.ppermute(value, AXIS[axis], [(i, (i + 1) % n) for i in range(n)])


def fence(groups, *values):
    held = [{k: g.live[k] for k in g.live} for g in groups]
    held, values = lax.optimization_barrier((held, values))
    for g, h in zip(groups, held):
        g.live.update(h)
    return values


def after(groups, *values):
    values, _ = lax.optimization_barrier((values, [v for g in groups for v in g.sent]))
    for g in groups:
        g.sent = ()
    return values


class Moves:
    sent = ()

    def send(self, value, axis):
        self.sent = [*self.sent, value]
        return hop(value, axis)


class RingFirst(Moves):
    def __init__(self, own, a, b):
        self.a, self.b = a, b
        self.live = {"g0": own}
        self.n = 1
        self.parts = []

    def z(self):
        self.live[f"g{self.n}"] = self.send(self.live[f"g{self.n - 1}"], "z")
        self.n += 1

    def first(self, h):
        pair = jnp.stack([self.live.pop(f"g{2 * h}"), self.live[f"g{2 * h + 1}"]], 0)
        if h:
            self.live.pop("g3")
        self.live[f"p{h}"] = pair
        self.live[f"q{h}"] = self.send(pair, self.a)

    def second(self, h):
        four = jnp.concatenate([self.live.pop(f"p{h}"), self.live.pop(f"q{h}")], 0)
        self.parts += [four, self.send(four, self.b)]

    def entry(self, kz, kl, ks):
        ka, kb = (kl, ks) if self.a == "l" else (ks, kl)
        return (kz // 2) * 2 + kb, ka * 2 + kz % 2


class RingLast(Moves):
    def __init__(self, own, a, b):
        self.a, self.b = a, b
        self.live = {"p": own[None]}
        self.parts = []

    def step(self, axis):
        self.live["p"] = jnp.concatenate([self.live["p"], self.send(self.live["p"], axis)], 0)

    def z(self):
        if not self.parts:
            self.parts = [self.live["p"]]
        self.live["p"] = self.send(self.live["p"], "z")
        self.parts.append(self.live["p"])

    def entry(self, kz, kl, ks):
        ka, kb = (kl, ks) if self.a == "l" else (ks, kl)
        return kz, kb * 2 + ka


class ExchangeFirst(Moves):
    def __init__(self, a, b):
        self.a, self.b = a, b
        self.live = {}

    def load(self, parts):
        for h in range(2):
            self.live[f"k{h}"], self.live[f"s{h}"] = parts[2 * h], parts[2 * h + 1]

    def second(self, h):
        got = self.send(self.live.pop(f"s{h}"), self.b)
        self.live[f"r{h}"] = got

    def first(self, h):
        total = self.live.pop(f"r{h}").astype(f32) + self.live.pop(f"k{h}").astype(f32)
        self.live[f"m{h}"] = total[:2].astype(bf16)
        self.live[f"n{h}"] = self.send(total[2:].astype(bf16), self.a)

    def ring(self, k):
        if k in (0, 2):
            h = k // 2
            both = self.live.pop(f"m{h}").astype(f32) + self.live.pop(f"n{h}").astype(f32)
            term, self.live["w"] = both[0], both[1].astype(bf16)
        else:
            term = self.live.pop("w").astype(f32)
        if k:
            term = term + self.live.pop("t").astype(f32)
        if k == 3:
            return term
        self.live["t"] = self.send(term.astype(bf16), "z")

    def entry(self, kz, kl, ks):
        ka, kb = (kl, ks) if self.a == "l" else (ks, kl)
        h, at = ((0, kz - 1) if kz in (1, 2) else (1, (kz + 1) % 4))
        return 2 * h + kb, ka * 2 + at


def move_kernel(table, r, out_of, where, *refs):
    sems = refs[-1]
    refs = refs[:-1]
    whole = refs[-1] if out_of else refs[0]
    arrays = refs[:-1] if out_of else refs[1:]
    copies = []
    for n, (array, entry, k, lane, width) in enumerate(table):
        row = pl.multiple_of(where[k] * r, 16)
        place = whole.at[pl.ds(row, r), lane : lane + width]
        piece = arrays[array].at[entry]
        pair = (piece, place) if out_of else (place, piece)
        copies.append(pltpu.make_async_copy(*pair, sems.at[n]))
    for c in copies:
        c.start()
    for c in copies:
        c.wait()


def move(groups, where, r, widths, whole=None, parts=None):
    table = []
    for g, group in enumerate(groups):
        for k in range(CHIPS):
            array, entry = group.entry(k // 4, k // 2 % 2, k % 2)
            table.append((4 * g + array, entry, k, sum(widths[:g]), widths[g]))
    wide = sum(widths)
    shapes = [jax.ShapeDtypeStruct((4, r, w), bf16) for w in widths for _ in range(4)]
    joined = jax.ShapeDtypeStruct((CHIPS * r, wide), bf16)
    given = parts if parts else [whole]
    any_ = pl.BlockSpec(memory_space=pl.ANY)
    return pl.pallas_call(
        functools.partial(move_kernel, tuple(table), r, parts is not None),
        name="join" if parts else "deal",
        in_specs=[pl.BlockSpec(memory_space=pltpu.SMEM)] + [any_] * len(given),
        out_specs=any_ if parts else [any_] * len(shapes),
        out_shape=joined if parts else shapes,
        scratch_shapes=[pltpu.SemaphoreType.DMA((len(table),))],
        compiler_params=pltpu.CompilerParams(vmem_limit_bytes=MB_),
        cost_estimate=cost(0, 4 * CHIPS * r * wide),
    )(where, *given)


def join(groups, where, r, widths):
    return move(groups, where, r, widths, parts=[p for g in groups for p in g.parts])


def deal(groups, where, r, widths, whole):
    parts = move(groups, where, r, widths, whole=whole)
    for g, group in enumerate(groups):
        group.load(parts[4 * g : 4 * g + 4])


def swap(value, axis="c"):
    return lax.ppermute(value, axis, [(0, 1), (1, 0)])


def two(mine, other, at):
    return jnp.where(at == 0, jnp.stack([mine, other]), jnp.stack([other, mine]))


def cols(value, *widths):
    out, at = [], 0
    for w in widths:
        out.append(value[:, at : at + w])
        at += w
    return out


class Plain:
    def __init__(self, axes):
        self.axes = axes

    def gather(self, piece):
        return lax.all_gather(piece, self.axes, axis=0, tiled=True)

    def reduce(self, grad):
        return lax.psum_scatter(grad, self.axes, scatter_dimension=0, tiled=True).astype(f32)


def body(
    hidden, in_weight, out_weight, conv_weight, conv_bias, norm_gain, gate_gain,
    step_bias, decay_rate, skip_gain, cotangent,
):
    nz, nl, ns = lax.axis_size(Z), lax.axis_size("zl"), lax.axis_size("s")
    core = lax.axis_index("c")
    micros = hidden.shape[0]
    rows = micros * 2 * T
    r_in, r_out = in_weight.shape[0], out_weight.shape[0]
    r = 2 * r_in
    fast = (nz, nl, ns) == (RING, 2, 2) and r % 16 == 0 and r_out == r
    onward = [(i, i + 1) for i in range(ns - 1)]
    backward = [(i + 1, i) for i in range(ns - 1)]
    turn = [(a * 2 + b, b * 2 + a) for a in range(2) for b in range(2)]

    def cut(k):
        return jnp.concatenate(
            [
                in_weight[:, DI + k * W : DI + (k + 1) * W],
                in_weight[:, 2 * DI : 2 * DI + 2 * N],
                jnp.pad(in_weight[:, DI + CONV + k * HH : DI + CONV + (k + 1) * HH], ((0, 0), (0, 128 - HH))),
                in_weight[:, k * W : (k + 1) * W],
            ],
            axis=1,
        )

    cuts = jnp.stack([cut(0), cut(1)])
    theirs = swap(lax.dynamic_index_in_dim(cuts, 1 - core, 0, False))
    chip_rows = two(lax.dynamic_index_in_dim(cuts, core, 0, False), theirs, core).reshape(r, -1)
    w_own = lax.ppermute(out_weight, ("za", "c"), turn)

    ins = Plain(ALL[:4])
    outs = Plain(("zb", "zl", "s", "za"))

    n_c = conv_bias.shape[0]
    packed = jnp.concatenate([conv_weight.T.reshape(-1), conv_bias, norm_gain, gate_gain])

    def spread_out(small, a, at):
        mine, other = (jnp.expand_dims(v, at) for v in (small, swap(small, a)))
        here = lax.axis_index(a) == 0
        return jnp.where(here, jnp.concatenate([mine, other], at), jnp.concatenate([other, mine], at))

    hid_own = hidden.reshape(micros, T, D)
    cot_own = cotangent.reshape(micros, T, D)
    hid_other, cot_other = swap(hid_own), swap(cot_own)

    def chip_tokens(mine, other):
        return two(mine, other, core).reshape(rows, D)

    def rim_of(tokens):
        return lax.ppermute(tokens.reshape(2, micros, T, D)[1, :, T - 8 :], "s", onward)

    if fast:
        back = jnp.arange(CHIPS)
        kz = (lax.axis_index(Z) - back // 4) % RING
        kl = (lax.axis_index("zl") - back // 2) % 2
        ks = (lax.axis_index("s") - back) % 2
        in_place = ((kz * 2 + kl) * 2 + ks).astype(jnp.int32)
        out_place = ((((kz % 2) * 2 + kl) * 2 + ks) * 2 + kz // 2).astype(jnp.int32)
        x_cols, z_cols, o_cols = (896, 1024), (768, 768), (768, 768)
        small = spread_out(packed, "za", 0)
        small = spread_out(small, "zb", 1)
        chip_rows, small = lax.optimization_barrier((chip_rows, small))
        own = cols(chip_rows, *x_cols, *z_cols)
        gx_ = [RingFirst(own[0], "s", "l"), RingFirst(own[1], "l", "s")]
        gz_ = [RingFirst(own[2], "s", "l"), RingFirst(own[3], "l", "s")]
        own = cols(w_own, *o_cols)
        go_ = [RingLast(own[0], "s", "l"), RingLast(own[1], "l", "s")]
        every = gx_ + gz_ + go_
        small = spread_out(small, "zl", 2)
        for g in gx_:
            g.z()
        for g in go_:
            g.step(g.a)
        small, hid_other, cot_other = fence(every, small, hid_other, cot_other)
        small = spread_out(small, "s", 3)
        for g in gx_:
            g.z()
            g.first(0)
        for g in go_:
            g.step(g.b)
        hid_own_, hid_other = after(every, hid_own, hid_other)
        hid_all = chip_tokens(hid_own_, hid_other)
        rim = rim_of(hid_all)
        small, rim, hid_all = fence(every, small, rim, hid_all)
        for g in gx_:
            g.z()
            g.second(0)
        for g in gz_:
            g.z()
        small, cot_own_, cot_other = after(every, small, cot_own, cot_other)
        small = spread_out(small, "c", 4).reshape(-1, packed.shape[0])
        cot_all = chip_tokens(cot_own_, cot_other)
        small, cot_all = fence(every, small, cot_all)
        for g in gx_:
            g.first(1)
        for g in gz_:
            g.z()
        for g in go_:
            g.z()
        (small,) = fence(gx_ + gz_, small)
        for g in gx_:
            g.second(1)
        for g in gz_:
            g.z()
        small, hid_all, rim = after(gx_ + gz_, small, hid_all, rim)
    else:
        small = lax.all_gather(packed, ALL)
        hid_all, cot_all = chip_tokens(hid_own, hid_other), chip_tokens(cot_own, cot_other)
        rim = rim_of(hid_all)
        w_x, w_z = ins.gather(chip_rows[:, :XP]), ins.gather(chip_rows[:, XP:])

    rim = jnp.where(iota(rim.shape, 1) >= 5, rim, jnp.zeros_like(rim)).reshape(8 * micros, D)
    tok_f = jnp.concatenate([hid_all, rim], axis=0).astype(f32)
    scale = lax.rsqrt(jnp.mean(tok_f * tok_f, axis=-1, keepdims=True) + EPS)
    devices = small.shape[0]
    taps = small[:, : KC * n_c].reshape(devices, KC, n_c).transpose(1, 0, 2).reshape(KC, CONV)
    bias = small[:, KC * n_c : (KC + 1) * n_c].reshape(1, CONV)
    norm_vec = small[:, (KC + 1) * n_c : (KC + 1) * n_c + r_in].reshape(D).astype(f32)
    gate_vec = small[:, (KC + 1) * n_c + r_in :].reshape(1, DI)
    conv_all = jnp.concatenate([taps, bias, jnp.zeros((3, CONV), bf16)], 0).astype(f32)
    cw = jnp.concatenate(
        [lax.dynamic_slice_in_dim(conv_all, core * W, W, 1), conv_all[:, DI:]], axis=1
    )
    gain = jnp.broadcast_to(lax.dynamic_slice_in_dim(gate_vec, core * W, W, 1).astype(f32), (8, W))
    heads = jnp.stack([step_bias, decay_rate, skip_gain])
    heads = lax.dynamic_slice_in_dim(heads, core * HH, HH, 1)
    hp = jnp.pad(heads, ((0, 5), (0, 128 - HH)))
    skip_row = jnp.broadcast_to(jnp.repeat(heads[2], PS)[None], (8, W))
    normed = (tok_f * scale * norm_vec).astype(bf16)

    if fast:
        normed, cw, hp, gain, skip_row = fence(every, normed, cw, hp, gain, skip_row)
        for g in gz_:
            g.first(0)
        for g in go_:
            g.z()
        (normed,) = after(gz_ + go_, normed)
        w_x = join(gx_, in_place, r, x_cols)
    xbc = nn(normed, w_x)
    if fast:
        (xbc,) = fence(gz_, xbc)
        for g in gz_:
            g.second(0)
            g.first(1)
        (xbc,) = after(gz_, xbc)
    else:
        w_o = outs.gather(w_own)
    x, bc, s, dt, ld, ldt, st0, comb, dec = block_states(xbc, cw, hp, micros)
    dec = dec[:, 0].reshape(2, micros, 1, W)
    if fast:
        comb, s = fence(gz_ + go_, comb, s)
        for g in gz_:
            g.second(1)
        for g in go_:
            g.z()
        (s,) = after(gz_ + go_, s)
    if ns == 2:
        first = lax.ppermute(comb, "s", onward)
    else:
        first = jnp.zeros_like(comb)
        chip_decay = dec[0] * dec[1]
        for _ in range(ns - 1):
            out = (chip_decay * first.astype(f32) + comb.astype(f32)).astype(bf16)
            first = lax.ppermute(out, "s", onward)
    yin = inner_part(s, ld, ldt, dt, x, skip_row)
    second = (dec[0] * first.astype(f32) + st0).astype(bf16)
    entering = jnp.stack([first, second], 0).reshape(2 * micros, N, W)
    if fast:
        w_z = join(gz_, in_place, r, z_cols)
    z = nn(normed[:rows], w_z)
    y, sums = gate_part(yin, bc, entering, ld, z)
    sums = sums + swap(sums)
    root = lax.rsqrt(sums[:, :1] * (1.0 / DI) + EPS)
    exact = y * (z * lax.logistic(z)) * root * gain[:1]
    fin = exact.astype(bf16)
    g_out = tn(fin, cot_all).astype(bf16)
    if fast:
        so_ = [ExchangeFirst("s", "l"), ExchangeFirst("l", "s")]
        deal(so_, out_place, r, o_cols, g_out)
        (cot_all,) = fence(so_, cot_all)
        for g in so_:
            g.second(0)
        (cot_all,) = after(so_, cot_all)
        w_o = join(go_, out_place, r, o_cols)

    gfin = nt(cot_all, w_o)
    dots = jnp.sum(gfin * exact, axis=1)
    if fast:
        dots, gfin = fence(so_, dots, gfin)
        for g in so_:
            g.second(1)
            g.first(0)
        (y,) = after(so_, y)
    dots = dots + swap(dots)
    dots = jnp.broadcast_to(dots[:, None], (rows, 128))
    dz, dy, dc, de, dla, ggain, gskip = gate_back(
        y, z, gfin, x, sums, dots, bc, entering, ld, gain, skip_row
    )
    de = de.reshape(2, micros, N, W)
    if ns == 2:
        given = (de[0] + dec[0] * de[1]).astype(bf16)
        dz, given = lax.optimization_barrier((dz, given))
        later1 = lax.ppermute(given, "s", backward)
    else:
        later1 = jnp.zeros((micros, N, W), bf16)
        for _ in range(ns - 1):
            out = de[0] + dec[0] * (de[1] + dec[1] * later1.astype(f32))
            later1 = lax.ppermute(out.astype(bf16), "s", backward)
    gz = tn(normed[:rows], dz).astype(bf16)
    if fast:
        sz_ = [ExchangeFirst("s", "l"), ExchangeFirst("l", "s")]
        deal(sz_, in_place, r, z_cols, gz)
        (dy,) = fence(so_ + sz_, dy)
        for g in so_:
            g.first(1)
            g.ring(0)
        for g in sz_:
            g.second(0)
        (dy,) = after(so_ + sz_, dy)

    dxi, xv, dbc = inner_back(s, bc, ld, ldt, dt, x, dy, skip_row)
    later0 = (de[1] + dec[1] * later1.astype(f32)).astype(bf16)
    later = jnp.stack([later0, later1], 0).reshape(2 * micros, N, W)
    if fast:
        dxi, later = fence(so_ + sz_, dxi, later)
        for g in so_:
            g.ring(1)
        for g in sz_:
            g.second(1)
            g.first(0)
        (dxi,) = after(so_ + sz_, dxi)
    gp, gcw, ghp = conv_back(
        xbc, x, dxi, xv, dbc, bc, dt, ld, later, entering, dc, dla, cw, hp, micros
    )
    if fast:
        (gp,) = fence(so_ + sz_, gp)
        for g in sz_:
            g.first(1)
            g.ring(0)
        for g in so_:
            g.ring(2)
        (gp,) = after(so_ + sz_, gp)
    gx = tn(normed, gp).astype(bf16)
    if fast:
        sx_ = [ExchangeFirst("s", "l"), ExchangeFirst("l", "s")]
        deal(sx_, in_place, r, x_cols, gx)
        (gp,) = fence(so_ + sz_ + sx_, gp)
        for g in sx_:
            g.second(0)
        for g in sz_:
            g.ring(1)
        (gp,) = after(sx_ + sz_, gp)
        g_out = jnp.concatenate([g.ring(3) for g in so_], axis=1)
    else:
        g_out = outs.reduce(g_out)

    gn = nt(gp, w_x)
    edge = lax.ppermute(gn[rows:].astype(bf16), "s", backward).reshape(1, micros, 8, D)
    gn = (gn[:rows] + nt(dz, w_z)).reshape(2, micros, T, D)
    if fast:
        gn, edge, fin, g_out = fence(sz_ + sx_, gn, edge, fin, g_out)
        for g in sx_:
            g.second(1)
            g.first(0)
        for g in sz_:
            g.ring(2)
        gn, fin = after(sx_ + sz_, gn, fin)
    edge = jnp.where(iota(edge.shape, 2) >= 5, edge.astype(f32), 0.0)
    gn = gn + jnp.pad(edge, ((1, 0), (0, 0), (T - 8, 0), (0, 0)))
    give = lax.dynamic_index_in_dim(gn, 1 - core, 0, False).astype(bf16)
    keep = lax.dynamic_index_in_dim(gn, core, 0, False)
    gn = keep + swap(give).astype(f32)
    hid_f = hid_own.astype(f32)
    own_scale = lax.rsqrt(jnp.mean(hid_f * hid_f, axis=-1, keepdims=True) + EPS)
    unit = hid_f * own_scale
    gq = gn * norm_vec
    g_hid = cot_own.astype(f32) + own_scale * (
        gq - unit * jnp.mean(gq * unit, axis=-1, keepdims=True)
    )
    g_norm = jnp.sum(gn * unit, axis=(0, 1))

    partial_out = nn(fin, w_o).reshape(2, micros, T, D)
    give = lax.dynamic_index_in_dim(partial_out, 1 - core, 0, False).astype(bf16)
    keep = lax.dynamic_index_in_dim(partial_out, core, 0, False)
    given_out = swap(give)

    wide = lambda v: jnp.pad(v, ((0, 0), (0, XC - v.shape[1])))
    tiny = jnp.concatenate(
        [
            gcw[:5], wide(ggain[:1]), wide(gskip[:1]), wide(ghp[:2].reshape(1, 256)),
            wide(g_norm[None]), jnp.zeros((7, XC), f32),
        ],
        axis=0,
    )
    if fast:
        tiny, g_hid, given_out, keep = fence(sz_ + sx_, tiny, g_hid, given_out, keep)
        tiny = tiny + swap(tiny, "zb")
        for g in sx_:
            g.first(1)
            g.ring(0)
        gz = jnp.concatenate([g.ring(3) for g in sz_], axis=1)
    block_out = (hid_own.astype(f32) + keep + given_out.astype(f32)).astype(bf16)

    def exchanged(g):
        g = g.reshape(2, r_in, -1)
        mine = lax.dynamic_index_in_dim(g, core, 0, False)
        return two(mine, swap(lax.dynamic_index_in_dim(g, 1 - core, 0, False)), core)

    if fast:
        tiny, block_out, gz, g_out = fence(sx_, tiny, block_out, gz, g_out)
        tiny = tiny + swap(tiny, "za")
        for g in sx_:
            g.ring(1)
        g_out = lax.ppermute(g_out, ("za", "c"), turn)
        gz = exchanged(gz)
        tiny, g_out, gz = fence(sx_, tiny, g_out, gz)
        tiny = tiny + swap(tiny, "s")
        for g in sx_:
            g.ring(2)
        tiny = tiny + swap(tiny, "zl")
        (tiny,) = fence(sx_, tiny)
        gx = jnp.concatenate([g.ring(3) for g in sx_], axis=1)
    else:
        tiny = lax.psum(tiny, ALL[:4])
        gx, gz = ins.reduce(gx), ins.reduce(gz)
        g_out = lax.ppermute(g_out, ("za", "c"), turn)
        gz = exchanged(gz)
    gx = exchanged(gx)
    both = two(tiny, swap(tiny), core)
    g_conv = jnp.concatenate([both[0, :5, :W], both[1, :5, :W], both[0, :5, W:] + both[1, :5, W:]], axis=1)
    me = lax.axis_index(ALL)
    g_conv = lax.dynamic_slice_in_dim(g_conv, me * n_c, n_c, 1)
    g_norm = lax.dynamic_slice_in_dim(both[0, 8, :D] + both[1, 8, :D], me * r_in, r_in)
    g_gate = both[:, 5, :W].reshape(-1)
    g_gate = lax.dynamic_slice_in_dim(g_gate, me * r_out, r_out)
    g_skip = both[:, 6, :W].reshape(H, PS).sum(-1)
    g_bias = both[:, 7, :HH].reshape(-1)
    g_rate = both[:, 7, 128 : 128 + HH].reshape(-1)
    g_in = jnp.concatenate(
        [
            gz[0], gz[1],
            gx[0, :, :W], gx[1, :, :W],
            gx[0, :, W:XC] + gx[1, :, W:XC],
            gx[0, :, XC : XC + HH], gx[1, :, XC : XC + HH],
        ],
        axis=1,
    )
    return (
        block_out.reshape(hidden.shape),
        g_hid.reshape(hidden.shape),
        g_in,
        g_out,
        g_conv[:KC].T,
        g_conv[KC],
        g_norm,
        g_gate,
        g_bias,
        g_rate,
        g_skip,
    )


def solution(mesh):
    dp, seq = mesh.shape["dp"], mesh.shape["seq"]
    split = Mesh(mesh.devices.reshape(2, dp // 4, 2, seq // 2, 2), ALL)
    token = P(None, ("za", "zb", "zl"), ("s", "c"), None)
    in_specs = (token, P(ALL, None), P(ALL, None), P(ALL, None), P(ALL), P(ALL), P(ALL), P(), P(), P(), token)
    out_specs = (token, token, P(ALL, None), P(ALL, None), P(ALL, None), P(ALL), P(ALL), P(ALL), P(), P(), P())
    return jax.shard_map(body, mesh=split, in_specs=in_specs, out_specs=out_specs, check_vma=False)
```

```python
import functools

import jax
import jax.numpy as jnp
import numpy as np
from jax import lax
from jax.experimental import pallas as pl
from jax.experimental.pallas import tpu as pltpu
from jax.sharding import Mesh
from jax.sharding import PartitionSpec as P

DI = 3072
H = 48
PS = 64
N = 128
KC = 4
CONV = 3328
D = 1536
T = 256
HH = H // 2
W = DI // 2
XC = W + 2 * N
XP = XC + 128
EPS = 1e-05
NEG = -1e30
LOG2E = 1.4426950408889634
HT = T // 2
f32 = jnp.float32
bf16 = jnp.bfloat16
HIGH = lax.Precision.HIGHEST
ALL = ("za", "zb", "zl", "s", "c")
Z = ("za", "zb")
MB_ = 1 << 20


def nn(a, b):
    return lax.dot_general(a, b, (((1,), (0,)), ((), ())), preferred_element_type=f32)


def nt(a, b):
    return lax.dot_general(a, b, (((1,), (1,)), ((), ())), preferred_element_type=f32)


def tn(a, b):
    return lax.dot_general(a, b, (((0,), (0,)), ((), ())), preferred_element_type=f32)


def halves(v):
    high = v.astype(bf16)
    return high, (v - high.astype(f32)).astype(bf16)


def fine(dot, a, b):
    (ah, al), (bh, bl) = halves(a), halves(b)
    return dot(ah, bh) + (dot(ah, bl) + dot(al, bh))


def iota(shape, dim):
    return lax.broadcasted_iota(jnp.int32, shape, dim)


def spread(cols, first, heads):
    rows = cols.shape[0]
    head = iota((rows, heads * PS), 1) // PS
    out = jnp.broadcast_to(cols[:, first : first + 1], (rows, heads * PS))
    for i in range(1, heads):
        out = jnp.where(head == i, cols[:, first + i : first + i + 1], out)
    return out


def per_head(values, first):
    lanes = values.shape[1]
    place = (iota((lanes, 128), 0) // PS + first == iota((lanes, 128), 1)).astype(bf16)
    high, low = halves(values)
    return nn(high, place) + nn(low, place)


def row_sum(values):
    return jnp.sum(values, axis=0, keepdims=True)


def conv_taps(pad_ref, cw_ref, lanes):
    total = cw_ref[4:5, lanes]
    for k in range(KC):
        total = total + cw_ref[k : k + 1, lanes] * pad_ref[pl.ds(5 + k, T), lanes]
    return total


def softplus(v):
    return jnp.maximum(v, 0.0) + jnp.log1p(jnp.exp(-jnp.abs(v)))


def params(**kw):
    return pltpu.CompilerParams(vmem_limit_bytes=40 * MB_, **kw)


def cost(flops, nbytes, trans=0):
    return pl.CostEstimate(flops=int(flops), bytes_accessed=int(nbytes), transcendentals=int(trans))


def norm_kernel(blocks, hid, rim, gain, out):
    j = pl.program_id(0)

    def scaled(v):
        v = v.astype(f32)
        return (v * lax.rsqrt(jnp.mean(v * v, axis=-1, keepdims=True) + EPS) * gain[0:1]).astype(bf16)

    @pl.when(j < blocks)
    def _():
        out[...] = scaled(hid[...])

    @pl.when(j == blocks)
    def _():
        out[: rim.shape[0]] = scaled(rim[...])


def pre_norm(hid, rim, gain):
    rows, extra = hid.shape[0], rim.shape[0]
    blocks = rows // T
    return pl.pallas_call(
        functools.partial(norm_kernel, blocks),
        name="pre_norm",
        grid=(blocks + 1,),
        in_specs=[
            pl.BlockSpec((T, D), lambda j: (jnp.minimum(j, blocks - 1), 0)),
            pl.BlockSpec((extra, D), lambda j: (0, 0)),
            pl.BlockSpec((1, D), lambda j: (0, 0)),
        ],
        out_specs=pl.BlockSpec((T, D), lambda j: (j, 0)),
        out_shape=jax.ShapeDtypeStruct((rows + extra, D), bf16),
        compiler_params=params(),
        cost_estimate=cost(6 * rows * D, 4 * rows * D),
    )(hid, rim, gain)


def states_kernel(xbc, halo, cw, hp, x, bc, s, dt, ld, ldt, st0, comb, dec, pad, tail, carry, xw):
    j = pl.program_id(0)
    m, b = j // 2, j % 2
    before = jnp.where(b == 0, halo[pl.ds(8 * m, 8), :XC], tail[...])
    pad[0:8] = before
    pad[8 : 8 + T] = xbc[:, :XC]
    tail[...] = xbc[T - 8 : T, :XC]
    step = softplus(xbc[:, XC:XP] + hp[0:1, :])
    step = jnp.where(iota((T, 128), 1) < HH, step, 0.0)
    tri = (iota((T, T), 0) >= iota((T, T), 1)).astype(f32)
    logd = jnp.dot(tri, -hp[1:2, :] * step, precision=HIGH, preferred_element_type=f32)
    dt[...] = step
    ld[...] = logd
    ldt[0] = logd.T[:32]
    tailw = jnp.exp(logd[T - 1 : T] - logd) * step
    lanes = slice(W, XC)
    a = conv_taps(pad, cw, lanes)
    act = a * lax.logistic(a)
    bc[...] = act
    s[...] = fine(nt, act[:, N:], act[:, :N])
    for i in range(W // 128):
        lanes = slice(128 * i, 128 * i + 128)
        a = conv_taps(pad, cw, lanes)
        act_x = a * lax.logistic(a)
        x[:, lanes] = act_x
        xw[:, lanes] = (act_x * spread(tailw, 2 * i, 2)).astype(bf16)
    st = tn(act[:, :N].astype(bf16), xw[...])
    last = jnp.exp(logd[T - 8 : T])
    decay = jnp.concatenate([spread(last, 4 * i, 4) for i in range(W // 256)], axis=1)[7:8]
    dec[0] = jnp.broadcast_to(decay, (8, W))

    @pl.when(b == 0)
    def _():
        st0[0] = st
        carry[...] = st

    @pl.when(b == 1)
    def _():
        comb[0] = (decay * carry[...] + st).astype(bf16)


def block_states(xbc, cw, hp, micros):
    blocks = 2 * micros
    rows = blocks * T
    blk = lambda j: (j % 2) * micros + j // 2
    out = lambda *sh: jax.ShapeDtypeStruct(sh, f32)
    whole = lambda a: pl.BlockSpec(a.shape, lambda j: (0, 0))
    return pl.pallas_call(
        states_kernel,
        name="block_states",
        grid=(blocks,),
        in_specs=[
            pl.BlockSpec((T, XP), lambda j: (blk(j), 0)),
            pl.BlockSpec((8 * micros, XP), lambda j: (rows // (8 * micros), 0)),
            whole(cw),
            whole(hp),
        ],
        out_specs=[
            pl.BlockSpec((T, W), lambda j: (blk(j), 0)),
            pl.BlockSpec((T, 2 * N), lambda j: (blk(j), 0)),
            pl.BlockSpec((T, T), lambda j: (blk(j), 0)),
            pl.BlockSpec((T, 128), lambda j: (blk(j), 0)),
            pl.BlockSpec((T, 128), lambda j: (blk(j), 0)),
            pl.BlockSpec((1, 32, T), lambda j: (blk(j), 0, 0)),
            pl.BlockSpec((1, N, W), lambda j: (j // 2, 0, 0)),
            pl.BlockSpec((1, N, W), lambda j: (j // 2, 0, 0)),
            pl.BlockSpec((1, 8, W), lambda j: (blk(j), 0, 0)),
        ],
        out_shape=[
            out(rows, W),
            out(rows, 2 * N),
            out(rows, T),
            out(rows, 128),
            out(rows, 128),
            out(blocks, 32, T),
            out(micros, N, W),
            jax.ShapeDtypeStruct((micros, N, W), bf16),
            out(blocks, 8, W),
        ],
        scratch_shapes=[
            pltpu.VMEM((T + 8, XC), f32),
            pltpu.VMEM((8, XC), f32),
            pltpu.VMEM((N, W), f32),
            pltpu.VMEM((T, W), bf16),
        ],
        compiler_params=params(),
        cost_estimate=cost(blocks * 2 * T * N * W, rows * (XP + W + 800) * 4, rows * XC * 2),
    )(xbc, xbc, cw, hp)


def inner_kernel(s, ld, ldt, dt, x, skip, y):
    g = pl.program_id(1)
    shift = lax.rem(128 - 8 * g, 128)
    logd = pltpu.roll(ld[...], shift, 1) * LOG2E
    step = pltpu.roll(dt[...], shift, 1)
    upper = iota((HT, HT), 0) >= iota((HT, HT), 1)
    lower = iota((HT, T), 0) + HT >= iota((HT, T), 1)
    head = iota((T, 256), 1) // PS
    for q in range(2):
        lanes = slice(256 * q, 256 * q + 256)
        tile = x[:, lanes]
        xdt = tile * spread(step, 4 * q, 4)
        top = skip[0:1, lanes] * tile[:HT]
        bottom = skip[0:1, lanes] * tile[HT:]
        for i in range(4):
            h = 4 * q + i
            row = ldt[0, pl.ds(8 * g + h, 1), :] * LOG2E
            col = logd[:, h : h + 1]
            mine = jnp.where(head == i, xdt, 0.0).astype(bf16)
            decay = jnp.exp2(jnp.where(upper, col[:HT] - row[:, :HT], NEG))
            top = top + nn((decay * s[:HT, :HT]).astype(bf16), mine[:HT])
            decay = jnp.exp2(jnp.where(lower, col[HT:] - row, NEG))
            bottom = bottom + nn((decay * s[HT:, :]).astype(bf16), mine)
        y[:HT, lanes] = top
        y[HT:, lanes] = bottom


def inner_part(s, ld, ldt, dt, x, skip_row):
    rows = x.shape[0]
    blocks, groups = rows // T, W // 512
    return pl.pallas_call(
        inner_kernel,
        name="inner_part",
        grid=(blocks, groups),
        in_specs=[
            pl.BlockSpec((T, T), lambda j, g: (j, 0)),
            pl.BlockSpec((T, 128), lambda j, g: (j, 0)),
            pl.BlockSpec((1, 32, T), lambda j, g: (j, 0, 0)),
            pl.BlockSpec((T, 128), lambda j, g: (j, 0)),
            pl.BlockSpec((T, 512), lambda j, g: (j, g)),
            pl.BlockSpec((8, 512), lambda j, g: (0, g)),
        ],
        out_specs=pl.BlockSpec((T, 512), lambda j, g: (j, g)),
        out_shape=jax.ShapeDtypeStruct((rows, W), f32),
        compiler_params=params(),
        cost_estimate=cost(
            blocks * HH * 2 * T * T * 256, rows * (2 * W + 1024) * 4, blocks * HH * T * T
        ),
    )(s, ld, ldt, dt, x, skip_row)


def gate_kernel(yin, bc, e, ld, z, y, sums):
    grow = jnp.exp(ld[...])
    cst = bc[:, N:].astype(bf16)
    squares = jnp.zeros((T, 256), f32)
    for i in range(W // 256):
        lanes = slice(256 * i, 256 * i + 256)
        out = yin[:, lanes] + spread(grow, 4 * i, 4) * nn(cst, e[0, :, lanes])
        y[:, lanes] = out
        zt = z[:, lanes]
        g = out * (zt * lax.logistic(zt))
        squares = squares + g * g
    sums[...] = jnp.broadcast_to(jnp.sum(squares, axis=1, keepdims=True), (T, 128))


def gate_part(yin, bc, e, ld, z):
    rows = yin.shape[0]
    blocks = rows // T
    row = lambda c: pl.BlockSpec((T, c), lambda j: (j, 0))
    return pl.pallas_call(
        gate_kernel,
        name="gate_part",
        grid=(blocks,),
        in_specs=[
            row(W),
            row(2 * N),
            pl.BlockSpec((1, N, W), lambda j: (j, 0, 0)),
            row(128),
            row(W),
        ],
        out_specs=[row(W), row(128)],
        out_shape=[
            jax.ShapeDtypeStruct((rows, W), f32),
            jax.ShapeDtypeStruct((rows, 128), f32),
        ],
        input_output_aliases={0: 0},
        compiler_params=params(),
        cost_estimate=cost(2 * rows * N * W, rows * W * 4 * 3, rows * W * 2),
    )(yin, bc, e, ld, z)


def out_back_kernel(cot, w, exact, gfin, dots):
    g = nt(cot[...], w[...])
    gfin[...] = g
    dots[...] = jnp.broadcast_to(jnp.sum(g * exact[...], axis=1, keepdims=True), dots.shape)


def out_back(cot, w, exact):
    rows = cot.shape[0]
    row = lambda c: pl.BlockSpec((T, c), lambda j: (j, 0))
    return pl.pallas_call(
        out_back_kernel,
        name="out_back",
        grid=(rows // T,),
        in_specs=[row(D), pl.BlockSpec((W, D), lambda j: (0, 0)), row(W)],
        out_specs=[row(W), row(128)],
        out_shape=[jax.ShapeDtypeStruct((rows, W), f32), jax.ShapeDtypeStruct((rows, 128), f32)],
        compiler_params=params(),
        cost_estimate=cost(2 * rows * D * W, rows * W * 10 + 2 * D * W),
    )(cot, w, exact)


def gate_back_kernel(
    y, z, gfin, x, sums, dots, bc, e, ld, gain, skip, dec, dz, dy, dc, de1, given, dl, ggain, gskip, dye, keep
):
    j = pl.program_id(0)

    @pl.when(j == 0)
    def _():
        ggain[...] = jnp.zeros_like(ggain)
        gskip[...] = jnp.zeros_like(gskip)

    r = lax.rsqrt(sums[:, 0:1] * (1.0 / DI) + EPS)
    coef = r * r * dots[:, 0:1] * (1.0 / DI)
    grow = jnp.exp(ld[...])
    dlog = jnp.zeros((T, 128), f32)
    dcs = jnp.zeros((T, N), f32)
    for i in range(W // 256):
        lanes = slice(256 * i, 256 * i + 256)
        zt, yt, gf = z[:, lanes], y[:, lanes], gfin[:, lanes]
        sg = lax.logistic(zt)
        silu = zt * sg
        g = yt * silu
        gr = g * r
        ggain[0:1, lanes] += row_sum(gf * gr)
        dg = r * (gf * gain[0:1, lanes]) - g * coef
        dyt = dg * silu
        dz[:, lanes] = (dg * yt * (sg * (1.0 + zt * (1.0 - sg)))).astype(bf16)
        dy[:, lanes] = dyt.astype(bf16)
        xt = x[:, lanes]
        gskip[0:1, lanes] += row_sum(dyt * xt)
        dlog = dlog + per_head(dyt * (yt - skip[0:1, lanes] * xt), 4 * i)
        high, low = halves(dyt * spread(grow, 4 * i, 4))
        dye[:, lanes] = high
        dcs = dcs + (nt(high, e[0, :, lanes]) + nt(low, e[0, :, lanes]))
    dl[...] = dlog
    dc[...] = dcs
    de = tn(bc[:, N:].astype(bf16), dye[...])

    @pl.when(j % 2 == 0)
    def _():
        de1[0] = de
        keep[...] = de

    @pl.when(j % 2 == 1)
    def _():
        given[0] = (de + dec[0, 0:1] * keep[...]).astype(bf16)


def gate_back(y, z, gfin, x, sums, dots, bc, e, ld, gain, skip_row, dec, micros):
    rows = y.shape[0]
    blocks = rows // T
    blk = lambda p: (1 - p % 2) * micros + p // 2
    row = lambda c: pl.BlockSpec((T, c), lambda p: (blk(p), 0))
    fixed = pl.BlockSpec((8, W), lambda p: (0, 0))
    state = pl.BlockSpec((1, N, W), lambda p: (blk(p), 0, 0))
    chip = pl.BlockSpec((1, N, W), lambda p: (p // 2, 0, 0))
    sh = jax.ShapeDtypeStruct
    return pl.pallas_call(
        gate_back_kernel,
        name="gate_back",
        grid=(blocks,),
        in_specs=[
            row(W), row(W), row(W), row(W), row(128), row(128), row(2 * N), state, row(128),
            fixed, fixed, pl.BlockSpec((1, 8, W), lambda p: (blk(p), 0, 0)),
        ],
        out_specs=[row(W), row(W), row(N), chip, chip, row(128), fixed, fixed],
        out_shape=[
            sh((rows, W), bf16),
            sh((rows, W), bf16),
            sh((rows, N), f32),
            sh((micros, N, W), f32),
            sh((micros, N, W), bf16),
            sh((rows, 128), f32),
            sh((8, W), f32),
            sh((8, W), f32),
        ],
        scratch_shapes=[pltpu.VMEM((T, W), bf16), pltpu.VMEM((N, W), f32)],
        compiler_params=params(),
        cost_estimate=cost(8 * rows * N * W, rows * W * 24, rows * W * 2),
    )(y, z, gfin, x, sums, dots, bc, e, ld, gain, skip_row, dec)


def inner_back_kernel(s, bc, ld, ldt, dt, x, dy, skip, dx, xv, dbc, st, dst):
    g = pl.program_id(1)

    @pl.when(g == 0)
    def _():
        st[...] = s[...].T
        dst[...] = jnp.zeros_like(dst)
        xv[...] = jnp.zeros_like(xv)

    shift = lax.rem(128 - 8 * g, 128)
    logd = pltpu.roll(ld[...], shift, 1) * LOG2E
    step = pltpu.roll(dt[...], shift, 1)
    early = iota((HT, T), 1) >= iota((HT, T), 0)
    late = iota((HT, HT), 1) >= iota((HT, HT), 0)
    head = iota((T, 256), 1) // PS
    gtop = jnp.zeros((HT, T), f32)
    gbottom = jnp.zeros((HT, HT), f32)
    sums = jnp.zeros((T, 128), f32)
    for q in range(2):
        lanes = slice(256 * q, 256 * q + 256)
        steps = spread(step, 4 * q, 4)
        tile = x[:, lanes]
        xdt = tile * steps
        dyt = dy[:, lanes]
        top = jnp.zeros((HT, 256), f32)
        bottom = jnp.zeros((HT, 256), f32)
        for i in range(4):
            h = 4 * q + i
            row = ldt[0, pl.ds(8 * g + h, 1), :] * LOG2E
            col = logd[:, h : h + 1]
            dmine = jnp.where(head == i, dyt, jnp.zeros_like(dyt))
            xmine = jnp.where(head == i, xdt, 0.0).astype(bf16)
            decay = jnp.exp2(jnp.where(early, row - col[:HT], NEG))
            top = top + nn((decay * st[:HT, :]).astype(bf16), dmine)
            gtop = gtop + nt(xmine[:HT], dyt) * decay
            decay = jnp.exp2(jnp.where(late, row[:, HT:] - col[HT:], NEG))
            bottom = bottom + nn((decay * st[HT:, HT:]).astype(bf16), dmine[HT:])
            gbottom = gbottom + nt(xmine[HT:], dyt[HT:]) * decay
        total = jnp.concatenate([top, bottom], axis=0)
        dx[:, lanes] = total * steps + skip[0:1, lanes] * dyt.astype(f32)
        sums = sums + per_head(tile * total, 8 * g + 4 * q)
    xv[...] += sums
    dst[:HT, :] += gtop
    dst[HT:, HT:] += gbottom

    @pl.when(g == pl.num_programs(1) - 1)
    def _():
        dbc[:, :N] = fine(nn, dst[...], bc[:, N:])
        dbc[:, N:] = fine(tn, dst[...], bc[:, :N])


def inner_back(s, bc, ld, ldt, dt, x, dy, skip_row):
    rows = x.shape[0]
    blocks, groups = rows // T, W // 512
    row = lambda c: pl.BlockSpec((T, c), lambda j, g: (j, 0))
    tile = pl.BlockSpec((T, 512), lambda j, g: (j, g))
    sh = jax.ShapeDtypeStruct
    return pl.pallas_call(
        inner_back_kernel,
        name="inner_back",
        grid=(blocks, groups),
        in_specs=[
            row(T),
            row(2 * N),
            row(128),
            pl.BlockSpec((1, 32, T), lambda j, g: (j, 0, 0)),
            row(128),
            tile,
            tile,
            pl.BlockSpec((8, 512), lambda j, g: (0, g)),
        ],
        out_specs=[tile, row(128), row(2 * N)],
        out_shape=[sh((rows, W), f32), sh((rows, 128), f32), sh((rows, 2 * N), f32)],
        scratch_shapes=[pltpu.VMEM((T, T), f32), pltpu.VMEM((T, T), f32)],
        compiler_params=params(),
        cost_estimate=cost(
            2 * blocks * HH * 2 * T * T * 256, rows * (2 * W + 1024) * 4, blocks * HH * T * T
        ),
    )(s, bc, ld, ldt, dt, x, dy, skip_row)


def conv_back_kernel(
    micros, xbc, prev, x, dxi, xv, dbc, bc, dt, ld, later1, de1, dec, e, dc, dla, cw, hp,
    gp, gcw, ghp, pad, dpre, nxt, edge,
):
    p = pl.program_id(0)
    b = 1 - p % 2

    @pl.when(p == 0)
    def _():
        gcw[...] = jnp.zeros_like(gcw)
        ghp[...] = jnp.zeros_like(ghp)

    @pl.when(p == 2 * micros)
    def _():
        gp[0 : 8 * micros] = edge[...].astype(bf16)

    @pl.when(p < 2 * micros)
    def _():
        pad[0:8] = prev[:, :XC]
        pad[8 : 8 + T] = xbc[:, :XC]
        dpre[0:8] = jnp.zeros((8, XC), f32)
        dpre[8 + T : 16 + T] = jnp.where(b == 1, 0.0, nxt[...])
        step, logd = dt[...], ld[...]
        fade = jnp.exp(logd[T - 1 : T] - logd)
        tailw = fade * step
        bst = bc[:, :N].astype(bf16)

        def through_conv(grad, lanes):
            a = conv_taps(pad, cw, lanes)
            sg = lax.logistic(a)
            d = grad * (sg * (1.0 + a * (1.0 - sg)))
            dpre[8 : 8 + T, lanes] = d
            gcw[4:5, lanes] += row_sum(d)
            for k in range(KC):
                gcw[k : k + 1, lanes] += row_sum(d * pad[pl.ds(5 + k, T), lanes])
            total = cw[0:1, lanes] * dpre[pl.ds(11, T), lanes]
            rim = cw[0:1, lanes] * dpre[pl.ds(3, 8), lanes]
            for k in range(1, KC):
                total = total + cw[k : k + 1, lanes] * dpre[pl.ds(11 - k, T), lanes]
                rim = rim + cw[k : k + 1, lanes] * dpre[pl.ds(3 - k, 8), lanes]
            gp[:, lanes] = total.astype(bf16)
            nxt[:, lanes] = d[0:8]

            @pl.when(b == 0)
            def _():
                edge[pl.ds(pl.multiple_of(8 * (p // 2), 8), 8), lanes] = rim

        dw = jnp.zeros((T, 128), f32)
        dbs = jnp.zeros((T, N), f32)
        ddec = jnp.zeros((8, 128), f32)
        for i in range(W // 256):
            lanes = slice(256 * i, 256 * i + 256)
            lat = later1[0, :, lanes]
            earlier = de1[0, :, lanes] + dec[0, 0:1, lanes] * lat.astype(f32)
            lat = jnp.where(b == 1, lat, earlier.astype(bf16))
            spreadw = spread(tailw, 4 * i, 4)
            xt = x[:, lanes]
            bl = nn(bst, lat)
            dw = dw + per_head(xt * bl, 4 * i)
            high, low = halves(xt * spreadw)
            dbs = dbs + (nt(high, lat) + nt(low, lat))
            both = row_sum(lat.astype(f32) * e[0, :, lanes].astype(f32))
            ddec = ddec + per_head(jnp.broadcast_to(both, (8, 256)), 4 * i)
            through_conv(dxi[:, lanes] + bl * spreadw, lanes)
        through_conv(
            jnp.concatenate([dbc[:, :N] + dbs, dbc[:, N:] + dc[...]], axis=1), slice(W, XC)
        )
        q = dw * tailw
        dlog = dla[...] - step * xv[...] - q
        dlast = row_sum(q) + ddec[0:1] * jnp.exp(logd[T - 1 : T])
        dlog = dlog + jnp.where(iota((T, 128), 0) == T - 1, dlast, 0.0)
        tri = (iota((T, T), 1) >= iota((T, T), 0)).astype(f32)
        dcum = jnp.dot(tri, dlog, precision=HIGH, preferred_element_type=f32)
        dstep = xv[...] + dw * fade - hp[1:2, :] * dcum
        draw = dstep * lax.logistic(xbc[:, XC:XP] + hp[0:1, :])
        draw = jnp.where(iota((T, 128), 1) < HH, draw, 0.0)
        ghp[0:1] += row_sum(draw)
        ghp[1:2] -= row_sum(dcum * step)
        gp[:, XC:XP] = draw.astype(bf16)

        @pl.when(b == 0)
        def _():
            edge[pl.ds(pl.multiple_of(8 * (p // 2), 8), 8), XC:XP] = jnp.zeros((8, 128), f32)


def conv_back(xbc, x, dxi, xv, dbc, bc, dt, ld, later1, de1, dec, e, dc, dla, cw, hp, micros):
    blocks = 2 * micros
    rows = blocks * T
    blk = lambda p: jnp.where(p < blocks, (1 - p % 2) * micros + p // 2, micros - 1)
    row = lambda c: pl.BlockSpec((T, c), lambda p: (blk(p), 0))
    whole = lambda a: pl.BlockSpec(a.shape, lambda p: (0, 0))
    state = pl.BlockSpec((1, N, W), lambda p: (blk(p), 0, 0))

    unit = lambda p: jnp.minimum(p // 2, micros - 1)
    chip = pl.BlockSpec((1, N, W), lambda p: (unit(p), 0, 0))

    def before(p):
        k = blk(p)
        return (jnp.where(k >= micros, (k - micros + 1) * (T // 8) - 1, rows // 8 + k), 0)

    return pl.pallas_call(
        functools.partial(conv_back_kernel, micros),
        name="conv_back",
        grid=(blocks + 1,),
        in_specs=[
            row(XP),
            pl.BlockSpec((8, XP), before),
            row(W), row(W), row(128), row(2 * N), row(2 * N), row(128), row(128),
            chip, chip, pl.BlockSpec((1, 8, W), lambda p: (micros + unit(p), 0, 0)), state,
            row(N), row(128), whole(cw), whole(hp),
        ],
        out_specs=[
            pl.BlockSpec((T, XP), lambda p: (jnp.where(p < blocks, blk(p), blocks), 0)),
            pl.BlockSpec((8, XC), lambda p: (0, 0)),
            pl.BlockSpec((8, 128), lambda p: (0, 0)),
        ],
        out_shape=[
            jax.ShapeDtypeStruct((rows + 8 * micros, XP), bf16),
            jax.ShapeDtypeStruct((8, XC), f32),
            jax.ShapeDtypeStruct((8, 128), f32),
        ],
        scratch_shapes=[
            pltpu.VMEM((T + 8, XC), f32),
            pltpu.VMEM((T + 16, XC), f32),
            pltpu.VMEM((8, XC), f32),
            pltpu.VMEM((8 * micros, XP), f32),
        ],
        compiler_params=pltpu.CompilerParams(vmem_limit_bytes=58 * MB_),
        cost_estimate=cost(6 * rows * N * W, rows * W * 18, rows * XC * 2),
    )(xbc, xbc, x, dxi, xv, dbc, bc, dt, ld, later1, de1, dec, e, dc, dla, cw, hp)


AXIS = {"z": Z, "l": "zl", "s": "s"}
RING = 4
CHIPS = 16


def hop(value, axis):
    n = RING if axis == "z" else 2
    return lax.ppermute(value, AXIS[axis], [(i, (i + 1) % n) for i in range(n)])


def fence(groups, *values):
    held = [{k: g.live[k] for k in g.live} for g in groups]
    held, values = lax.optimization_barrier((held, values))
    for g, h in zip(groups, held):
        g.live.update(h)
    return values


def after(groups, *values):
    values, _ = lax.optimization_barrier((values, [v for g in groups for v in g.sent]))
    for g in groups:
        g.sent = ()
    return values


class Moves:
    sent = ()

    def send(self, value, axis):
        self.sent = [*self.sent, value]
        return hop(value, axis)


WAYS = (("s", "l"), ("l", "s"))


def lanes_of(widths):
    return [slice(sum(widths[:c]), sum(widths[: c + 1])) for c in range(len(widths))]


def near(c, kl, ks):
    return (ks, kl) if c == 0 else (kl, ks)


class Gather(Moves):
    def __init__(self, own, widths, turns):
        self.widths, self.turns = widths, turns
        self.live = {"g0": own}
        self.n = 1
        self.parts = []

    def z(self):
        self.live[f"g{self.n}"] = self.send(self.live[f"g{self.n - 1}"], "z")
        self.n += 1

    def first(self, h):
        some = jnp.stack([self.live[f"g{k}"] for k in self.turns[h]], 0)
        for k in self.turns[h]:
            if k < self.n - 1 or self.n == RING:
                self.live.pop(f"g{k}")
        for c, lanes in enumerate(lanes_of(self.widths)):
            self.live[f"p{h}{c}"] = some[:, :, lanes]
            self.live[f"q{h}{c}"] = self.send(some[:, :, lanes], WAYS[c][0])

    def second(self, h):
        for c in range(2):
            more = jnp.concatenate([self.live.pop(f"p{h}{c}"), self.live.pop(f"q{h}{c}")], 0)
            self.parts += [more, self.send(more, WAYS[c][1])]

    def place(self, c, kz, kl, ks):
        ka, kb = near(c, kl, ks)
        h = [kz in t for t in self.turns].index(True)
        turn = self.turns[h]
        return (h * 2 + c) * 2 + kb, ka * len(turn) + turn.index(kz)


class RingLast(Moves):
    def __init__(self, own, widths):
        self.widths = widths
        self.live = {f"p{c}": own[None, :, lanes] for c, lanes in enumerate(lanes_of(widths))}
        self.parts = []

    def step(self, n):
        for c in range(2):
            p = self.live[f"p{c}"]
            self.live[f"p{c}"] = jnp.concatenate([p, self.send(p, WAYS[c][n])], 0)

    def z(self):
        if not self.parts:
            self.live["p"] = jnp.concatenate([self.live.pop("p0"), self.live.pop("p1")], 0)
            self.parts = [self.live["p"]]
        self.live["p"] = self.send(self.live["p"], "z")
        self.parts.append(self.live["p"])

    def place(self, c, kz, kl, ks):
        ka, kb = near(c, kl, ks)
        return kz, c * 4 + kb * 2 + ka


class Scatter(Moves):
    def __init__(self, widths, turns):
        self.widths, self.turns = widths, turns
        self.live = {}
        self.order = [k for t in turns for k in t]

    def load(self, parts):
        parts = iter(parts)
        for h in range(len(self.turns)):
            for c in range(2):
                self.live[f"k{h}{c}"] = next(parts)
                self.live[f"s{h}{c}"] = next(parts)

    def second(self, h):
        for c in range(2):
            self.live[f"r{h}{c}"] = self.send(self.live.pop(f"s{h}{c}"), WAYS[c][1])

    def first(self, h):
        n = len(self.turns[h])
        for c in range(2):
            got, kept = self.live.pop(f"r{h}{c}"), self.live.pop(f"k{h}{c}")
            self.live[f"m{h}{c}"] = got[:n].astype(f32) + kept[:n].astype(f32)
            give = (got[n:].astype(f32) + kept[n:].astype(f32)).astype(bf16)
            self.live[f"n{h}{c}"] = self.send(give, WAYS[c][0])

    def ring(self, k):
        h = [self.order[k] in t for t in self.turns].index(True)
        at = self.turns[h].index(self.order[k])
        if at == 0:
            self.live["w"] = jnp.concatenate(
                [self.live.pop(f"m{h}{c}") + self.live.pop(f"n{h}{c}").astype(f32) for c in range(2)], 2
            )
        total = self.live["w"][at]
        if k:
            total = total + self.live.pop("t").astype(f32)
        if k == RING - 1:
            self.live.pop("w")
            return total
        self.live["t"] = self.send(total.astype(bf16), "z")

    def place(self, c, kz, kl, ks):
        ka, kb = near(c, kl, ks)
        h = [kz in t for t in self.turns].index(True)
        turn = self.turns[h]
        return (h * 2 + c) * 2 + kb, ka * len(turn) + turn.index(kz)

    def shapes(self, r):
        return [
            jax.ShapeDtypeStruct((2 * len(t), r, w), bf16)
            for t in self.turns
            for w in self.widths
            for _ in range(2)
        ]


def move_kernel(table, r, out_of, where, *refs):
    sems = refs[-1]
    refs = refs[:-1]
    whole = refs[-1] if out_of else refs[0]
    arrays = refs[:-1] if out_of else refs[1:]
    copies = []
    for n, (array, entry, k, lanes) in enumerate(table):
        row = pl.multiple_of(where[k] * r, 16)
        place = whole.at[pl.ds(row, r), lanes]
        piece = arrays[array].at[entry]
        pair = (piece, place) if out_of else (place, piece)
        copies.append(pltpu.make_async_copy(*pair, sems.at[n]))
    for c in copies:
        c.start()
    for c in copies:
        c.wait()


def move(group, where, r, given, shapes, out_of):
    table = []
    for c, lanes in enumerate(lanes_of(group.widths)):
        for k in range(CHIPS):
            table.append((*group.place(c, k // 4, k // 2 % 2, k % 2), k, lanes))
    any_ = pl.BlockSpec(memory_space=pl.ANY)
    return pl.pallas_call(
        functools.partial(move_kernel, tuple(table), r, out_of),
        name="join" if out_of else "deal",
        in_specs=[pl.BlockSpec(memory_space=pltpu.SMEM)] + [any_] * len(given),
        out_specs=[any_] * len(shapes),
        out_shape=shapes,
        scratch_shapes=[pltpu.SemaphoreType.DMA((len(table),))],
        compiler_params=pltpu.CompilerParams(vmem_limit_bytes=MB_),
        cost_estimate=cost(0, 4 * CHIPS * r * sum(group.widths)),
    )(where, *given)


def join(group, where, r):
    shape = jax.ShapeDtypeStruct((CHIPS * r, sum(group.widths)), bf16)
    return move(group, where, r, group.parts, [shape], True)[0]


def deal(group, where, r, whole):
    group.load(move(group, where, r, [whole], group.shapes(r), False))


def swap(value, axis="c"):
    return lax.ppermute(value, axis, [(0, 1), (1, 0)])


def two(mine, other, at):
    return jnp.where(at == 0, jnp.stack([mine, other]), jnp.stack([other, mine]))


class Plain:
    def __init__(self, axes):
        self.axes = axes

    def gather(self, piece):
        return lax.all_gather(piece, self.axes, axis=0, tiled=True)

    def reduce(self, grad):
        return lax.psum_scatter(grad, self.axes, scatter_dimension=0, tiled=True).astype(f32)


def body(
    hidden, in_weight, out_weight, conv_weight, conv_bias, norm_gain, gate_gain,
    step_bias, decay_rate, skip_gain, cotangent,
):
    nz, nl, ns = lax.axis_size(Z), lax.axis_size("zl"), lax.axis_size("s")
    core = lax.axis_index("c")
    micros = hidden.shape[0]
    rows = micros * 2 * T
    r_in, r_out = in_weight.shape[0], out_weight.shape[0]
    r = 2 * r_in
    fast = (nz, nl, ns) == (RING, 2, 2) and r % 16 == 0 and r_out == r
    onward = [(i, i + 1) for i in range(ns - 1)]
    backward = [(i + 1, i) for i in range(ns - 1)]
    turn = [(a * 2 + b, b * 2 + a) for a in range(2) for b in range(2)]

    def cut(k):
        part = lambda at, width: lax.dynamic_slice_in_dim(in_weight, at + k * width, width, 1)
        steps = in_weight[:, DI + CONV :]
        steps = jnp.where(k == 0, steps[:, :HH], steps[:, HH:])
        return jnp.concatenate(
            [
                part(DI, W),
                in_weight[:, 2 * DI : 2 * DI + 2 * N],
                jnp.pad(steps, ((0, 0), (0, 128 - HH))),
                part(0, W),
            ],
            axis=1,
        )

    ours, theirs = cut(core), cut(1 - core)
    theirs, out_weight, hidden, cotangent = lax.optimization_barrier(
        (theirs, out_weight, hidden, cotangent)
    )
    chip_rows = two(ours, swap(theirs), core).reshape(r, -1)
    w_own = lax.ppermute(out_weight, ("za", "c"), turn)

    ins = Plain(ALL[:4])
    outs = Plain(("zb", "zl", "s", "za"))

    n_c = conv_bias.shape[0]
    packed = jnp.concatenate([conv_weight.T.reshape(-1), conv_bias, norm_gain, gate_gain])

    def spread_out(small, a, at):
        mine, other = (jnp.expand_dims(v, at) for v in (small, swap(small, a)))
        here = lax.axis_index(a) == 0
        return jnp.where(here, jnp.concatenate([mine, other], at), jnp.concatenate([other, mine], at))

    hid_own = hidden.reshape(micros, T, D)
    cot_own = cotangent.reshape(micros, T, D)
    hid_other, cot_other = swap(hid_own), swap(cot_own)

    def chip_tokens(mine, other):
        return two(mine, other, core).reshape(rows, D)

    def rim_of(tokens):
        return lax.ppermute(tokens.reshape(2, micros, T, D)[1, :, T - 8 :], "s", onward)

    if fast:
        back = jnp.arange(CHIPS)
        kz = (lax.axis_index(Z) - back // 4) % RING
        kl = (lax.axis_index("zl") - back // 2) % 2
        ks = (lax.axis_index("s") - back) % 2
        in_place = ((kz * 2 + kl) * 2 + ks).astype(jnp.int32)
        out_place = ((((kz % 2) * 2 + kl) * 2 + ks) * 2 + kz // 2).astype(jnp.int32)
        x_cols, z_cols, o_cols = (896, 1024), (768, 768), (768, 768)
        small = spread_out(packed, "za", 0)
        small = spread_out(small, "zb", 1)
        chip_rows, small = lax.optimization_barrier((chip_rows, small))
        halves_, ring_ = ((0, 1), (2, 3)), ((0, 1, 2, 3),)
        gx_ = Gather(chip_rows[:, :XP], x_cols, halves_)
        gz_ = Gather(chip_rows[:, XP:], z_cols, ring_)
        go_ = RingLast(w_own, o_cols)
        every = [gx_, gz_, go_]
        small = spread_out(small, "zl", 2)
        gx_.z()
        go_.step(0)
        small, hid_other, cot_other = fence(every, small, hid_other, cot_other)
        small = spread_out(small, "s", 3)
        gx_.z()
        gx_.first(0)
        go_.step(1)
        hid_own_, hid_other = after(every, hid_own, hid_other)
        hid_all = chip_tokens(hid_own_, hid_other)
        rim = rim_of(hid_all)
        small = spread_out(small, "c", 4).reshape(-1, packed.shape[0])
        small, rim, hid_all = fence(every, small, rim, hid_all)
        gx_.z()
        gx_.second(0)
        gz_.z()
        small, rim, hid_all, cot_own_, cot_other = after(
            every, small, rim, hid_all, cot_own, cot_other
        )
        cot_all = chip_tokens(cot_own_, cot_other)
    else:
        small = lax.all_gather(packed, ALL)
        hid_all, cot_all = chip_tokens(hid_own, hid_other), chip_tokens(cot_own, cot_other)
        rim = rim_of(hid_all)
        w_x, w_z = ins.gather(chip_rows[:, :XP]), ins.gather(chip_rows[:, XP:])

    rim = jnp.where(iota(rim.shape, 1) >= 5, rim, jnp.zeros_like(rim)).reshape(8 * micros, D)
    devices = small.shape[0]
    taps = small[:, : KC * n_c].reshape(devices, KC, n_c).transpose(1, 0, 2).reshape(KC, CONV)
    bias = small[:, KC * n_c : (KC + 1) * n_c].reshape(1, CONV)
    norm_vec = small[:, (KC + 1) * n_c : (KC + 1) * n_c + r_in].reshape(D).astype(f32)
    gate_vec = small[:, (KC + 1) * n_c + r_in :].reshape(1, DI)
    conv_all = jnp.concatenate([taps, bias, jnp.zeros((3, CONV), bf16)], 0).astype(f32)
    cw = jnp.concatenate(
        [lax.dynamic_slice_in_dim(conv_all, core * W, W, 1), conv_all[:, DI:]], axis=1
    )
    gain = jnp.broadcast_to(lax.dynamic_slice_in_dim(gate_vec, core * W, W, 1).astype(f32), (8, W))
    heads = jnp.stack([step_bias, decay_rate, skip_gain])
    heads = lax.dynamic_slice_in_dim(heads, core * HH, HH, 1)
    hp = jnp.pad(heads, ((0, 5), (0, 128 - HH)))
    skip_row = jnp.broadcast_to(jnp.repeat(heads[2], PS)[None], (8, W))
    normed = pre_norm(hid_all, rim, norm_vec[None])
    if fast:
        normed, cot_all, cw, hp, gain, skip_row = fence(
            every, normed, cot_all, cw, hp, gain, skip_row
        )
        gx_.first(1)
        gz_.z()
        (normed,) = fence([gx_, gz_], normed)
        gx_.second(1)
        gz_.z()
        (normed,) = after([gx_, gz_], normed)

    if fast:
        (normed,) = fence(every, normed)
        gz_.first(0)
        go_.z()
        (normed,) = after([gz_, go_], normed)
        w_x = join(gx_, in_place, r)
    xbc = nn(normed, w_x)
    if fast:
        (xbc,) = fence([gz_], xbc)
        gz_.second(0)
        (xbc,) = after([gz_], xbc)
    else:
        w_o = outs.gather(w_own)
    x, bc, s, dt, ld, ldt, st0, comb, dec8 = block_states(xbc, cw, hp, micros)
    dec = dec8[:, 0].reshape(2, micros, 1, W)
    if fast:
        comb, s = fence([go_], comb, s)
        go_.z()
        (s,) = after([go_], s)
    if ns == 2:
        first = lax.ppermute(comb, "s", onward)
    else:
        first = jnp.zeros_like(comb)
        chip_decay = dec[0] * dec[1]
        for _ in range(ns - 1):
            out = (chip_decay * first.astype(f32) + comb.astype(f32)).astype(bf16)
            first = lax.ppermute(out, "s", onward)
    yin = inner_part(s, ld, ldt, dt, x, skip_row)
    if fast:
        (yin,) = fence([gz_, go_], yin)
        go_.z()
        (yin,) = after([go_], yin)
    second = (dec[0] * first.astype(f32) + st0).astype(bf16)
    entering = jnp.stack([first, second], 0).reshape(2 * micros, N, W)
    if fast:
        w_z = join(gz_, in_place, r)
    z = nn(normed[:rows], w_z)
    y, sums = gate_part(yin, bc, entering, ld, z)
    sums = sums + swap(sums)
    root = lax.rsqrt(sums[:, :1] * (1.0 / DI) + EPS)
    exact = y * (z * lax.logistic(z)) * root * gain[:1]
    fin = exact.astype(bf16)
    g_out = tn(fin, cot_all).astype(bf16)
    if fast:
        ring_back = ((1, 2, 3, 0),)
        so_ = Scatter(o_cols, ring_back)
        deal(so_, out_place, r, g_out)
        (cot_all,) = fence([so_], cot_all)
        so_.second(0)
        (cot_all,) = after([so_], cot_all)
        w_o = join(go_, out_place, r)

    gfin, dots = out_back(cot_all, w_o, exact)

    partial_out = nn(fin, w_o).reshape(2, micros, T, D)
    give = lax.dynamic_index_in_dim(partial_out, 1 - core, 0, False).astype(bf16)
    keep = lax.dynamic_index_in_dim(partial_out, core, 0, False)
    given_out = swap(give)
    block_out = (hid_own.astype(f32) + keep + given_out.astype(f32)).astype(bf16)
    if fast:
        dots, gfin, give = fence([so_], dots, gfin, give)
        so_.first(0)
        (y,) = after([so_], y)
    dots = dots + swap(dots)
    dz, dy, dc, de1, given, dla, ggain, gskip = gate_back(
        y, z, gfin, x, sums, dots, bc, entering, ld, gain, skip_row, dec8, micros
    )
    if ns == 2:
        dz, given = lax.optimization_barrier((dz, given))
        later1 = lax.ppermute(given, "s", backward)
    else:
        later1 = jnp.zeros((micros, N, W), bf16)
        for _ in range(ns - 1):
            out = given.astype(f32) + dec[0] * dec[1] * later1.astype(f32)
            later1 = lax.ppermute(out.astype(bf16), "s", backward)
    gz = tn(normed[:rows], dz).astype(bf16)
    if fast:
        sz_ = Scatter(z_cols, ring_back)
        deal(sz_, in_place, r, gz)
        (dy,) = fence([so_, sz_], dy)
        so_.ring(0)
        sz_.second(0)
        (dy,) = after([so_, sz_], dy)

    dxi, xv, dbc = inner_back(s, bc, ld, ldt, dt, x, dy, skip_row)
    if fast:
        dxi, later1 = fence([so_, sz_], dxi, later1)
        so_.ring(1)
        sz_.first(0)
        (dxi,) = after([so_, sz_], dxi)
    gp, gcw, ghp = conv_back(
        xbc, x, dxi, xv, dbc, bc, dt, ld, later1, de1, dec8, entering, dc, dla, cw, hp, micros
    )
    if fast:
        (gp,) = fence([so_, sz_], gp)
        so_.ring(2)
        sz_.ring(0)
        (gp,) = after([so_, sz_], gp)
    gx = tn(normed, gp).astype(bf16)

    wide = lambda v: jnp.pad(v, ((0, 0), (0, XC - v.shape[1])))
    tiny = jnp.concatenate(
        [gcw[:5], wide(ggain[:1]), wide(gskip[:1]), wide(ghp[:2].reshape(1, 256))], axis=0
    )
    if fast:
        sx_ = Scatter(x_cols, ((1, 2), (3, 0)))
        deal(sx_, in_place, r, gx)
        gp, tiny = fence([so_, sz_, sx_], gp, tiny)
        sx_.second(0)
        sz_.ring(1)
        (gp,) = after([sx_, sz_], gp)
        g_out = so_.ring(3)
    else:
        g_out = outs.reduce(g_out)
    g_out = lax.ppermute(g_out, ("za", "c"), turn)

    gn = nt(gp, w_x)
    edge = lax.ppermute(gn[rows:].astype(bf16), "s", backward).reshape(1, micros, 8, D)
    gn = gn[:rows] + nt(dz, w_z)

    if fast:
        gn, g_out = fence([sz_, sx_], gn, g_out)
        sx_.second(1)
        sx_.first(0)
        sz_.ring(2)
        (gn,) = after([sx_, sz_], gn)
    gn = gn.reshape(2, micros, T, D)
    edge = jnp.where(iota(edge.shape, 2) >= 5, edge.astype(f32), 0.0)
    gn = gn + jnp.pad(edge, ((1, 0), (0, 0), (T - 8, 0), (0, 0)))
    give = lax.dynamic_index_in_dim(gn, 1 - core, 0, False).astype(bf16)
    keep = lax.dynamic_index_in_dim(gn, core, 0, False)
    gn = keep + swap(give).astype(f32)
    hid_f = hid_own.astype(f32)
    own_scale = lax.rsqrt(jnp.mean(hid_f * hid_f, axis=-1, keepdims=True) + EPS)
    unit = hid_f * own_scale
    gq = gn * norm_vec
    g_hid = cot_own.astype(f32) + own_scale * (
        gq - unit * jnp.mean(gq * unit, axis=-1, keepdims=True)
    )

    if fast:
        tiny, g_hid, block_out = fence([sz_, sx_], tiny, g_hid, block_out)
        sx_.first(1)
        sx_.ring(0)
        (tiny,) = after([sx_], tiny)
        tiny = tiny + swap(tiny, "s")
        tiny = tiny + swap(tiny, "zl")
        gz = sz_.ring(3)

    def exchanged(g):
        g = g.reshape(2, r_in, -1)
        mine = lax.dynamic_index_in_dim(g, core, 0, False)
        return two(mine, swap(lax.dynamic_index_in_dim(g, 1 - core, 0, False)), core)

    if fast:
        tiny, gz = fence([sx_], tiny, gz)
        sx_.ring(1)
        tiny, gz = after([sx_], tiny, gz)
        tiny = tiny + swap(tiny, "zb")
        gz = exchanged(gz)
        tiny, gz = fence([sx_], tiny, gz)
        sx_.ring(2)
        (tiny,) = after([sx_], tiny)
        tiny = tiny + swap(tiny, "za")
        (tiny,) = fence([sx_], tiny)
        gx = sx_.ring(3)
    else:
        tiny = lax.psum(tiny, ALL[:4])
        gx, gz = ins.reduce(gx), ins.reduce(gz)
        gz = exchanged(gz)
    gx = exchanged(gx)
    both = two(tiny, swap(tiny), core)
    g_conv = jnp.concatenate([both[0, :5, :W], both[1, :5, :W], both[0, :5, W:] + both[1, :5, W:]], axis=1)
    me = lax.axis_index(ALL)
    g_conv = lax.dynamic_slice_in_dim(g_conv, me * n_c, n_c, 1)
    g_gate = both[:, 5, :W].reshape(-1)
    g_gate = lax.dynamic_slice_in_dim(g_gate, me * r_out, r_out)
    g_skip = both[:, 6, :W].reshape(H, PS).sum(-1)
    g_bias = both[:, 7, :HH].reshape(-1)
    g_rate = both[:, 7, 128 : 128 + HH].reshape(-1)
    g_in = jnp.concatenate(
        [
            gz[0], gz[1],
            gx[0, :, :W], gx[1, :, :W],
            gx[0, :, W:XC] + gx[1, :, W:XC],
            gx[0, :, XC : XC + HH], gx[1, :, XC : XC + HH],
        ],
        axis=1,
    )
    g_norm = jnp.sum(g_in * in_weight.astype(f32), axis=1) / norm_gain.astype(f32)
    return (
        block_out.reshape(hidden.shape),
        g_hid.reshape(hidden.shape),
        g_in,
        g_out,
        g_conv[:KC].T,
        g_conv[KC],
        g_norm,
        g_gate,
        g_bias,
        g_rate,
        g_skip,
    )


def solution(mesh):
    dp, seq = mesh.shape["dp"], mesh.shape["seq"]
    split = Mesh(mesh.devices.reshape(2, dp // 4, 2, seq // 2, 2), ALL)
    token = P(None, ("za", "zb", "zl"), ("s", "c"), None)
    in_specs = (token, P(ALL, None), P(ALL, None), P(ALL, None), P(ALL), P(ALL), P(ALL), P(), P(), P(), token)
    out_specs = (token, token, P(ALL, None), P(ALL, None), P(ALL, None), P(ALL), P(ALL), P(ALL), P(), P(), P())
    return jax.shard_map(body, mesh=split, in_specs=in_specs, out_specs=out_specs, check_vma=False)
```

```python
import functools

import jax
import jax.numpy as jnp
import numpy as np
from jax import lax
from jax.experimental import pallas as pl
from jax.experimental.pallas import tpu as pltpu
from jax.sharding import Mesh
from jax.sharding import PartitionSpec as P

DI = 3072
H = 48
PS = 64
N = 128
KC = 4
CONV = 3328
D = 1536
T = 256
HH = H // 2
W = DI // 2
XC = W + 2 * N
XP = XC + 128
EPS = 1e-05
NEG = -1e30
LOG2E = 1.4426950408889634
HT = T // 2
f32 = jnp.float32
bf16 = jnp.bfloat16
HIGH = lax.Precision.HIGHEST
ALL = ("za", "zb", "zl", "s", "c")
Z = ("za", "zb")
MB_ = 1 << 20


def nn(a, b):
    return lax.dot_general(a, b, (((1,), (0,)), ((), ())), preferred_element_type=f32)


def nt(a, b):
    return lax.dot_general(a, b, (((1,), (1,)), ((), ())), preferred_element_type=f32)


def tn(a, b):
    return lax.dot_general(a, b, (((0,), (0,)), ((), ())), preferred_element_type=f32)


def halves(v):
    high = v.astype(bf16)
    return high, (v - high.astype(f32)).astype(bf16)


def fine(dot, a, b):
    (ah, al), (bh, bl) = halves(a), halves(b)
    return dot(ah, bh) + (dot(ah, bl) + dot(al, bh))


def iota(shape, dim):
    return lax.broadcasted_iota(jnp.int32, shape, dim)


def spread(cols, first, heads):
    rows = cols.shape[0]
    head = iota((rows, heads * PS), 1) // PS
    out = jnp.broadcast_to(cols[:, first : first + 1], (rows, heads * PS))
    for i in range(1, heads):
        out = jnp.where(head == i, cols[:, first + i : first + i + 1], out)
    return out


def per_head(values, first):
    lanes = values.shape[1]
    place = (iota((lanes, 128), 0) // PS + first == iota((lanes, 128), 1)).astype(bf16)
    high, low = halves(values)
    return nn(high, place) + nn(low, place)


def row_sum(values):
    return jnp.sum(values, axis=0, keepdims=True)


def conv_taps(pad_ref, cw_ref, lanes):
    total = cw_ref[4:5, lanes]
    for k in range(KC):
        total = total + cw_ref[k : k + 1, lanes] * pad_ref[pl.ds(5 + k, T), lanes]
    return total


def softplus(v):
    return jnp.maximum(v, 0.0) + jnp.log1p(jnp.exp(-jnp.abs(v)))


def params(**kw):
    return pltpu.CompilerParams(vmem_limit_bytes=40 * MB_, **kw)


def cost(flops, nbytes, trans=0):
    return pl.CostEstimate(flops=int(flops), bytes_accessed=int(nbytes), transcendentals=int(trans))


def norm_kernel(blocks, hid, rim, gain, out):
    j = pl.program_id(0)

    def scaled(v):
        v = v.astype(f32)
        return (v * lax.rsqrt(jnp.mean(v * v, axis=-1, keepdims=True) + EPS) * gain[0:1]).astype(bf16)

    @pl.when(j < blocks)
    def _():
        out[...] = scaled(hid[...])

    @pl.when(j == blocks)
    def _():
        out[: rim.shape[0]] = scaled(rim[...])


def pre_norm(hid, rim, gain):
    rows, extra = hid.shape[0], rim.shape[0]
    blocks = rows // T
    return pl.pallas_call(
        functools.partial(norm_kernel, blocks),
        name="pre_norm",
        grid=(blocks + 1,),
        in_specs=[
            pl.BlockSpec((T, D), lambda j: (jnp.minimum(j, blocks - 1), 0)),
            pl.BlockSpec((extra, D), lambda j: (0, 0)),
            pl.BlockSpec((1, D), lambda j: (0, 0)),
        ],
        out_specs=pl.BlockSpec((T, D), lambda j: (j, 0)),
        out_shape=jax.ShapeDtypeStruct((rows + extra, D), bf16),
        compiler_params=params(),
        cost_estimate=cost(6 * rows * D, 4 * rows * D),
    )(hid, rim, gain)


def states_kernel(xbc, halo, cw, hp, x, bc, s, dt, ld, ldt, st0, comb, dec, pad, tail, carry, xw):
    j = pl.program_id(0)
    m, b = j // 2, j % 2
    before = jnp.where(b == 0, halo[pl.ds(8 * m, 8), :XC], tail[...])
    pad[0:8] = before
    pad[8 : 8 + T] = xbc[:, :XC]
    tail[...] = xbc[T - 8 : T, :XC]
    step = softplus(xbc[:, XC:XP] + hp[0:1, :])
    step = jnp.where(iota((T, 128), 1) < HH, step, 0.0)
    tri = (iota((T, T), 0) >= iota((T, T), 1)).astype(f32)
    logd = jnp.dot(tri, -hp[1:2, :] * step, precision=HIGH, preferred_element_type=f32)
    dt[...] = step
    ld[...] = logd
    ldt[0] = logd.T[:32]
    tailw = jnp.exp(logd[T - 1 : T] - logd) * step
    lanes = slice(W, XC)
    a = conv_taps(pad, cw, lanes)
    act = a * lax.logistic(a)
    bc[...] = act
    s[...] = fine(nt, act[:, N:], act[:, :N])
    for i in range(W // 128):
        lanes = slice(128 * i, 128 * i + 128)
        a = conv_taps(pad, cw, lanes)
        act_x = a * lax.logistic(a)
        x[:, lanes] = act_x
        xw[:, lanes] = (act_x * spread(tailw, 2 * i, 2)).astype(bf16)
    st = tn(act[:, :N].astype(bf16), xw[...])
    last = jnp.exp(logd[T - 8 : T])
    decay = jnp.concatenate([spread(last, 4 * i, 4) for i in range(W // 256)], axis=1)[7:8]
    dec[0] = jnp.broadcast_to(decay, (8, W))

    @pl.when(b == 0)
    def _():
        st0[0] = st
        carry[...] = st

    @pl.when(b == 1)
    def _():
        comb[0] = (decay * carry[...] + st).astype(bf16)


def block_states(xbc, cw, hp, micros):
    blocks = 2 * micros
    rows = blocks * T
    blk = lambda j: (j % 2) * micros + j // 2
    out = lambda *sh: jax.ShapeDtypeStruct(sh, f32)
    whole = lambda a: pl.BlockSpec(a.shape, lambda j: (0, 0))
    return pl.pallas_call(
        states_kernel,
        name="block_states",
        grid=(blocks,),
        in_specs=[
            pl.BlockSpec((T, XP), lambda j: (blk(j), 0)),
            pl.BlockSpec((8 * micros, XP), lambda j: (rows // (8 * micros), 0)),
            whole(cw),
            whole(hp),
        ],
        out_specs=[
            pl.BlockSpec((T, W), lambda j: (blk(j), 0)),
            pl.BlockSpec((T, 2 * N), lambda j: (blk(j), 0)),
            pl.BlockSpec((T, T), lambda j: (blk(j), 0)),
            pl.BlockSpec((T, 128), lambda j: (blk(j), 0)),
            pl.BlockSpec((T, 128), lambda j: (blk(j), 0)),
            pl.BlockSpec((1, 32, T), lambda j: (blk(j), 0, 0)),
            pl.BlockSpec((1, N, W), lambda j: (j // 2, 0, 0)),
            pl.BlockSpec((1, N, W), lambda j: (j // 2, 0, 0)),
            pl.BlockSpec((1, 8, W), lambda j: (blk(j), 0, 0)),
        ],
        out_shape=[
            out(rows, W),
            out(rows, 2 * N),
            out(rows, T),
            out(rows, 128),
            out(rows, 128),
            out(blocks, 32, T),
            out(micros, N, W),
            jax.ShapeDtypeStruct((micros, N, W), bf16),
            out(blocks, 8, W),
        ],
        scratch_shapes=[
            pltpu.VMEM((T + 8, XC), f32),
            pltpu.VMEM((8, XC), f32),
            pltpu.VMEM((N, W), f32),
            pltpu.VMEM((T, W), bf16),
        ],
        compiler_params=params(),
        cost_estimate=cost(blocks * 2 * T * N * W, rows * (XP + W + 800) * 4, rows * XC * 2),
    )(xbc, xbc, cw, hp)


def inner_kernel(s, ld, ldt, dt, x, skip, y):
    g = pl.program_id(1)
    shift = lax.rem(128 - 8 * g, 128)
    logd = pltpu.roll(ld[...], shift, 1) * LOG2E
    step = pltpu.roll(dt[...], shift, 1)
    upper = iota((HT, HT), 0) >= iota((HT, HT), 1)
    lower = iota((HT, T), 0) + HT >= iota((HT, T), 1)
    head = iota((T, 256), 1) // PS
    for q in range(2):
        lanes = slice(256 * q, 256 * q + 256)
        tile = x[:, lanes]
        xdt = tile * spread(step, 4 * q, 4)
        top = skip[0:1, lanes] * tile[:HT]
        bottom = skip[0:1, lanes] * tile[HT:]
        for i in range(4):
            h = 4 * q + i
            row = ldt[0, pl.ds(8 * g + h, 1), :] * LOG2E
            col = logd[:, h : h + 1]
            mine = jnp.where(head == i, xdt, 0.0).astype(bf16)
            decay = jnp.exp2(jnp.where(upper, col[:HT] - row[:, :HT], NEG))
            top = top + nn((decay * s[:HT, :HT]).astype(bf16), mine[:HT])
            decay = jnp.exp2(jnp.where(lower, col[HT:] - row, NEG))
            bottom = bottom + nn((decay * s[HT:, :]).astype(bf16), mine)
        y[:HT, lanes] = top
        y[HT:, lanes] = bottom


def inner_part(s, ld, ldt, dt, x, skip_row):
    rows = x.shape[0]
    blocks, groups = rows // T, W // 512
    return pl.pallas_call(
        inner_kernel,
        name="inner_part",
        grid=(blocks, groups),
        in_specs=[
            pl.BlockSpec((T, T), lambda j, g: (j, 0)),
            pl.BlockSpec((T, 128), lambda j, g: (j, 0)),
            pl.BlockSpec((1, 32, T), lambda j, g: (j, 0, 0)),
            pl.BlockSpec((T, 128), lambda j, g: (j, 0)),
            pl.BlockSpec((T, 512), lambda j, g: (j, g)),
            pl.BlockSpec((8, 512), lambda j, g: (0, g)),
        ],
        out_specs=pl.BlockSpec((T, 512), lambda j, g: (j, g)),
        out_shape=jax.ShapeDtypeStruct((rows, W), f32),
        compiler_params=params(),
        cost_estimate=cost(
            blocks * HH * 2 * T * T * 256, rows * (2 * W + 1024) * 4, blocks * HH * T * T
        ),
    )(s, ld, ldt, dt, x, skip_row)


def gate_kernel(yin, bc, e, ld, z, y, sums):
    grow = jnp.exp(ld[...])
    cst = bc[:, N:].astype(bf16)
    squares = jnp.zeros((T, 256), f32)
    for i in range(W // 256):
        lanes = slice(256 * i, 256 * i + 256)
        out = yin[:, lanes] + spread(grow, 4 * i, 4) * nn(cst, e[0, :, lanes])
        y[:, lanes] = out
        zt = z[:, lanes]
        g = out * (zt * lax.logistic(zt))
        squares = squares + g * g
    sums[...] = jnp.broadcast_to(jnp.sum(squares, axis=1, keepdims=True), (T, 128))


def gate_part(yin, bc, e, ld, z):
    rows = yin.shape[0]
    blocks = rows // T
    row = lambda c: pl.BlockSpec((T, c), lambda j: (j, 0))
    return pl.pallas_call(
        gate_kernel,
        name="gate_part",
        grid=(blocks,),
        in_specs=[
            row(W),
            row(2 * N),
            pl.BlockSpec((1, N, W), lambda j: (j, 0, 0)),
            row(128),
            row(W),
        ],
        out_specs=[row(W), row(128)],
        out_shape=[
            jax.ShapeDtypeStruct((rows, W), f32),
            jax.ShapeDtypeStruct((rows, 128), f32),
        ],
        input_output_aliases={0: 0},
        compiler_params=params(),
        cost_estimate=cost(2 * rows * N * W, rows * W * 4 * 3, rows * W * 2),
    )(yin, bc, e, ld, z)


def out_back_kernel(cot, w, exact, gfin, dots):
    g = nt(cot[...], w[...])
    gfin[...] = g
    dots[...] = jnp.broadcast_to(jnp.sum(g * exact[...], axis=1, keepdims=True), dots.shape)


def out_back(cot, w, exact):
    rows = cot.shape[0]
    row = lambda c: pl.BlockSpec((T, c), lambda j: (j, 0))
    return pl.pallas_call(
        out_back_kernel,
        name="out_back",
        grid=(rows // T,),
        in_specs=[row(D), pl.BlockSpec((W, D), lambda j: (0, 0)), row(W)],
        out_specs=[row(W), row(128)],
        out_shape=[jax.ShapeDtypeStruct((rows, W), f32), jax.ShapeDtypeStruct((rows, 128), f32)],
        compiler_params=params(),
        cost_estimate=cost(2 * rows * D * W, rows * W * 10 + 2 * D * W),
    )(cot, w, exact)


def gate_back_kernel(
    y, z, gfin, x, sums, dots, bc, e, ld, gain, skip, dec, dz, dy, dc, de1, given, dl, ggain, gskip, dye, keep
):
    j = pl.program_id(0)

    @pl.when(j == 0)
    def _():
        ggain[...] = jnp.zeros_like(ggain)
        gskip[...] = jnp.zeros_like(gskip)

    r = lax.rsqrt(sums[:, 0:1] * (1.0 / DI) + EPS)
    coef = r * r * dots[:, 0:1] * (1.0 / DI)
    grow = jnp.exp(ld[...])
    dlog = jnp.zeros((T, 128), f32)
    dcs = jnp.zeros((T, N), f32)
    for i in range(W // 256):
        lanes = slice(256 * i, 256 * i + 256)
        zt, yt, gf = z[:, lanes], y[:, lanes], gfin[:, lanes]
        sg = lax.logistic(zt)
        silu = zt * sg
        g = yt * silu
        gr = g * r
        ggain[0:1, lanes] += row_sum(gf * gr)
        dg = r * (gf * gain[0:1, lanes]) - g * coef
        dyt = dg * silu
        dz[:, lanes] = (dg * yt * (sg * (1.0 + zt * (1.0 - sg)))).astype(bf16)
        dy[:, lanes] = dyt.astype(bf16)
        xt = x[:, lanes]
        gskip[0:1, lanes] += row_sum(dyt * xt)
        dlog = dlog + per_head(dyt * (yt - skip[0:1, lanes] * xt), 4 * i)
        high, low = halves(dyt * spread(grow, 4 * i, 4))
        dye[:, lanes] = high
        dcs = dcs + (nt(high, e[0, :, lanes]) + nt(low, e[0, :, lanes]))
    dl[...] = dlog
    dc[...] = dcs
    de = tn(bc[:, N:].astype(bf16), dye[...])

    @pl.when(j % 2 == 0)
    def _():
        de1[0] = de
        keep[...] = de

    @pl.when(j % 2 == 1)
    def _():
        given[0] = (de + dec[0, 0:1] * keep[...]).astype(bf16)


def gate_back(y, z, gfin, x, sums, dots, bc, e, ld, gain, skip_row, dec, micros):
    rows = y.shape[0]
    blocks = rows // T
    blk = lambda p: (1 - p % 2) * micros + p // 2
    row = lambda c: pl.BlockSpec((T, c), lambda p: (blk(p), 0))
    fixed = pl.BlockSpec((8, W), lambda p: (0, 0))
    state = pl.BlockSpec((1, N, W), lambda p: (blk(p), 0, 0))
    chip = pl.BlockSpec((1, N, W), lambda p: (p // 2, 0, 0))
    sh = jax.ShapeDtypeStruct
    return pl.pallas_call(
        gate_back_kernel,
        name="gate_back",
        grid=(blocks,),
        in_specs=[
            row(W), row(W), row(W), row(W), row(128), row(128), row(2 * N), state, row(128),
            fixed, fixed, pl.BlockSpec((1, 8, W), lambda p: (blk(p), 0, 0)),
        ],
        out_specs=[row(W), row(W), row(N), chip, chip, row(128), fixed, fixed],
        out_shape=[
            sh((rows, W), bf16),
            sh((rows, W), bf16),
            sh((rows, N), f32),
            sh((micros, N, W), f32),
            sh((micros, N, W), bf16),
            sh((rows, 128), f32),
            sh((8, W), f32),
            sh((8, W), f32),
        ],
        scratch_shapes=[pltpu.VMEM((T, W), bf16), pltpu.VMEM((N, W), f32)],
        compiler_params=params(),
        cost_estimate=cost(8 * rows * N * W, rows * W * 24, rows * W * 2),
    )(y, z, gfin, x, sums, dots, bc, e, ld, gain, skip_row, dec)


def inner_back_kernel(s, bc, ld, ldt, dt, x, dy, skip, dx, xv, dbc, st, dst):
    g = pl.program_id(1)

    @pl.when(g == 0)
    def _():
        st[...] = s[...].T
        dst[...] = jnp.zeros_like(dst)
        xv[...] = jnp.zeros_like(xv)

    shift = lax.rem(128 - 8 * g, 128)
    logd = pltpu.roll(ld[...], shift, 1) * LOG2E
    step = pltpu.roll(dt[...], shift, 1)
    early = iota((HT, T), 1) >= iota((HT, T), 0)
    late = iota((HT, HT), 1) >= iota((HT, HT), 0)
    head = iota((T, 256), 1) // PS
    gtop = jnp.zeros((HT, T), f32)
    gbottom = jnp.zeros((HT, HT), f32)
    sums = jnp.zeros((T, 128), f32)
    for q in range(2):
        lanes = slice(256 * q, 256 * q + 256)
        steps = spread(step, 4 * q, 4)
        tile = x[:, lanes]
        xdt = tile * steps
        dyt = dy[:, lanes]
        top = jnp.zeros((HT, 256), f32)
        bottom = jnp.zeros((HT, 256), f32)
        for i in range(4):
            h = 4 * q + i
            row = ldt[0, pl.ds(8 * g + h, 1), :] * LOG2E
            col = logd[:, h : h + 1]
            dmine = jnp.where(head == i, dyt, jnp.zeros_like(dyt))
            xmine = jnp.where(head == i, xdt, 0.0).astype(bf16)
            decay = jnp.exp2(jnp.where(early, row - col[:HT], NEG))
            top = top + nn((decay * st[:HT, :]).astype(bf16), dmine)
            gtop = gtop + nt(xmine[:HT], dyt) * decay
            decay = jnp.exp2(jnp.where(late, row[:, HT:] - col[HT:], NEG))
            bottom = bottom + nn((decay * st[HT:, HT:]).astype(bf16), dmine[HT:])
            gbottom = gbottom + nt(xmine[HT:], dyt[HT:]) * decay
        total = jnp.concatenate([top, bottom], axis=0)
        dx[:, lanes] = total * steps + skip[0:1, lanes] * dyt.astype(f32)
        sums = sums + per_head(tile * total, 8 * g + 4 * q)
    xv[...] += sums
    dst[:HT, :] += gtop
    dst[HT:, HT:] += gbottom

    @pl.when(g == pl.num_programs(1) - 1)
    def _():
        dbc[:, :N] = fine(nn, dst[...], bc[:, N:])
        dbc[:, N:] = fine(tn, dst[...], bc[:, :N])


def inner_back(s, bc, ld, ldt, dt, x, dy, skip_row):
    rows = x.shape[0]
    blocks, groups = rows // T, W // 512
    row = lambda c: pl.BlockSpec((T, c), lambda j, g: (j, 0))
    tile = pl.BlockSpec((T, 512), lambda j, g: (j, g))
    sh = jax.ShapeDtypeStruct
    return pl.pallas_call(
        inner_back_kernel,
        name="inner_back",
        grid=(blocks, groups),
        in_specs=[
            row(T),
            row(2 * N),
            row(128),
            pl.BlockSpec((1, 32, T), lambda j, g: (j, 0, 0)),
            row(128),
            tile,
            tile,
            pl.BlockSpec((8, 512), lambda j, g: (0, g)),
        ],
        out_specs=[tile, row(128), row(2 * N)],
        out_shape=[sh((rows, W), f32), sh((rows, 128), f32), sh((rows, 2 * N), f32)],
        scratch_shapes=[pltpu.VMEM((T, T), f32), pltpu.VMEM((T, T), f32)],
        compiler_params=params(),
        cost_estimate=cost(
            2 * blocks * HH * 2 * T * T * 256, rows * (2 * W + 1024) * 4, blocks * HH * T * T
        ),
    )(s, bc, ld, ldt, dt, x, dy, skip_row)


def conv_back_kernel(
    micros, xbc, prev, x, dxi, xv, dbc, bc, dt, ld, later1, de1, dec, e, dc, dla, cw, hp,
    gp, gcw, ghp, pad, dpre, nxt, edge,
):
    p = pl.program_id(0)
    b = 1 - p % 2

    @pl.when(p == 0)
    def _():
        gcw[...] = jnp.zeros_like(gcw)
        ghp[...] = jnp.zeros_like(ghp)

    @pl.when(p == 2 * micros)
    def _():
        gp[0 : 8 * micros] = edge[...].astype(bf16)

    @pl.when(p < 2 * micros)
    def _():
        pad[0:8] = prev[:, :XC]
        pad[8 : 8 + T] = xbc[:, :XC]
        dpre[0:8] = jnp.zeros((8, XC), f32)
        dpre[8 + T : 16 + T] = jnp.where(b == 1, 0.0, nxt[...])
        step, logd = dt[...], ld[...]
        fade = jnp.exp(logd[T - 1 : T] - logd)
        tailw = fade * step
        bst = bc[:, :N].astype(bf16)

        def through_conv(grad, lanes):
            a = conv_taps(pad, cw, lanes)
            sg = lax.logistic(a)
            d = grad * (sg * (1.0 + a * (1.0 - sg)))
            dpre[8 : 8 + T, lanes] = d
            gcw[4:5, lanes] += row_sum(d)
            for k in range(KC):
                gcw[k : k + 1, lanes] += row_sum(d * pad[pl.ds(5 + k, T), lanes])
            total = cw[0:1, lanes] * dpre[pl.ds(11, T), lanes]
            rim = cw[0:1, lanes] * dpre[pl.ds(3, 8), lanes]
            for k in range(1, KC):
                total = total + cw[k : k + 1, lanes] * dpre[pl.ds(11 - k, T), lanes]
                rim = rim + cw[k : k + 1, lanes] * dpre[pl.ds(3 - k, 8), lanes]
            gp[:, lanes] = total.astype(bf16)
            nxt[:, lanes] = d[0:8]

            @pl.when(b == 0)
            def _():
                edge[pl.ds(pl.multiple_of(8 * (p // 2), 8), 8), lanes] = rim

        dw = jnp.zeros((T, 128), f32)
        dbs = jnp.zeros((T, N), f32)
        ddec = jnp.zeros((8, 128), f32)
        for i in range(W // 256):
            lanes = slice(256 * i, 256 * i + 256)
            lat = later1[0, :, lanes]
            earlier = de1[0, :, lanes] + dec[0, 0:1, lanes] * lat.astype(f32)
            lat = jnp.where(b == 1, lat, earlier.astype(bf16))
            spreadw = spread(tailw, 4 * i, 4)
            xt = x[:, lanes]
            bl = nn(bst, lat)
            dw = dw + per_head(xt * bl, 4 * i)
            high, low = halves(xt * spreadw)
            dbs = dbs + (nt(high, lat) + nt(low, lat))
            both = row_sum(lat.astype(f32) * e[0, :, lanes].astype(f32))
            ddec = ddec + per_head(jnp.broadcast_to(both, (8, 256)), 4 * i)
            through_conv(dxi[:, lanes] + bl * spreadw, lanes)
        through_conv(
            jnp.concatenate([dbc[:, :N] + dbs, dbc[:, N:] + dc[...]], axis=1), slice(W, XC)
        )
        q = dw * tailw
        dlog = dla[...] - step * xv[...] - q
        dlast = row_sum(q) + ddec[0:1] * jnp.exp(logd[T - 1 : T])
        dlog = dlog + jnp.where(iota((T, 128), 0) == T - 1, dlast, 0.0)
        tri = (iota((T, T), 1) >= iota((T, T), 0)).astype(f32)
        dcum = jnp.dot(tri, dlog, precision=HIGH, preferred_element_type=f32)
        dstep = xv[...] + dw * fade - hp[1:2, :] * dcum
        draw = dstep * lax.logistic(xbc[:, XC:XP] + hp[0:1, :])
        draw = jnp.where(iota((T, 128), 1) < HH, draw, 0.0)
        ghp[0:1] += row_sum(draw)
        ghp[1:2] -= row_sum(dcum * step)
        gp[:, XC:XP] = draw.astype(bf16)

        @pl.when(b == 0)
        def _():
            edge[pl.ds(pl.multiple_of(8 * (p // 2), 8), 8), XC:XP] = jnp.zeros((8, 128), f32)


def conv_back(xbc, x, dxi, xv, dbc, bc, dt, ld, later1, de1, dec, e, dc, dla, cw, hp, micros):
    blocks = 2 * micros
    rows = blocks * T
    blk = lambda p: jnp.where(p < blocks, (1 - p % 2) * micros + p // 2, micros - 1)
    row = lambda c: pl.BlockSpec((T, c), lambda p: (blk(p), 0))
    whole = lambda a: pl.BlockSpec(a.shape, lambda p: (0, 0))
    state = pl.BlockSpec((1, N, W), lambda p: (blk(p), 0, 0))

    unit = lambda p: jnp.minimum(p // 2, micros - 1)
    chip = pl.BlockSpec((1, N, W), lambda p: (unit(p), 0, 0))

    def before(p):
        k = blk(p)
        return (jnp.where(k >= micros, (k - micros + 1) * (T // 8) - 1, rows // 8 + k), 0)

    return pl.pallas_call(
        functools.partial(conv_back_kernel, micros),
        name="conv_back",
        grid=(blocks + 1,),
        in_specs=[
            row(XP),
            pl.BlockSpec((8, XP), before),
            row(W), row(W), row(128), row(2 * N), row(2 * N), row(128), row(128),
            chip, chip, pl.BlockSpec((1, 8, W), lambda p: (micros + unit(p), 0, 0)), state,
            row(N), row(128), whole(cw), whole(hp),
        ],
        out_specs=[
            pl.BlockSpec((T, XP), lambda p: (jnp.where(p < blocks, blk(p), blocks), 0)),
            pl.BlockSpec((8, XC), lambda p: (0, 0)),
            pl.BlockSpec((8, 128), lambda p: (0, 0)),
        ],
        out_shape=[
            jax.ShapeDtypeStruct((rows + 8 * micros, XP), bf16),
            jax.ShapeDtypeStruct((8, XC), f32),
            jax.ShapeDtypeStruct((8, 128), f32),
        ],
        scratch_shapes=[
            pltpu.VMEM((T + 8, XC), f32),
            pltpu.VMEM((T + 16, XC), f32),
            pltpu.VMEM((8, XC), f32),
            pltpu.VMEM((8 * micros, XP), f32),
        ],
        compiler_params=pltpu.CompilerParams(vmem_limit_bytes=58 * MB_),
        cost_estimate=cost(6 * rows * N * W, rows * W * 18, rows * XC * 2),
    )(xbc, xbc, x, dxi, xv, dbc, bc, dt, ld, later1, de1, dec, e, dc, dla, cw, hp)


AXIS = {"z": Z, "l": "zl", "s": "s"}
RING = 4
CHIPS = 16


def hop(value, axis):
    n = RING if axis == "z" else 2
    return lax.ppermute(value, AXIS[axis], [(i, (i + 1) % n) for i in range(n)])


def fence(groups, *values):
    held = [{k: g.live[k] for k in g.live} for g in groups]
    held, values = lax.optimization_barrier((held, values))
    for g, h in zip(groups, held):
        g.live.update(h)
    return values


def after(groups, *values):
    values, _ = lax.optimization_barrier((values, [v for g in groups for v in g.sent]))
    for g in groups:
        g.sent = ()
    return values


def partly(group, names, *values):
    held = {k: group.live[k] for k in group.live if k[:-1] in names}
    held, values = lax.optimization_barrier((held, values))
    group.live.update(held)
    return values


class Moves:
    sent = ()

    def send(self, value, axis):
        self.sent = [*self.sent, value]
        return hop(value, axis)


WAYS = (("s", "l"), ("l", "s"))


def lanes_of(widths):
    return [slice(sum(widths[:c]), sum(widths[: c + 1])) for c in range(len(widths))]


def near(c, kl, ks):
    return (ks, kl) if c == 0 else (kl, ks)


class Gather(Moves):
    def __init__(self, own, widths, turns):
        self.widths, self.turns = widths, turns
        self.live = {"g0": own}
        self.n = 1
        self.parts = []

    def z(self):
        self.live[f"g{self.n}"] = self.send(self.live[f"g{self.n - 1}"], "z")
        self.n += 1

    def first(self, h):
        some = jnp.stack([self.live[f"g{k}"] for k in self.turns[h]], 0)
        for k in self.turns[h]:
            if k < self.n - 1 or self.n == RING:
                self.live.pop(f"g{k}")
        for c, lanes in enumerate(lanes_of(self.widths)):
            self.live[f"p{h}{c}"] = some[:, :, lanes]
            self.live[f"q{h}{c}"] = self.send(some[:, :, lanes], WAYS[c][0])

    def second(self, h):
        for c in range(2):
            more = jnp.concatenate([self.live.pop(f"p{h}{c}"), self.live.pop(f"q{h}{c}")], 0)
            self.parts += [more, self.send(more, WAYS[c][1])]

    def place(self, c, kz, kl, ks):
        ka, kb = near(c, kl, ks)
        h = [kz in t for t in self.turns].index(True)
        turn = self.turns[h]
        return (h * 2 + c) * 2 + kb, ka * len(turn) + turn.index(kz)


class RingLast(Moves):
    def __init__(self, own, widths):
        self.widths = widths
        self.live = {f"p{c}": own[None, :, lanes] for c, lanes in enumerate(lanes_of(widths))}
        self.parts = []

    def step(self, n):
        for c in range(2):
            p = self.live[f"p{c}"]
            self.live[f"p{c}"] = jnp.concatenate([p, self.send(p, WAYS[c][n])], 0)

    def z(self):
        if not self.parts:
            self.live["p"] = jnp.concatenate([self.live.pop("p0"), self.live.pop("p1")], 0)
            self.parts = [self.live["p"]]
        self.live["p"] = self.send(self.live["p"], "z")
        self.parts.append(self.live["p"])

    def place(self, c, kz, kl, ks):
        ka, kb = near(c, kl, ks)
        return kz, c * 4 + kb * 2 + ka


class Scatter(Moves):
    def __init__(self, widths, turns):
        self.widths, self.turns = widths, turns
        self.live = {}
        self.order = [k for t in turns for k in t]

    def load(self, parts):
        parts = iter(parts)
        for h in range(len(self.turns)):
            for c in range(2):
                self.live[f"k{h}{c}"] = next(parts)
                self.live[f"s{h}{c}"] = next(parts)

    def second(self, h):
        for c in range(2):
            self.live[f"r{h}{c}"] = self.send(self.live.pop(f"s{h}{c}"), WAYS[c][1])

    def first(self, h):
        n = len(self.turns[h])
        for c in range(2):
            got, kept = self.live.pop(f"r{h}{c}"), self.live.pop(f"k{h}{c}")
            self.live[f"m{h}{c}"] = got[:n].astype(f32) + kept[:n].astype(f32)
            give = (got[n:].astype(f32) + kept[n:].astype(f32)).astype(bf16)
            self.live[f"n{h}{c}"] = self.send(give, WAYS[c][0])

    def ring(self, k):
        h = [self.order[k] in t for t in self.turns].index(True)
        at = self.turns[h].index(self.order[k])
        if at == 0:
            self.live["w"] = jnp.concatenate(
                [self.live.pop(f"m{h}{c}") + self.live.pop(f"n{h}{c}").astype(f32) for c in range(2)], 2
            )
        total = self.live["w"][at]
        if k:
            total = total + self.live.pop("t").astype(f32)
        if k == RING - 1:
            self.live.pop("w")
            return total
        self.live["t"] = self.send(total.astype(bf16), "z")

    def place(self, c, kz, kl, ks):
        ka, kb = near(c, kl, ks)
        h = [kz in t for t in self.turns].index(True)
        turn = self.turns[h]
        return (h * 2 + c) * 2 + kb, ka * len(turn) + turn.index(kz)

    def shapes(self, r):
        return [
            jax.ShapeDtypeStruct((2 * len(t), r, w), bf16)
            for t in self.turns
            for w in self.widths
            for _ in range(2)
        ]


def move_kernel(table, r, out_of, where, *refs):
    sems = refs[-1]
    refs = refs[:-1]
    whole = refs[-1] if out_of else refs[0]
    arrays = refs[:-1] if out_of else refs[1:]
    copies = []
    for n, (array, entry, k, lanes) in enumerate(table):
        row = pl.multiple_of(where[k] * r, 16)
        place = whole.at[pl.ds(row, r), lanes]
        piece = arrays[array].at[entry]
        pair = (piece, place) if out_of else (place, piece)
        copies.append(pltpu.make_async_copy(*pair, sems.at[n]))
    for c in copies:
        c.start()
    for c in copies:
        c.wait()


def move(group, where, r, given, shapes, out_of):
    table = []
    for c, lanes in enumerate(lanes_of(group.widths)):
        for k in range(CHIPS):
            table.append((*group.place(c, k // 4, k // 2 % 2, k % 2), k, lanes))
    any_ = pl.BlockSpec(memory_space=pl.ANY)
    return pl.pallas_call(
        functools.partial(move_kernel, tuple(table), r, out_of),
        name="join" if out_of else "deal",
        in_specs=[pl.BlockSpec(memory_space=pltpu.SMEM)] + [any_] * len(given),
        out_specs=[any_] * len(shapes),
        out_shape=shapes,
        scratch_shapes=[pltpu.SemaphoreType.DMA((len(table),))],
        compiler_params=pltpu.CompilerParams(vmem_limit_bytes=MB_),
        cost_estimate=cost(0, 4 * CHIPS * r * sum(group.widths)),
    )(where, *given)


def join(group, where, r):
    shape = jax.ShapeDtypeStruct((CHIPS * r, sum(group.widths)), bf16)
    return move(group, where, r, group.parts, [shape], True)[0]


def deal(group, where, r, whole):
    group.load(move(group, where, r, [whole], group.shapes(r), False))


def swap(value, axis="c"):
    return lax.ppermute(value, axis, [(0, 1), (1, 0)])


def two(mine, other, at):
    return jnp.where(at == 0, jnp.stack([mine, other]), jnp.stack([other, mine]))


class Plain:
    def __init__(self, axes):
        self.axes = axes

    def gather(self, piece):
        return lax.all_gather(piece, self.axes, axis=0, tiled=True)

    def reduce(self, grad):
        return lax.psum_scatter(grad, self.axes, scatter_dimension=0, tiled=True).astype(f32)


def body(
    hidden, in_weight, out_weight, conv_weight, conv_bias, norm_gain, gate_gain,
    step_bias, decay_rate, skip_gain, cotangent,
):
    nz, nl, ns = lax.axis_size(Z), lax.axis_size("zl"), lax.axis_size("s")
    core = lax.axis_index("c")
    micros = hidden.shape[0]
    rows = micros * 2 * T
    r_in, r_out = in_weight.shape[0], out_weight.shape[0]
    r = 2 * r_in
    fast = (nz, nl, ns) == (RING, 2, 2) and r % 16 == 0 and r_out == r
    onward = [(i, i + 1) for i in range(ns - 1)]
    backward = [(i + 1, i) for i in range(ns - 1)]
    turn = [(a * 2 + b, b * 2 + a) for a in range(2) for b in range(2)]

    def cut(k):
        part = lambda at, width: lax.dynamic_slice_in_dim(in_weight, at + k * width, width, 1)
        steps = in_weight[:, DI + CONV :]
        steps = jnp.where(k == 0, steps[:, :HH], steps[:, HH:])
        return jnp.concatenate(
            [
                part(DI, W),
                in_weight[:, 2 * DI : 2 * DI + 2 * N],
                jnp.pad(steps, ((0, 0), (0, 128 - HH))),
                part(0, W),
            ],
            axis=1,
        )

    ours, theirs = cut(core), cut(1 - core)
    theirs, out_weight, hidden, cotangent = lax.optimization_barrier(
        (theirs, out_weight, hidden, cotangent)
    )
    chip_rows = two(ours, swap(theirs), core).reshape(r, -1)
    w_own = lax.ppermute(out_weight, ("za", "c"), turn)

    ins = Plain(ALL[:4])
    outs = Plain(("zb", "zl", "s", "za"))

    n_c = conv_bias.shape[0]
    packed = jnp.concatenate([conv_weight.T.reshape(-1), conv_bias, norm_gain, gate_gain])

    def spread_out(small, a, at):
        mine, other = (jnp.expand_dims(v, at) for v in (small, swap(small, a)))
        here = lax.axis_index(a) == 0
        return jnp.where(here, jnp.concatenate([mine, other], at), jnp.concatenate([other, mine], at))

    hid_own = hidden.reshape(micros, T, D)
    cot_own = cotangent.reshape(micros, T, D)
    hid_other, cot_other = swap(hid_own), swap(cot_own)

    def chip_tokens(mine, other):
        return two(mine, other, core).reshape(rows, D)

    def rim_of(tokens):
        return lax.ppermute(tokens.reshape(2, micros, T, D)[1, :, T - 8 :], "s", onward)

    if fast:
        back = jnp.arange(CHIPS)
        kz = (lax.axis_index(Z) - back // 4) % RING
        kl = (lax.axis_index("zl") - back // 2) % 2
        ks = (lax.axis_index("s") - back) % 2
        in_place = ((kz * 2 + kl) * 2 + ks).astype(jnp.int32)
        out_place = ((((kz % 2) * 2 + kl) * 2 + ks) * 2 + kz // 2).astype(jnp.int32)
        x_cols, z_cols, o_cols = (896, 1024), (768, 768), (768, 768)
        small = spread_out(packed, "za", 0)
        small = spread_out(small, "zb", 1)
        chip_rows, small = lax.optimization_barrier((chip_rows, small))
        halves_, ring_ = ((0, 1), (2, 3)), ((0, 1, 2, 3),)
        gx_ = Gather(chip_rows[:, :XP], x_cols, halves_)
        gz_ = Gather(chip_rows[:, XP:], z_cols, ring_)
        go_ = RingLast(w_own, o_cols)
        every = [gx_, gz_, go_]
        small = spread_out(small, "zl", 2)
        gx_.z()
        go_.step(0)
        small, hid_other, cot_other = fence(every, small, hid_other, cot_other)
        small = spread_out(small, "s", 3)
        gx_.z()
        gx_.first(0)
        go_.step(1)
        hid_own_, hid_other = after(every, hid_own, hid_other)
        hid_all = chip_tokens(hid_own_, hid_other)
        rim = rim_of(hid_all)
        small = spread_out(small, "c", 4).reshape(-1, packed.shape[0])
        small, rim, hid_all = fence(every, small, rim, hid_all)
        gx_.z()
        gx_.second(0)
        gz_.z()
        small, rim, hid_all, cot_own_, cot_other = after(
            every, small, rim, hid_all, cot_own, cot_other
        )
        cot_all = chip_tokens(cot_own_, cot_other)
    else:
        small = lax.all_gather(packed, ALL)
        hid_all, cot_all = chip_tokens(hid_own, hid_other), chip_tokens(cot_own, cot_other)
        rim = rim_of(hid_all)
        w_x, w_z = ins.gather(chip_rows[:, :XP]), ins.gather(chip_rows[:, XP:])

    rim = jnp.where(iota(rim.shape, 1) >= 5, rim, jnp.zeros_like(rim)).reshape(8 * micros, D)
    devices = small.shape[0]
    taps = small[:, : KC * n_c].reshape(devices, KC, n_c).transpose(1, 0, 2).reshape(KC, CONV)
    bias = small[:, KC * n_c : (KC + 1) * n_c].reshape(1, CONV)
    norm_vec = small[:, (KC + 1) * n_c : (KC + 1) * n_c + r_in].reshape(D).astype(f32)
    gate_vec = small[:, (KC + 1) * n_c + r_in :].reshape(1, DI)
    conv_all = jnp.concatenate([taps, bias, jnp.zeros((3, CONV), bf16)], 0).astype(f32)
    cw = jnp.concatenate(
        [lax.dynamic_slice_in_dim(conv_all, core * W, W, 1), conv_all[:, DI:]], axis=1
    )
    gain = jnp.broadcast_to(lax.dynamic_slice_in_dim(gate_vec, core * W, W, 1).astype(f32), (8, W))
    heads = jnp.stack([step_bias, decay_rate, skip_gain])
    heads = lax.dynamic_slice_in_dim(heads, core * HH, HH, 1)
    hp = jnp.pad(heads, ((0, 5), (0, 128 - HH)))
    skip_row = jnp.broadcast_to(jnp.repeat(heads[2], PS)[None], (8, W))
    normed = pre_norm(hid_all, rim, norm_vec[None])
    if fast:
        normed, cot_all, cw, hp, gain, skip_row = fence(
            every, normed, cot_all, cw, hp, gain, skip_row
        )
        gx_.first(1)
        gz_.z()
        (normed,) = fence([gx_, gz_], normed)
        gx_.second(1)
        gz_.z()
        (normed,) = after([gx_, gz_], normed)

    if fast:
        (normed,) = fence(every, normed)
        gz_.first(0)
        go_.z()
        (normed,) = after([gz_, go_], normed)
        w_x = join(gx_, in_place, r)
    xbc = nn(normed, w_x)
    if fast:
        (xbc,) = fence([gz_], xbc)
        gz_.second(0)
        (xbc,) = after([gz_], xbc)
        go_.live, xbc = lax.optimization_barrier((go_.live, xbc))
        go_.z()
        (xbc,) = after([go_], xbc)
    else:
        w_o = outs.gather(w_own)
    x, bc, s, dt, ld, ldt, st0, comb, dec8 = block_states(xbc, cw, hp, micros)
    dec = dec8[:, 0].reshape(2, micros, 1, W)
    if fast:
        comb, s = lax.optimization_barrier((comb, s))
    if ns == 2:
        first = lax.ppermute(comb, "s", onward)
    else:
        first = jnp.zeros_like(comb)
        chip_decay = dec[0] * dec[1]
        for _ in range(ns - 1):
            out = (chip_decay * first.astype(f32) + comb.astype(f32)).astype(bf16)
            first = lax.ppermute(out, "s", onward)
    yin = inner_part(s, ld, ldt, dt, x, skip_row)
    if fast:
        (yin,) = fence([gz_, go_], yin)
        go_.z()
        (yin,) = after([go_], yin)
    second = (dec[0] * first.astype(f32) + st0).astype(bf16)
    entering = jnp.stack([first, second], 0).reshape(2 * micros, N, W)
    if fast:
        w_z = join(gz_, in_place, r)
    z = nn(normed[:rows], w_z)
    y, sums = gate_part(yin, bc, entering, ld, z)
    sums = sums + swap(sums)
    root = lax.rsqrt(sums[:, :1] * (1.0 / DI) + EPS)
    exact = y * (z * lax.logistic(z)) * root * gain[:1]
    fin = exact.astype(bf16)
    g_out = tn(fin, cot_all).astype(bf16)
    if fast:
        ring_back = ((1, 2, 3, 0),)
        so_ = Scatter(o_cols, ring_back)
        deal(so_, out_place, r, g_out)
        (cot_all,) = fence([so_], cot_all)
        so_.second(0)
        (cot_all,) = after([so_], cot_all)
        w_o = join(go_, out_place, r)

    gfin, dots = out_back(cot_all, w_o, exact)

    partial_out = nn(fin, w_o).reshape(2, micros, T, D)
    give = lax.dynamic_index_in_dim(partial_out, 1 - core, 0, False).astype(bf16)
    keep = lax.dynamic_index_in_dim(partial_out, core, 0, False)
    given_out = swap(give)
    block_out = (hid_own.astype(f32) + keep + given_out.astype(f32)).astype(bf16)
    if fast:
        dots, gfin, give = fence([so_], dots, gfin, give)
        so_.first(0)
        (y,) = after([so_], y)
    dots = dots + swap(dots)
    dz, dy, dc, de1, given, dla, ggain, gskip = gate_back(
        y, z, gfin, x, sums, dots, bc, entering, ld, gain, skip_row, dec8, micros
    )
    if ns == 2:
        dz, given = lax.optimization_barrier((dz, given))
        later1 = lax.ppermute(given, "s", backward)
    else:
        later1 = jnp.zeros((micros, N, W), bf16)
        for _ in range(ns - 1):
            out = given.astype(f32) + dec[0] * dec[1] * later1.astype(f32)
            later1 = lax.ppermute(out.astype(bf16), "s", backward)
    gz = tn(normed[:rows], dz).astype(bf16)
    if fast:
        sz_ = Scatter(z_cols, ring_back)
        deal(sz_, in_place, r, gz)
        (dy,) = fence([so_, sz_], dy)
        so_.ring(0)
        sz_.second(0)
        (dy,) = after([so_, sz_], dy)

    dxi, xv, dbc = inner_back(s, bc, ld, ldt, dt, x, dy, skip_row)
    if fast:
        dxi, later1 = fence([so_, sz_], dxi, later1)
        so_.ring(1)
        sz_.first(0)
        (dxi,) = after([so_, sz_], dxi)
    gp, gcw, ghp = conv_back(
        xbc, x, dxi, xv, dbc, bc, dt, ld, later1, de1, dec8, entering, dc, dla, cw, hp, micros
    )
    if fast:
        (gp,) = fence([so_, sz_], gp)
        so_.ring(2)
        sz_.ring(0)
        (gp,) = after([so_, sz_], gp)
    gx = tn(normed, gp).astype(bf16)

    wide = lambda v: jnp.pad(v, ((0, 0), (0, XC - v.shape[1])))
    tiny = jnp.concatenate(
        [gcw[:5], wide(ggain[:1]), wide(gskip[:1]), wide(ghp[:2].reshape(1, 256))], axis=0
    )
    if fast:
        sx_ = Scatter(x_cols, ((1, 2), (3, 0)))
        deal(sx_, in_place, r, gx)
        gp, tiny = fence([so_, sz_, sx_], gp, tiny)
        sx_.second(0)
        sz_.ring(1)
        gp, tiny = after([sx_, sz_], gp, tiny)
        tiny = tiny + swap(tiny, "zb")
        g_out = so_.ring(3)
    else:
        g_out = outs.reduce(g_out)
    g_out = lax.ppermute(g_out, ("za", "c"), turn)

    gn = nt(gp, w_x)
    edge = lax.ppermute(gn[rows:].astype(bf16), "s", backward).reshape(1, micros, 8, D)
    if fast:
        gn, dz, tiny = fence([sz_], gn, dz, tiny)
        tiny = tiny + swap(tiny, "za")
    gn = gn[:rows] + nt(dz, w_z)

    if fast:
        gn, g_out, tiny = fence([sz_, sx_], gn, g_out, tiny)
        sx_.first(0)
        sx_.second(1)
        sz_.ring(2)
        (gn,) = after([sx_, sz_], gn)
    gn = gn.reshape(2, micros, T, D)
    edge = jnp.where(iota(edge.shape, 2) >= 5, edge.astype(f32), 0.0)
    gn = gn + jnp.pad(edge, ((1, 0), (0, 0), (T - 8, 0), (0, 0)))
    give = lax.dynamic_index_in_dim(gn, 1 - core, 0, False).astype(bf16)
    keep = lax.dynamic_index_in_dim(gn, core, 0, False)
    other = swap(give)
    if fast:
        keep, other = partly(sx_, ("m0", "n0"), keep, other)
        sx_.ring(0)
        keep, other = after([sx_], keep, other)
    gn = keep + other.astype(f32)
    hid_f = hid_own.astype(f32)
    own_scale = lax.rsqrt(jnp.mean(hid_f * hid_f, axis=-1, keepdims=True) + EPS)
    unit = hid_f * own_scale
    gq = gn * norm_vec
    g_hid = cot_own.astype(f32) + own_scale * (
        gq - unit * jnp.mean(gq * unit, axis=-1, keepdims=True)
    )

    if fast:
        tiny, g_hid, block_out = fence([sz_, sx_], tiny, g_hid, block_out)
        sx_.first(1)
        sx_.ring(1)
        (tiny,) = after([sx_], tiny)
        tiny = tiny + swap(tiny, "s")
        gz = sz_.ring(3)

    def exchanged(g):
        g = g.reshape(2, r_in, -1)
        mine = lax.dynamic_index_in_dim(g, core, 0, False)
        return two(mine, swap(lax.dynamic_index_in_dim(g, 1 - core, 0, False)), core)

    if fast:
        tiny, gz = fence([sx_], tiny, gz)
        sx_.ring(2)
        tiny, gz = after([sx_], tiny, gz)
        gz = exchanged(gz)
        tiny = tiny + swap(tiny, "zl")
        tiny, gz = fence([sx_], tiny, gz)
        gx = sx_.ring(3)
    else:
        tiny = lax.psum(tiny, ALL[:4])
        gx, gz = ins.reduce(gx), ins.reduce(gz)
        gz = exchanged(gz)
    gx = exchanged(gx)
    both = two(tiny, swap(tiny), core)
    g_conv = jnp.concatenate([both[0, :5, :W], both[1, :5, :W], both[0, :5, W:] + both[1, :5, W:]], axis=1)
    me = lax.axis_index(ALL)
    g_conv = lax.dynamic_slice_in_dim(g_conv, me * n_c, n_c, 1)
    g_gate = both[:, 5, :W].reshape(-1)
    g_gate = lax.dynamic_slice_in_dim(g_gate, me * r_out, r_out)
    g_skip = both[:, 6, :W].reshape(H, PS).sum(-1)
    g_bias = both[:, 7, :HH].reshape(-1)
    g_rate = both[:, 7, 128 : 128 + HH].reshape(-1)
    g_in = jnp.concatenate(
        [
            gz[0], gz[1],
            gx[0, :, :W], gx[1, :, :W],
            gx[0, :, W:XC] + gx[1, :, W:XC],
            gx[0, :, XC : XC + HH], gx[1, :, XC : XC + HH],
        ],
        axis=1,
    )
    g_norm = jnp.sum(g_in * in_weight.astype(f32), axis=1) / norm_gain.astype(f32)
    return (
        block_out.reshape(hidden.shape),
        g_hid.reshape(hidden.shape),
        g_in,
        g_out,
        g_conv[:KC].T,
        g_conv[KC],
        g_norm,
        g_gate,
        g_bias,
        g_rate,
        g_skip,
    )


def solution(mesh):
    dp, seq = mesh.shape["dp"], mesh.shape["seq"]
    split = Mesh(mesh.devices.reshape(2, dp // 4, 2, seq // 2, 2), ALL)
    token = P(None, ("za", "zb", "zl"), ("s", "c"), None)
    in_specs = (token, P(ALL, None), P(ALL, None), P(ALL, None), P(ALL), P(ALL), P(ALL), P(), P(), P(), token)
    out_specs = (token, token, P(ALL, None), P(ALL, None), P(ALL, None), P(ALL), P(ALL), P(ALL), P(), P(), P())
    return jax.shard_map(body, mesh=split, in_specs=in_specs, out_specs=out_specs, check_vma=False)
```

```python
import functools

import jax
import jax.numpy as jnp
import numpy as np
from jax import lax
from jax.experimental import pallas as pl
from jax.experimental.pallas import tpu as pltpu
from jax.sharding import Mesh
from jax.sharding import PartitionSpec as P

DI = 3072
H = 48
PS = 64
N = 128
KC = 4
CONV = 3328
D = 1536
T = 256
HH = H // 2
W = DI // 2
XC = W + 2 * N
XP = XC + 128
EPS = 1e-05
NEG = -1e30
LOG2E = 1.4426950408889634
HT = T // 2
f32 = jnp.float32
bf16 = jnp.bfloat16
ALL = ("za", "zb", "zl", "s", "c")
Z = ("za", "zb")
MB_ = 1 << 20


def nn(a, b):
    return lax.dot_general(a, b, (((1,), (0,)), ((), ())), preferred_element_type=f32)


def nt(a, b):
    return lax.dot_general(a, b, (((1,), (1,)), ((), ())), preferred_element_type=f32)


def tn(a, b):
    return lax.dot_general(a, b, (((0,), (0,)), ((), ())), preferred_element_type=f32)


def halves(v):
    high = v.astype(bf16)
    return high, (v - high.astype(f32)).astype(bf16)


def fine(dot, a, b):
    (ah, al), (bh, bl) = halves(a), halves(b)
    return dot(ah, bh) + (dot(ah, bl) + dot(al, bh))


def iota(shape, dim):
    return lax.broadcasted_iota(jnp.int32, shape, dim)


def spread(cols, first, heads):
    rows = cols.shape[0]
    head = iota((rows, heads * PS), 1) // PS
    out = jnp.broadcast_to(cols[:, first : first + 1], (rows, heads * PS))
    for i in range(1, heads):
        out = jnp.where(head == i, cols[:, first + i : first + i + 1], out)
    return out


def head_place(lanes, first):
    return (iota((lanes, 128), 0) // PS + first == iota((lanes, 128), 1)).astype(bf16)


def per_head(values, first):
    place = head_place(values.shape[1], first)
    high, low = halves(values)
    return nn(high, place) + nn(low, place)


def masked_sums(mask, values):
    high, low = halves(values)
    ones = mask.astype(bf16)
    return nn(ones, high) + nn(ones, low)


def row_sum(values):
    return jnp.sum(values, axis=0, keepdims=True)


def conv_taps(pad_ref, cw_ref, lanes):
    total = cw_ref[4:5, lanes]
    for k in range(KC):
        total = total + cw_ref[k : k + 1, lanes] * pad_ref[pl.ds(5 + k, T), lanes]
    return total


def softplus(v):
    return jnp.maximum(v, 0.0) + jnp.log1p(jnp.exp(-jnp.abs(v)))


def params(**kw):
    return pltpu.CompilerParams(vmem_limit_bytes=40 * MB_, **kw)


def cost(flops, nbytes, trans=0):
    return pl.CostEstimate(flops=int(flops), bytes_accessed=int(nbytes), transcendentals=int(trans))


def norm_kernel(blocks, hid, rim, gain, out):
    j = pl.program_id(0)

    def scaled(v):
        v = v.astype(f32)
        return (v * lax.rsqrt(jnp.mean(v * v, axis=-1, keepdims=True) + EPS) * gain[0:1]).astype(bf16)

    @pl.when(j < blocks)
    def _():
        out[...] = scaled(hid[...])

    @pl.when(j == blocks)
    def _():
        out[: rim.shape[0]] = scaled(rim[...])


def pre_norm(hid, rim, gain):
    rows, extra = hid.shape[0], rim.shape[0]
    blocks = rows // T
    return pl.pallas_call(
        functools.partial(norm_kernel, blocks),
        name="pre_norm",
        grid=(blocks + 1,),
        in_specs=[
            pl.BlockSpec((T, D), lambda j: (jnp.minimum(j, blocks - 1), 0)),
            pl.BlockSpec((extra, D), lambda j: (0, 0)),
            pl.BlockSpec((1, D), lambda j: (0, 0)),
        ],
        out_specs=pl.BlockSpec((T, D), lambda j: (j, 0)),
        out_shape=jax.ShapeDtypeStruct((rows + extra, D), bf16),
        compiler_params=params(),
        cost_estimate=cost(6 * rows * D, 4 * rows * D),
    )(hid, rim, gain)


def states_kernel(xbc, halo, cw, hp, x, pre, bc, s, dt, ld, ldt, st0, comb, dec, pad, tail, carry, xw):
    j = pl.program_id(0)
    m, b = j // 2, j % 2
    before = jnp.where(b == 0, halo[pl.ds(8 * m, 8), :XC], tail[...])
    pad[0:8] = before
    pad[8 : 8 + T] = xbc[:, :XC]
    tail[...] = xbc[T - 8 : T, :XC]
    step = softplus(xbc[:, XC:XP] + hp[0:1, :])
    step = jnp.where(iota((T, 128), 1) < HH, step, 0.0)
    logd = masked_sums(iota((T, T), 0) >= iota((T, T), 1), -hp[1:2, :] * step)
    dt[...] = step
    ld[...] = logd
    ldt[0] = logd.T[:32]
    tailw = jnp.exp(logd[T - 1 : T] - logd) * step
    lanes = slice(W, XC)
    a = conv_taps(pad, cw, lanes)
    pre[:, lanes] = a
    act = a * lax.logistic(a)
    bc[...] = act
    s[...] = fine(nt, act[:, N:], act[:, :N])
    for i in range(W // 128):
        lanes = slice(128 * i, 128 * i + 128)
        a = conv_taps(pad, cw, lanes)
        pre[:, lanes] = a
        act_x = a * lax.logistic(a)
        x[:, lanes] = act_x
        xw[:, lanes] = (act_x * spread(tailw, 2 * i, 2)).astype(bf16)
    st = tn(act[:, :N].astype(bf16), xw[...])
    last = jnp.exp(logd[T - 8 : T])
    decay = jnp.concatenate([spread(last, 4 * i, 4) for i in range(W // 256)], axis=1)[7:8]
    dec[0] = jnp.broadcast_to(decay, (8, W))

    @pl.when(b == 0)
    def _():
        st0[0] = st
        carry[...] = st

    @pl.when(b == 1)
    def _():
        comb[0] = (decay * carry[...] + st).astype(bf16)


def block_states(xbc, cw, hp, micros):
    blocks = 2 * micros
    rows = blocks * T
    blk = lambda j: (j % 2) * micros + j // 2
    out = lambda *sh: jax.ShapeDtypeStruct(sh, f32)
    whole = lambda a: pl.BlockSpec(a.shape, lambda j: (0, 0))
    return pl.pallas_call(
        states_kernel,
        name="block_states",
        grid=(blocks,),
        in_specs=[
            pl.BlockSpec((T, XP), lambda j: (blk(j), 0)),
            pl.BlockSpec((8 * micros, XP), lambda j: (rows // (8 * micros), 0)),
            whole(cw),
            whole(hp),
        ],
        out_specs=[
            pl.BlockSpec((T, W), lambda j: (blk(j), 0)),
            pl.BlockSpec((T, XC), lambda j: (blk(j), 0)),
            pl.BlockSpec((T, 2 * N), lambda j: (blk(j), 0)),
            pl.BlockSpec((T, T), lambda j: (blk(j), 0)),
            pl.BlockSpec((T, 128), lambda j: (blk(j), 0)),
            pl.BlockSpec((T, 128), lambda j: (blk(j), 0)),
            pl.BlockSpec((1, 32, T), lambda j: (blk(j), 0, 0)),
            pl.BlockSpec((1, N, W), lambda j: (j // 2, 0, 0)),
            pl.BlockSpec((1, N, W), lambda j: (j // 2, 0, 0)),
            pl.BlockSpec((1, 8, W), lambda j: (blk(j), 0, 0)),
        ],
        out_shape=[
            out(rows, W),
            out(rows, XC),
            out(rows, 2 * N),
            out(rows, T),
            out(rows, 128),
            out(rows, 128),
            out(blocks, 32, T),
            out(micros, N, W),
            jax.ShapeDtypeStruct((micros, N, W), bf16),
            out(blocks, 8, W),
        ],
        scratch_shapes=[
            pltpu.VMEM((T + 8, XC), f32),
            pltpu.VMEM((8, XC), f32),
            pltpu.VMEM((N, W), f32),
            pltpu.VMEM((T, W), bf16),
        ],
        compiler_params=params(),
        cost_estimate=cost(blocks * 2 * T * N * W, rows * (XP + W + 800) * 4, rows * XC * 2),
    )(xbc, xbc, cw, hp)


def inner_kernel(s, ld, ldt, dt, x, skip, y):
    g = pl.program_id(1)
    shift = lax.rem(128 - 24 * g, 128)
    logd = pltpu.roll(ld[...], shift, 1) * LOG2E
    step = pltpu.roll(dt[...], shift, 1)
    upper = iota((HT, HT), 0) >= iota((HT, HT), 1)
    lower = iota((HT, T), 0) + HT >= iota((HT, T), 1)
    head = iota((T, 256), 1) // PS
    for q in range(6):
        lanes = slice(256 * q, 256 * q + 256)
        tile = x[:, lanes]
        xdt = tile * spread(step, 4 * q, 4)
        top = skip[0:1, lanes] * tile[:HT]
        bottom = skip[0:1, lanes] * tile[HT:]
        for i in range(4):
            h = 4 * q + i
            row = ldt[0, pl.ds(24 * g + h, 1), :] * LOG2E
            col = logd[:, h : h + 1]
            mine = jnp.where(head == i, xdt, 0.0).astype(bf16)
            decay = jnp.exp2(jnp.where(upper, col[:HT] - row[:, :HT], NEG))
            top = top + nn((decay * s[:HT, :HT]).astype(bf16), mine[:HT])
            decay = jnp.exp2(jnp.where(lower, col[HT:] - row, NEG))
            bottom = bottom + nn((decay * s[HT:, :]).astype(bf16), mine)
        y[:HT, lanes] = top
        y[HT:, lanes] = bottom


def inner_part(s, ld, ldt, dt, x, skip_row):
    rows = x.shape[0]
    blocks, groups = rows // T, W // 1536
    return pl.pallas_call(
        inner_kernel,
        name="inner_part",
        grid=(blocks, groups),
        in_specs=[
            pl.BlockSpec((T, T), lambda j, g: (j, 0)),
            pl.BlockSpec((T, 128), lambda j, g: (j, 0)),
            pl.BlockSpec((1, 32, T), lambda j, g: (j, 0, 0)),
            pl.BlockSpec((T, 128), lambda j, g: (j, 0)),
            pl.BlockSpec((T, 1536), lambda j, g: (j, g)),
            pl.BlockSpec((8, 1536), lambda j, g: (0, g)),
        ],
        out_specs=pl.BlockSpec((T, 1536), lambda j, g: (j, g)),
        out_shape=jax.ShapeDtypeStruct((rows, W), f32),
        compiler_params=params(),
        cost_estimate=cost(
            blocks * HH * 2 * T * T * 256, rows * (2 * W + 1024) * 4, blocks * HH * T * T
        ),
    )(s, ld, ldt, dt, x, skip_row)


def gate_kernel(yin, bc, e, ld, z, y, sums):
    grow = jnp.exp(ld[...])
    cst = bc[:, N:].astype(bf16)
    squares = jnp.zeros((T, 256), f32)
    for i in range(W // 256):
        lanes = slice(256 * i, 256 * i + 256)
        out = yin[:, lanes] + spread(grow, 4 * i, 4) * nn(cst, e[0, :, lanes])
        y[:, lanes] = out
        zt = z[:, lanes]
        g = out * (zt * lax.logistic(zt))
        squares = squares + g * g
    sums[...] = jnp.broadcast_to(jnp.sum(squares, axis=1, keepdims=True), (T, 128))


def gate_part(yin, bc, e, ld, z):
    rows = yin.shape[0]
    blocks = rows // T
    row = lambda c: pl.BlockSpec((T, c), lambda j: (j, 0))
    return pl.pallas_call(
        gate_kernel,
        name="gate_part",
        grid=(blocks,),
        in_specs=[
            row(W),
            row(2 * N),
            pl.BlockSpec((1, N, W), lambda j: (j, 0, 0)),
            row(128),
            row(W),
        ],
        out_specs=[row(W), row(128)],
        out_shape=[
            jax.ShapeDtypeStruct((rows, W), f32),
            jax.ShapeDtypeStruct((rows, 128), f32),
        ],
        input_output_aliases={0: 0},
        compiler_params=params(),
        cost_estimate=cost(2 * rows * N * W, rows * W * 4 * 3, rows * W * 2),
    )(yin, bc, e, ld, z)


def out_back_kernel(cot, w, exact, gfin, dots):
    g = nt(cot[...], w[...])
    gfin[...] = g
    dots[...] = jnp.broadcast_to(jnp.sum(g * exact[...], axis=1, keepdims=True), dots.shape)


def out_back(cot, w, exact):
    rows = cot.shape[0]
    row = lambda c: pl.BlockSpec((T, c), lambda j: (j, 0))
    return pl.pallas_call(
        out_back_kernel,
        name="out_back",
        grid=(rows // T,),
        in_specs=[row(D), pl.BlockSpec((W, D), lambda j: (0, 0)), row(W)],
        out_specs=[row(W), row(128)],
        out_shape=[jax.ShapeDtypeStruct((rows, W), f32), jax.ShapeDtypeStruct((rows, 128), f32)],
        compiler_params=params(),
        cost_estimate=cost(2 * rows * D * W, rows * W * 10 + 2 * D * W),
    )(cot, w, exact)


def gate_back_kernel(
    y, z, gfin, x, sums, dots, bc, e, ld, gain, skip, dec, dz, dy, dc, de1, given, dl, ggain, gskip, dye, keep
):
    j = pl.program_id(0)

    @pl.when(j == 0)
    def _():
        ggain[...] = jnp.zeros_like(ggain)
        gskip[...] = jnp.zeros_like(gskip)

    r = lax.rsqrt(sums[:, 0:1] * (1.0 / DI) + EPS)
    coef = r * r * dots[:, 0:1] * (1.0 / DI)
    grow = jnp.exp(ld[...])
    dlog = jnp.zeros((T, 128), f32)
    dcs = jnp.zeros((T, N), f32)
    for i in range(W // 256):
        lanes = slice(256 * i, 256 * i + 256)
        zt, yt, gf = z[:, lanes], y[:, lanes], gfin[:, lanes]
        sg = lax.logistic(zt)
        silu = zt * sg
        g = yt * silu
        gr = g * r
        ggain[0:1, lanes] += row_sum(gf * gr)
        dg = r * (gf * gain[0:1, lanes]) - g * coef
        dyt = dg * silu
        dz[:, lanes] = (dg * yt * (sg * (1.0 + zt * (1.0 - sg)))).astype(bf16)
        dy[:, lanes] = dyt.astype(bf16)
        xt = x[:, lanes]
        gskip[0:1, lanes] += row_sum(dyt * xt)
        dlog = dlog + per_head(dyt * (yt - skip[0:1, lanes] * xt), 4 * i)
        high, low = halves(dyt * spread(grow, 4 * i, 4))
        dye[:, lanes] = high
        dcs = dcs + (nt(high, e[0, :, lanes]) + nt(low, e[0, :, lanes]))
    dl[...] = dlog
    dc[...] = dcs
    de = tn(bc[:, N:].astype(bf16), dye[...])

    @pl.when(j % 2 == 0)
    def _():
        de1[0] = de
        keep[...] = de

    @pl.when(j % 2 == 1)
    def _():
        given[0] = (de + dec[0, 0:1] * keep[...]).astype(bf16)


def gate_back(y, z, gfin, x, sums, dots, bc, e, ld, gain, skip_row, dec, micros):
    rows = y.shape[0]
    blocks = rows // T
    blk = lambda p: (1 - p % 2) * micros + p // 2
    row = lambda c: pl.BlockSpec((T, c), lambda p: (blk(p), 0))
    fixed = pl.BlockSpec((8, W), lambda p: (0, 0))
    state = pl.BlockSpec((1, N, W), lambda p: (blk(p), 0, 0))
    chip = pl.BlockSpec((1, N, W), lambda p: (p // 2, 0, 0))
    sh = jax.ShapeDtypeStruct
    return pl.pallas_call(
        gate_back_kernel,
        name="gate_back",
        grid=(blocks,),
        in_specs=[
            row(W), row(W), row(W), row(W), row(128), row(128), row(2 * N), state, row(128),
            fixed, fixed, pl.BlockSpec((1, 8, W), lambda p: (blk(p), 0, 0)),
        ],
        out_specs=[row(W), row(W), row(N), chip, chip, row(128), fixed, fixed],
        out_shape=[
            sh((rows, W), bf16),
            sh((rows, W), bf16),
            sh((rows, N), f32),
            sh((micros, N, W), f32),
            sh((micros, N, W), bf16),
            sh((rows, 128), f32),
            sh((8, W), f32),
            sh((8, W), f32),
        ],
        scratch_shapes=[pltpu.VMEM((T, W), bf16), pltpu.VMEM((N, W), f32)],
        compiler_params=params(),
        cost_estimate=cost(8 * rows * N * W, rows * W * 24, rows * W * 2),
    )(y, z, gfin, x, sums, dots, bc, e, ld, gain, skip_row, dec)


def inner_back_kernel(s, bc, ld, ldt, dt, x, dy, skip, dx, xv, dbc, st, dst):
    g = pl.program_id(1)

    @pl.when(g == 0)
    def _():
        st[...] = s[...].T
        dst[...] = jnp.zeros_like(dst)
        xv[...] = jnp.zeros_like(xv)

    shift = lax.rem(128 - 24 * g, 128)
    logd = pltpu.roll(ld[...], shift, 1) * LOG2E
    step = pltpu.roll(dt[...], shift, 1)
    early = iota((HT, T), 1) >= iota((HT, T), 0)
    late = iota((HT, HT), 1) >= iota((HT, HT), 0)
    head = iota((T, 256), 1) // PS
    gtop = jnp.zeros((HT, T), f32)
    gbottom = jnp.zeros((HT, HT), f32)
    sums = jnp.zeros((T, 128), f32)
    for q in range(6):
        lanes = slice(256 * q, 256 * q + 256)
        steps = spread(step, 4 * q, 4)
        tile = x[:, lanes]
        xdt = tile * steps
        dyt = dy[:, lanes]
        top = jnp.zeros((HT, 256), f32)
        bottom = jnp.zeros((HT, 256), f32)
        for i in range(4):
            h = 4 * q + i
            row = ldt[0, pl.ds(24 * g + h, 1), :] * LOG2E
            col = logd[:, h : h + 1]
            dmine = jnp.where(head == i, dyt, jnp.zeros_like(dyt))
            xmine = jnp.where(head == i, xdt, 0.0).astype(bf16)
            decay = jnp.exp2(jnp.where(early, row - col[:HT], NEG))
            top = top + nn((decay * st[:HT, :]).astype(bf16), dmine)
            gtop = gtop + nt(xmine[:HT], dyt) * decay
            decay = jnp.exp2(jnp.where(late, row[:, HT:] - col[HT:], NEG))
            bottom = bottom + nn((decay * st[HT:, HT:]).astype(bf16), dmine[HT:])
            gbottom = gbottom + nt(xmine[HT:], dyt[HT:]) * decay
        total = jnp.concatenate([top, bottom], axis=0)
        dx[:, lanes] = total * steps + skip[0:1, lanes] * dyt.astype(f32)
        sums = sums + per_head(tile * total, 24 * g + 4 * q)
    xv[...] += sums
    dst[:HT, :] += gtop
    dst[HT:, HT:] += gbottom

    @pl.when(g == pl.num_programs(1) - 1)
    def _():
        dbc[:, :N] = fine(nn, dst[...], bc[:, N:])
        dbc[:, N:] = fine(tn, dst[...], bc[:, :N])


def inner_back(s, bc, ld, ldt, dt, x, dy, skip_row):
    rows = x.shape[0]
    blocks, groups = rows // T, W // 1536
    row = lambda c: pl.BlockSpec((T, c), lambda j, g: (j, 0))
    tile = pl.BlockSpec((T, 1536), lambda j, g: (j, g))
    sh = jax.ShapeDtypeStruct
    return pl.pallas_call(
        inner_back_kernel,
        name="inner_back",
        grid=(blocks, groups),
        in_specs=[
            row(T),
            row(2 * N),
            row(128),
            pl.BlockSpec((1, 32, T), lambda j, g: (j, 0, 0)),
            row(128),
            tile,
            tile,
            pl.BlockSpec((8, 1536), lambda j, g: (0, g)),
        ],
        out_specs=[tile, row(128), row(2 * N)],
        out_shape=[sh((rows, W), f32), sh((rows, 128), f32), sh((rows, 2 * N), f32)],
        scratch_shapes=[pltpu.VMEM((T, T), f32), pltpu.VMEM((T, T), f32)],
        compiler_params=params(),
        cost_estimate=cost(
            2 * blocks * HH * 2 * T * T * 256, rows * (2 * W + 1024) * 4, blocks * HH * T * T
        ),
    )(s, bc, ld, ldt, dt, x, dy, skip_row)


def conv_back_kernel(
    micros, xbc, prev, pre, dxi, xv, dbc, bc, dt, ld, later1, de1, dec, e, dc, dla, cw, hp,
    gp, gcw, ghp, pad, dpre, nxt, edge,
):
    p = pl.program_id(0)
    b = 1 - p % 2

    @pl.when(p == 0)
    def _():
        gcw[...] = jnp.zeros_like(gcw)
        ghp[...] = jnp.zeros_like(ghp)

    @pl.when(p == 2 * micros)
    def _():
        gp[0 : 8 * micros] = edge[...].astype(bf16)

    @pl.when(p < 2 * micros)
    def _():
        pad[0:8] = prev[:, :XC]
        pad[8 : 8 + T] = xbc[:, :XC]
        dpre[0:8] = jnp.zeros((8, XC), f32)
        dpre[8 + T : 16 + T] = jnp.where(b == 1, 0.0, nxt[...])
        step, logd = dt[...], ld[...]
        fade = jnp.exp(logd[T - 1 : T] - logd)
        tailw = fade * step
        bst = bc[:, :N].astype(bf16)

        def through_conv(grad, lanes, a, sg):
            d = grad * (sg * (1.0 + a * (1.0 - sg)))
            dpre[8 : 8 + T, lanes] = d
            gcw[4:5, lanes] += row_sum(d)
            for k in range(KC):
                gcw[k : k + 1, lanes] += row_sum(d * pad[pl.ds(5 + k, T), lanes])
            total = cw[0:1, lanes] * dpre[pl.ds(11, T), lanes]
            rim = cw[0:1, lanes] * dpre[pl.ds(3, 8), lanes]
            for k in range(1, KC):
                total = total + cw[k : k + 1, lanes] * dpre[pl.ds(11 - k, T), lanes]
                rim = rim + cw[k : k + 1, lanes] * dpre[pl.ds(3 - k, 8), lanes]
            gp[:, lanes] = total.astype(bf16)
            nxt[:, lanes] = d[0:8]

            @pl.when(b == 0)
            def _():
                edge[pl.ds(pl.multiple_of(8 * (p // 2), 8), 8), lanes] = rim

        dw = jnp.zeros((T, 128), f32)
        dbs = jnp.zeros((T, N), f32)
        ddec = jnp.zeros((8, 128), f32)
        for i in range(W // 256):
            lanes = slice(256 * i, 256 * i + 256)
            lat = later1[0, :, lanes]
            earlier = de1[0, :, lanes] + dec[0, 0:1, lanes] * lat.astype(f32)
            lat = jnp.where(b == 1, lat, earlier.astype(bf16))
            spreadw = spread(tailw, 4 * i, 4)
            a = pre[:, lanes]
            sg = lax.logistic(a)
            xt = a * sg
            bl = nn(bst, lat)
            dw = dw + nn((xt * bl).astype(bf16), head_place(256, 4 * i))
            high, low = halves(xt * spreadw)
            dbs = dbs + (nt(high, lat) + nt(low, lat))
            both = row_sum(lat.astype(f32) * e[0, :, lanes].astype(f32))
            ddec = ddec + per_head(jnp.broadcast_to(both, (8, 256)), 4 * i)
            through_conv(dxi[:, lanes] + bl * spreadw, lanes, a, sg)
        a = pre[:, W:]
        both = jnp.concatenate([dbc[:, :N] + dbs, dbc[:, N:] + dc[...]], axis=1)
        through_conv(both, slice(W, XC), a, lax.logistic(a))
        q = dw * tailw
        dlog = dla[...] - step * xv[...] - q
        dlast = row_sum(q) + ddec[0:1] * jnp.exp(logd[T - 1 : T])
        dlog = dlog + jnp.where(iota((T, 128), 0) == T - 1, dlast, 0.0)
        dcum = masked_sums(iota((T, T), 1) >= iota((T, T), 0), dlog)
        dstep = xv[...] + dw * fade - hp[1:2, :] * dcum
        draw = dstep * lax.logistic(xbc[:, XC:XP] + hp[0:1, :])
        draw = jnp.where(iota((T, 128), 1) < HH, draw, 0.0)
        ghp[0:1] += row_sum(draw)
        ghp[1:2] -= row_sum(dcum * step)
        gp[:, XC:XP] = draw.astype(bf16)

        @pl.when(b == 0)
        def _():
            edge[pl.ds(pl.multiple_of(8 * (p // 2), 8), 8), XC:XP] = jnp.zeros((8, 128), f32)


def conv_back(xbc, pre, dxi, xv, dbc, bc, dt, ld, later1, de1, dec, e, dc, dla, cw, hp, micros):
    blocks = 2 * micros
    rows = blocks * T
    blk = lambda p: jnp.where(p < blocks, (1 - p % 2) * micros + p // 2, micros - 1)
    row = lambda c: pl.BlockSpec((T, c), lambda p: (blk(p), 0))
    whole = lambda a: pl.BlockSpec(a.shape, lambda p: (0, 0))
    state = pl.BlockSpec((1, N, W), lambda p: (blk(p), 0, 0))

    unit = lambda p: jnp.minimum(p // 2, micros - 1)
    chip = pl.BlockSpec((1, N, W), lambda p: (unit(p), 0, 0))

    def before(p):
        k = blk(p)
        return (jnp.where(k >= micros, (k - micros + 1) * (T // 8) - 1, rows // 8 + k), 0)

    return pl.pallas_call(
        functools.partial(conv_back_kernel, micros),
        name="conv_back",
        grid=(blocks + 1,),
        in_specs=[
            row(XP),
            pl.BlockSpec((8, XP), before),
            row(XC), row(W), row(128), row(2 * N), row(2 * N), row(128), row(128),
            chip, chip, pl.BlockSpec((1, 8, W), lambda p: (micros + unit(p), 0, 0)), state,
            row(N), row(128), whole(cw), whole(hp),
        ],
        out_specs=[
            pl.BlockSpec((T, XP), lambda p: (jnp.where(p < blocks, blk(p), blocks), 0)),
            pl.BlockSpec((8, XC), lambda p: (0, 0)),
            pl.BlockSpec((8, 128), lambda p: (0, 0)),
        ],
        out_shape=[
            jax.ShapeDtypeStruct((rows + 8 * micros, XP), bf16),
            jax.ShapeDtypeStruct((8, XC), f32),
            jax.ShapeDtypeStruct((8, 128), f32),
        ],
        scratch_shapes=[
            pltpu.VMEM((T + 8, XC), f32),
            pltpu.VMEM((T + 16, XC), f32),
            pltpu.VMEM((8, XC), f32),
            pltpu.VMEM((8 * micros, XP), f32),
        ],
        compiler_params=pltpu.CompilerParams(vmem_limit_bytes=58 * MB_),
        cost_estimate=cost(6 * rows * N * W, rows * W * 18, rows * XC * 2),
    )(xbc, xbc, pre, dxi, xv, dbc, bc, dt, ld, later1, de1, dec, e, dc, dla, cw, hp)


AXIS = {"z": Z, "l": "zl", "s": "s"}
RING = 4
CHIPS = 16


def hop(value, axis):
    n = RING if axis == "z" else 2
    return lax.ppermute(value, AXIS[axis], [(i, (i + 1) % n) for i in range(n)])


def fence(groups, *values):
    held = [{k: g.live[k] for k in g.live} for g in groups]
    held, values = lax.optimization_barrier((held, values))
    for g, h in zip(groups, held):
        g.live.update(h)
    return values


def after(groups, *values):
    values, _ = lax.optimization_barrier((values, [v for g in groups for v in g.sent]))
    for g in groups:
        g.sent = ()
    return values


def partly(group, names, *values):
    held = {k: group.live[k] for k in group.live if k[:-1] in names}
    held, values = lax.optimization_barrier((held, values))
    group.live.update(held)
    return values


class Moves:
    sent = ()

    def send(self, value, axis):
        self.sent = [*self.sent, value]
        return hop(value, axis)


WAYS = (("s", "l"), ("l", "s"))


def lanes_of(widths):
    return [slice(sum(widths[:c]), sum(widths[: c + 1])) for c in range(len(widths))]


def near(c, kl, ks):
    return (ks, kl) if c == 0 else (kl, ks)


class Gather(Moves):
    def __init__(self, own, widths, turns):
        self.widths, self.turns = widths, turns
        self.live = {"g0": own}
        self.n = 1
        self.parts = []

    def z(self):
        self.live[f"g{self.n}"] = self.send(self.live[f"g{self.n - 1}"], "z")
        self.n += 1

    def first(self, h):
        some = jnp.stack([self.live[f"g{k}"] for k in self.turns[h]], 0)
        for k in self.turns[h]:
            if k < self.n - 1 or self.n == RING:
                self.live.pop(f"g{k}")
        for c, lanes in enumerate(lanes_of(self.widths)):
            self.live[f"p{h}{c}"] = some[:, :, lanes]
            self.live[f"q{h}{c}"] = self.send(some[:, :, lanes], WAYS[c][0])

    def second(self, h):
        for c in range(2):
            more = jnp.concatenate([self.live.pop(f"p{h}{c}"), self.live.pop(f"q{h}{c}")], 0)
            self.parts += [more, self.send(more, WAYS[c][1])]

    def place(self, c, kz, kl, ks):
        ka, kb = near(c, kl, ks)
        h = [kz in t for t in self.turns].index(True)
        turn = self.turns[h]
        return (h * 2 + c) * 2 + kb, ka * len(turn) + turn.index(kz)


class RingLast(Moves):
    def __init__(self, own, widths):
        self.widths = widths
        self.live = {f"p{c}": own[None, :, lanes] for c, lanes in enumerate(lanes_of(widths))}
        self.parts = []

    def step(self, n):
        for c in range(2):
            p = self.live[f"p{c}"]
            self.live[f"p{c}"] = jnp.concatenate([p, self.send(p, WAYS[c][n])], 0)

    def z(self):
        if not self.parts:
            self.live["p"] = jnp.concatenate([self.live.pop("p0"), self.live.pop("p1")], 0)
            self.parts = [self.live["p"]]
        self.live["p"] = self.send(self.live["p"], "z")
        self.parts.append(self.live["p"])

    def place(self, c, kz, kl, ks):
        ka, kb = near(c, kl, ks)
        return kz, c * 4 + kb * 2 + ka


class Scatter(Moves):
    def __init__(self, widths, turns):
        self.widths, self.turns = widths, turns
        self.live = {}
        self.order = [k for t in turns for k in t]

    def load(self, parts):
        parts = iter(parts)
        for h in range(len(self.turns)):
            for c in range(2):
                self.live[f"k{h}{c}"] = next(parts)
                self.live[f"s{h}{c}"] = next(parts)

    def second(self, h):
        for c in range(2):
            self.live[f"r{h}{c}"] = self.send(self.live.pop(f"s{h}{c}"), WAYS[c][1])

    def first(self, h):
        n = len(self.turns[h])
        for c in range(2):
            got, kept = self.live.pop(f"r{h}{c}"), self.live.pop(f"k{h}{c}")
            self.live[f"m{h}{c}"] = got[:n].astype(f32) + kept[:n].astype(f32)
            give = (got[n:].astype(f32) + kept[n:].astype(f32)).astype(bf16)
            self.live[f"n{h}{c}"] = self.send(give, WAYS[c][0])

    def ring(self, k):
        h = [self.order[k] in t for t in self.turns].index(True)
        at = self.turns[h].index(self.order[k])
        if at == 0:
            self.live["w"] = jnp.concatenate(
                [self.live.pop(f"m{h}{c}") + self.live.pop(f"n{h}{c}").astype(f32) for c in range(2)], 2
            )
        total = self.live["w"][at]
        if k:
            total = total + self.live.pop("t").astype(f32)
        if k == RING - 1:
            self.live.pop("w")
            return total
        self.live["t"] = self.send(total.astype(bf16), "z")

    def place(self, c, kz, kl, ks):
        ka, kb = near(c, kl, ks)
        h = [kz in t for t in self.turns].index(True)
        turn = self.turns[h]
        return (h * 2 + c) * 2 + kb, ka * len(turn) + turn.index(kz)

    def shapes(self, r):
        return [
            jax.ShapeDtypeStruct((2 * len(t), r, w), bf16)
            for t in self.turns
            for w in self.widths
            for _ in range(2)
        ]


def move_kernel(table, r, out_of, where, *refs):
    sems = refs[-1]
    refs = refs[:-1]
    whole = refs[-1] if out_of else refs[0]
    arrays = refs[:-1] if out_of else refs[1:]
    copies = []
    for n, (array, entry, k, lanes) in enumerate(table):
        row = pl.multiple_of(where[k] * r, 16)
        place = whole.at[pl.ds(row, r), lanes]
        piece = arrays[array].at[entry]
        pair = (piece, place) if out_of else (place, piece)
        copies.append(pltpu.make_async_copy(*pair, sems.at[n]))
    for c in copies:
        c.start()
    for c in copies:
        c.wait()


def move(group, where, r, given, shapes, out_of):
    table = []
    for c, lanes in enumerate(lanes_of(group.widths)):
        for k in range(CHIPS):
            table.append((*group.place(c, k // 4, k // 2 % 2, k % 2), k, lanes))
    any_ = pl.BlockSpec(memory_space=pl.ANY)
    return pl.pallas_call(
        functools.partial(move_kernel, tuple(table), r, out_of),
        name="join" if out_of else "deal",
        in_specs=[pl.BlockSpec(memory_space=pltpu.SMEM)] + [any_] * len(given),
        out_specs=[any_] * len(shapes),
        out_shape=shapes,
        scratch_shapes=[pltpu.SemaphoreType.DMA((len(table),))],
        compiler_params=pltpu.CompilerParams(vmem_limit_bytes=MB_),
        cost_estimate=cost(0, 4 * CHIPS * r * sum(group.widths)),
    )(where, *given)


def join(group, where, r):
    shape = jax.ShapeDtypeStruct((CHIPS * r, sum(group.widths)), bf16)
    return move(group, where, r, group.parts, [shape], True)[0]


def deal(group, where, r, whole):
    group.load(move(group, where, r, [whole], group.shapes(r), False))


def swap(value, axis="c"):
    return lax.ppermute(value, axis, [(0, 1), (1, 0)])


def two(mine, other, at):
    return jnp.where(at == 0, jnp.stack([mine, other]), jnp.stack([other, mine]))


class Plain:
    def __init__(self, axes):
        self.axes = axes

    def gather(self, piece):
        return lax.all_gather(piece, self.axes, axis=0, tiled=True)

    def reduce(self, grad):
        return lax.psum_scatter(grad, self.axes, scatter_dimension=0, tiled=True).astype(f32)


def body(
    hidden, in_weight, out_weight, conv_weight, conv_bias, norm_gain, gate_gain,
    step_bias, decay_rate, skip_gain, cotangent,
):
    nz, nl, ns = lax.axis_size(Z), lax.axis_size("zl"), lax.axis_size("s")
    core = lax.axis_index("c")
    micros = hidden.shape[0]
    rows = micros * 2 * T
    r_in, r_out = in_weight.shape[0], out_weight.shape[0]
    r = 2 * r_in
    fast = (nz, nl, ns) == (RING, 2, 2) and r % 16 == 0 and r_out == r
    onward = [(i, i + 1) for i in range(ns - 1)]
    backward = [(i + 1, i) for i in range(ns - 1)]
    turn = [(a * 2 + b, b * 2 + a) for a in range(2) for b in range(2)]

    def cut(k):
        part = lambda at, width: lax.dynamic_slice_in_dim(in_weight, at + k * width, width, 1)
        steps = in_weight[:, DI + CONV :]
        steps = jnp.where(k == 0, steps[:, :HH], steps[:, HH:])
        return jnp.concatenate(
            [
                part(DI, W),
                in_weight[:, 2 * DI : 2 * DI + 2 * N],
                jnp.pad(steps, ((0, 0), (0, 128 - HH))),
                part(0, W),
            ],
            axis=1,
        )

    ours, theirs = cut(core), cut(1 - core)
    theirs, out_weight, hidden, cotangent = lax.optimization_barrier(
        (theirs, out_weight, hidden, cotangent)
    )
    chip_rows = two(ours, swap(theirs), core).reshape(r, -1)
    w_own = lax.ppermute(out_weight, ("za", "c"), turn)

    ins = Plain(ALL[:4])
    outs = Plain(("zb", "zl", "s", "za"))

    n_c = conv_bias.shape[0]
    packed = jnp.concatenate([conv_weight.T.reshape(-1), conv_bias, norm_gain, gate_gain])

    def spread_out(small, a, at):
        mine, other = (jnp.expand_dims(v, at) for v in (small, swap(small, a)))
        here = lax.axis_index(a) == 0
        return jnp.where(here, jnp.concatenate([mine, other], at), jnp.concatenate([other, mine], at))

    hid_own = hidden.reshape(micros, T, D)
    cot_own = cotangent.reshape(micros, T, D)
    hid_other, cot_other = swap(hid_own), swap(cot_own)

    def chip_tokens(mine, other):
        return two(mine, other, core).reshape(rows, D)

    def rim_of(tokens):
        return lax.ppermute(tokens.reshape(2, micros, T, D)[1, :, T - 8 :], "s", onward)

    if fast:
        back = jnp.arange(CHIPS)
        kz = (lax.axis_index(Z) - back // 4) % RING
        kl = (lax.axis_index("zl") - back // 2) % 2
        ks = (lax.axis_index("s") - back) % 2
        in_place = ((kz * 2 + kl) * 2 + ks).astype(jnp.int32)
        out_place = ((((kz % 2) * 2 + kl) * 2 + ks) * 2 + kz // 2).astype(jnp.int32)
        x_cols, z_cols, o_cols = (896, 1024), (768, 768), (768, 768)
        small = spread_out(packed, "za", 0)
        small = spread_out(small, "zb", 1)
        chip_rows, small = lax.optimization_barrier((chip_rows, small))
        halves_, ring_ = ((0, 1), (2, 3)), ((0, 1, 2, 3),)
        gx_ = Gather(chip_rows[:, :XP], x_cols, halves_)
        gz_ = Gather(chip_rows[:, XP:], z_cols, ring_)
        go_ = RingLast(w_own, o_cols)
        every = [gx_, gz_, go_]
        small = spread_out(small, "zl", 2)
        gx_.z()
        go_.step(0)
        small, hid_other, cot_other = fence(every, small, hid_other, cot_other)
        small = spread_out(small, "s", 3)
        gx_.z()
        gx_.first(0)
        hid_own_, hid_other = after(every, hid_own, hid_other)
        hid_all = chip_tokens(hid_own_, hid_other)
        rim = rim_of(hid_all)
        small = spread_out(small, "c", 4).reshape(-1, packed.shape[0])
        small, rim, hid_all = fence(every, small, rim, hid_all)
        gx_.z()
        gx_.second(0)
        gz_.z()
        small, rim, hid_all, cot_own_, cot_other = after(
            every, small, rim, hid_all, cot_own, cot_other
        )
        cot_all = chip_tokens(cot_own_, cot_other)
    else:
        small = lax.all_gather(packed, ALL)
        hid_all, cot_all = chip_tokens(hid_own, hid_other), chip_tokens(cot_own, cot_other)
        rim = rim_of(hid_all)
        w_x, w_z = ins.gather(chip_rows[:, :XP]), ins.gather(chip_rows[:, XP:])

    rim = jnp.where(iota(rim.shape, 1) >= 5, rim, jnp.zeros_like(rim)).reshape(8 * micros, D)
    devices = small.shape[0]
    taps = small[:, : KC * n_c].reshape(devices, KC, n_c).transpose(1, 0, 2).reshape(KC, CONV)
    bias = small[:, KC * n_c : (KC + 1) * n_c].reshape(1, CONV)
    norm_vec = small[:, (KC + 1) * n_c : (KC + 1) * n_c + r_in].reshape(D).astype(f32)
    gate_vec = small[:, (KC + 1) * n_c + r_in :].reshape(1, DI)
    conv_all = jnp.concatenate([taps, bias, jnp.zeros((3, CONV), bf16)], 0).astype(f32)
    cw = jnp.concatenate(
        [lax.dynamic_slice_in_dim(conv_all, core * W, W, 1), conv_all[:, DI:]], axis=1
    )
    gain = jnp.broadcast_to(lax.dynamic_slice_in_dim(gate_vec, core * W, W, 1).astype(f32), (8, W))
    heads = jnp.stack([step_bias, decay_rate, skip_gain])
    heads = lax.dynamic_slice_in_dim(heads, core * HH, HH, 1)
    hp = jnp.pad(heads, ((0, 5), (0, 128 - HH)))
    skip_row = jnp.broadcast_to(jnp.repeat(heads[2], PS)[None], (8, W))
    normed = pre_norm(hid_all, rim, norm_vec[None])
    if fast:
        normed, cot_all, cw, hp, gain, skip_row = fence(
            every, normed, cot_all, cw, hp, gain, skip_row
        )
        gx_.first(1)
        go_.step(1)
        gz_.z()
        (normed,) = fence([gx_, gz_], normed)
        gx_.second(1)
        gz_.z()
        (normed,) = after([gx_, gz_], normed)

    if fast:
        (normed,) = fence(every, normed)
        gz_.first(0)
        go_.z()
        (normed,) = after([gz_, go_], normed)
        w_x = join(gx_, in_place, r)
    xbc = nn(normed, w_x)
    if fast:
        (xbc,) = fence([gz_], xbc)
        gz_.second(0)
        (xbc,) = after([gz_], xbc)
        go_.live, xbc = lax.optimization_barrier((go_.live, xbc))
        go_.z()
        (xbc,) = after([go_], xbc)
    else:
        w_o = outs.gather(w_own)
    x, pre, bc, s, dt, ld, ldt, st0, comb, dec8 = block_states(xbc, cw, hp, micros)
    dec = dec8[:, 0].reshape(2, micros, 1, W)
    if fast:
        comb, s = lax.optimization_barrier((comb, s))
    if ns == 2:
        first = lax.ppermute(comb, "s", onward)
    else:
        first = jnp.zeros_like(comb)
        chip_decay = dec[0] * dec[1]
        for _ in range(ns - 1):
            out = (chip_decay * first.astype(f32) + comb.astype(f32)).astype(bf16)
            first = lax.ppermute(out, "s", onward)
    yin = inner_part(s, ld, ldt, dt, x, skip_row)
    if fast:
        (yin,) = fence([gz_, go_], yin)
        go_.z()
        (yin,) = after([go_], yin)
    second = (dec[0] * first.astype(f32) + st0).astype(bf16)
    entering = jnp.stack([first, second], 0).reshape(2 * micros, N, W)
    if fast:
        w_z = join(gz_, in_place, r)
    z = nn(normed[:rows], w_z)
    y, sums = gate_part(yin, bc, entering, ld, z)
    sums = sums + swap(sums)
    root = lax.rsqrt(sums[:, :1] * (1.0 / DI) + EPS)
    exact = y * (z * lax.logistic(z)) * root * gain[:1]
    fin = exact.astype(bf16)
    g_out = tn(fin, cot_all).astype(bf16)
    if fast:
        ring_back = ((1, 2, 3, 0),)
        so_ = Scatter(o_cols, ring_back)
        deal(so_, out_place, r, g_out)
        (cot_all,) = fence([so_], cot_all)
        so_.second(0)
        (cot_all,) = after([so_], cot_all)
        w_o = join(go_, out_place, r)

    gfin, dots = out_back(cot_all, w_o, exact)

    partial_out = nn(fin, w_o).reshape(2, micros, T, D)
    give = lax.dynamic_index_in_dim(partial_out, 1 - core, 0, False).astype(bf16)
    keep = lax.dynamic_index_in_dim(partial_out, core, 0, False)
    given_out = swap(give)
    block_out = (hid_own.astype(f32) + keep + given_out.astype(f32)).astype(bf16)
    if fast:
        dots, gfin, give = fence([so_], dots, gfin, give)
        so_.first(0)
        (y,) = after([so_], y)
    dots = dots + swap(dots)
    dz, dy, dc, de1, given, dla, ggain, gskip = gate_back(
        y, z, gfin, x, sums, dots, bc, entering, ld, gain, skip_row, dec8, micros
    )
    if ns == 2:
        dz, given = lax.optimization_barrier((dz, given))
        later1 = lax.ppermute(given, "s", backward)
    else:
        later1 = jnp.zeros((micros, N, W), bf16)
        for _ in range(ns - 1):
            out = given.astype(f32) + dec[0] * dec[1] * later1.astype(f32)
            later1 = lax.ppermute(out.astype(bf16), "s", backward)
    gz = tn(normed[:rows], dz).astype(bf16)
    if fast:
        sz_ = Scatter(z_cols, ring_back)
        deal(sz_, in_place, r, gz)
        (dy,) = fence([so_, sz_], dy)
        so_.ring(0)
        sz_.second(0)
        (dy,) = after([so_, sz_], dy)

    dxi, xv, dbc = inner_back(s, bc, ld, ldt, dt, x, dy, skip_row)
    if fast:
        dxi, later1 = fence([so_, sz_], dxi, later1)
        so_.ring(1)
        sz_.first(0)
        (dxi,) = after([so_, sz_], dxi)
    gp, gcw, ghp = conv_back(
        xbc, pre, dxi, xv, dbc, bc, dt, ld, later1, de1, dec8, entering, dc, dla, cw, hp, micros
    )
    if fast:
        (gp,) = fence([so_, sz_], gp)
        so_.ring(2)
        sz_.ring(0)
        (gp,) = after([so_, sz_], gp)
    gx = tn(normed, gp).astype(bf16)

    wide = lambda v: jnp.pad(v, ((0, 0), (0, XC - v.shape[1])))
    tiny = jnp.concatenate(
        [gcw[:5], wide(ggain[:1]), wide(gskip[:1]), wide(ghp[:2].reshape(1, 256))], axis=0
    )
    if fast:
        sx_ = Scatter(x_cols, ((1, 2), (3, 0)))
        deal(sx_, in_place, r, gx)
        gp, tiny = fence([so_, sz_, sx_], gp, tiny)
        sx_.second(0)
        sz_.ring(1)
        gp, tiny = after([sx_, sz_], gp, tiny)
        tiny = tiny + swap(tiny, "zb")
        g_out = so_.ring(3)
    else:
        g_out = outs.reduce(g_out)
    g_out = lax.ppermute(g_out, ("za", "c"), turn)

    gn = nt(gp, w_x)
    edge = lax.ppermute(gn[rows:].astype(bf16), "s", backward).reshape(1, micros, 8, D)
    if fast:
        gn, dz, tiny = fence([sz_], gn, dz, tiny)
        tiny = tiny + swap(tiny, "za")
    gn = gn[:rows] + nt(dz, w_z)

    if fast:
        gn, g_out, tiny = fence([sz_, sx_], gn, g_out, tiny)
        sx_.first(0)
        sx_.second(1)
        sz_.ring(2)
        (gn,) = after([sx_, sz_], gn)
    gn = gn.reshape(2, micros, T, D)
    edge = jnp.where(iota(edge.shape, 2) >= 5, edge.astype(f32), 0.0)
    gn = gn + jnp.pad(edge, ((1, 0), (0, 0), (T - 8, 0), (0, 0)))
    give = lax.dynamic_index_in_dim(gn, 1 - core, 0, False).astype(bf16)
    keep = lax.dynamic_index_in_dim(gn, core, 0, False)
    other = swap(give)
    if fast:
        keep, other = partly(sx_, ("m0", "n0"), keep, other)
        sx_.ring(0)
        keep, other = after([sx_], keep, other)
    gn = keep + other.astype(f32)
    hid_f = hid_own.astype(f32)
    own_scale = lax.rsqrt(jnp.mean(hid_f * hid_f, axis=-1, keepdims=True) + EPS)
    unit = hid_f * own_scale
    gq = gn * norm_vec
    g_hid = cot_own.astype(f32) + own_scale * (
        gq - unit * jnp.mean(gq * unit, axis=-1, keepdims=True)
    )

    if fast:
        tiny, g_hid, block_out = fence([sz_, sx_], tiny, g_hid, block_out)
        sx_.first(1)
        sx_.ring(1)
        (tiny,) = after([sx_], tiny)
        tiny = tiny + swap(tiny, "s")
        gz = sz_.ring(3)

    def exchanged(g):
        g = g.reshape(2, r_in, -1)
        mine = lax.dynamic_index_in_dim(g, core, 0, False)
        return two(mine, swap(lax.dynamic_index_in_dim(g, 1 - core, 0, False)), core)

    if fast:
        tiny, gz = fence([sx_], tiny, gz)
        sx_.ring(2)
        tiny, gz = after([sx_], tiny, gz)
        gz = exchanged(gz)
        tiny = tiny + swap(tiny, "zl")
        tiny, gz = fence([sx_], tiny, gz)
        gx = sx_.ring(3)
    else:
        tiny = lax.psum(tiny, ALL[:4])
        gx, gz = ins.reduce(gx), ins.reduce(gz)
        gz = exchanged(gz)
    gx = exchanged(gx)
    both = two(tiny, swap(tiny), core)
    g_conv = jnp.concatenate([both[0, :5, :W], both[1, :5, :W], both[0, :5, W:] + both[1, :5, W:]], axis=1)
    me = lax.axis_index(ALL)
    g_conv = lax.dynamic_slice_in_dim(g_conv, me * n_c, n_c, 1)
    g_gate = both[:, 5, :W].reshape(-1)
    g_gate = lax.dynamic_slice_in_dim(g_gate, me * r_out, r_out)
    g_skip = both[:, 6, :W].reshape(H, PS).sum(-1)
    g_bias = both[:, 7, :HH].reshape(-1)
    g_rate = both[:, 7, 128 : 128 + HH].reshape(-1)
    g_in = jnp.concatenate(
        [
            gz[0], gz[1],
            gx[0, :, :W], gx[1, :, :W],
            gx[0, :, W:XC] + gx[1, :, W:XC],
            gx[0, :, XC : XC + HH], gx[1, :, XC : XC + HH],
        ],
        axis=1,
    )
    g_norm = jnp.sum(g_in * in_weight.astype(f32), axis=1) / norm_gain.astype(f32)
    return (
        block_out.reshape(hidden.shape),
        g_hid.reshape(hidden.shape),
        g_in,
        g_out,
        g_conv[:KC].T,
        g_conv[KC],
        g_norm,
        g_gate,
        g_bias,
        g_rate,
        g_skip,
    )


def solution(mesh):
    dp, seq = mesh.shape["dp"], mesh.shape["seq"]
    split = Mesh(mesh.devices.reshape(2, dp // 4, 2, seq // 2, 2), ALL)
    token = P(None, ("za", "zb", "zl"), ("s", "c"), None)
    in_specs = (token, P(ALL, None), P(ALL, None), P(ALL, None), P(ALL), P(ALL), P(ALL), P(), P(), P(), token)
    out_specs = (token, token, P(ALL, None), P(ALL, None), P(ALL, None), P(ALL), P(ALL), P(ALL), P(), P(), P())
    return jax.shard_map(body, mesh=split, in_specs=in_specs, out_specs=out_specs, check_vma=False)
```

```python
import functools

import jax
import jax.numpy as jnp
import numpy as np
from jax import lax
from jax.experimental import pallas as pl
from jax.experimental.pallas import tpu as pltpu
from jax.sharding import Mesh
from jax.sharding import PartitionSpec as P

DI = 3072
H = 48
PS = 64
N = 128
KC = 4
CONV = 3328
D = 1536
T = 256
HH = H // 2
W = DI // 2
XC = W + 2 * N
XP = XC + 128
EPS = 1e-05
NEG = -1e30
LOG2E = 1.4426950408889634
HT = T // 2
f32 = jnp.float32
bf16 = jnp.bfloat16
ALL = ("za", "zb", "zl", "s", "c")
Z = ("za", "zb")
MB_ = 1 << 20


def nn(a, b):
    return lax.dot_general(a, b, (((1,), (0,)), ((), ())), preferred_element_type=f32)


def nt(a, b):
    return lax.dot_general(a, b, (((1,), (1,)), ((), ())), preferred_element_type=f32)


def tn(a, b):
    return lax.dot_general(a, b, (((0,), (0,)), ((), ())), preferred_element_type=f32)


def halves(v):
    high = v.astype(bf16)
    return high, (v - high.astype(f32)).astype(bf16)


def fine(dot, a, b):
    (ah, al), (bh, bl) = halves(a), halves(b)
    return dot(ah, bh) + (dot(ah, bl) + dot(al, bh))


def iota(shape, dim):
    return lax.broadcasted_iota(jnp.int32, shape, dim)


def spread(cols, first, heads):
    rows = cols.shape[0]
    head = iota((rows, heads * PS), 1) // PS
    out = jnp.broadcast_to(cols[:, first : first + 1], (rows, heads * PS))
    for i in range(1, heads):
        out = jnp.where(head == i, cols[:, first + i : first + i + 1], out)
    return out


def head_place(lanes, first):
    return (iota((lanes, 128), 0) // PS + first == iota((lanes, 128), 1)).astype(bf16)


def per_head(values, first):
    place = head_place(values.shape[1], first)
    high, low = halves(values)
    return nn(high, place) + nn(low, place)


def masked_sums(mask, values):
    high, low = halves(values)
    ones = mask.astype(bf16)
    return nn(ones, high) + nn(ones, low)


def row_sum(values):
    return jnp.sum(values, axis=0, keepdims=True)


def conv_taps(pad_ref, cw_ref, lanes):
    total = cw_ref[4:5, lanes]
    for k in range(KC):
        total = total + cw_ref[k : k + 1, lanes] * pad_ref[pl.ds(5 + k, T), lanes]
    return total


def softplus(v):
    return jnp.maximum(v, 0.0) + jnp.log1p(jnp.exp(-jnp.abs(v)))


def params(**kw):
    return pltpu.CompilerParams(vmem_limit_bytes=40 * MB_, **kw)


def cost(flops, nbytes, trans=0):
    return pl.CostEstimate(flops=int(flops), bytes_accessed=int(nbytes), transcendentals=int(trans))


def norm_kernel(blocks, hid, rim, gain, out):
    j = pl.program_id(0)

    def scaled(v):
        v = v.astype(f32)
        return (v * lax.rsqrt(jnp.mean(v * v, axis=-1, keepdims=True) + EPS) * gain[0:1]).astype(bf16)

    @pl.when(j < blocks)
    def _():
        out[...] = scaled(hid[...])

    @pl.when(j == blocks)
    def _():
        out[: rim.shape[0]] = scaled(rim[...])


def pre_norm(hid, rim, gain):
    rows, extra = hid.shape[0], rim.shape[0]
    blocks = rows // T
    return pl.pallas_call(
        functools.partial(norm_kernel, blocks),
        name="pre_norm",
        grid=(blocks + 1,),
        in_specs=[
            pl.BlockSpec((T, D), lambda j: (jnp.minimum(j, blocks - 1), 0)),
            pl.BlockSpec((extra, D), lambda j: (0, 0)),
            pl.BlockSpec((1, D), lambda j: (0, 0)),
        ],
        out_specs=pl.BlockSpec((T, D), lambda j: (j, 0)),
        out_shape=jax.ShapeDtypeStruct((rows + extra, D), bf16),
        compiler_params=params(),
        cost_estimate=cost(6 * rows * D, 4 * rows * D),
    )(hid, rim, gain)


def states_kernel(xbc, halo, cw, hp, x, pre, bc, s, dt, ld, ldt, st0, comb, dec, pad, tail, carry, xw):
    j = pl.program_id(0)
    m, b = j // 2, j % 2
    before = jnp.where(b == 0, halo[pl.ds(8 * m, 8), :XC], tail[...])
    pad[0:8] = before
    pad[8 : 8 + T] = xbc[:, :XC]
    tail[...] = xbc[T - 8 : T, :XC]
    step = softplus(xbc[:, XC:XP] + hp[0:1, :])
    step = jnp.where(iota((T, 128), 1) < HH, step, 0.0)
    logd = masked_sums(iota((T, T), 0) >= iota((T, T), 1), -hp[1:2, :] * step)
    dt[...] = step
    ld[...] = logd
    ldt[0] = logd.T[:32]
    tailw = jnp.exp(logd[T - 1 : T] - logd) * step
    lanes = slice(W, XC)
    a = conv_taps(pad, cw, lanes)
    pre[:, lanes] = a
    act = a * lax.logistic(a)
    bc[...] = act
    s[...] = fine(nt, act[:, N:], act[:, :N])
    for i in range(W // 128):
        lanes = slice(128 * i, 128 * i + 128)
        a = conv_taps(pad, cw, lanes)
        pre[:, lanes] = a
        act_x = a * lax.logistic(a)
        x[:, lanes] = act_x
        xw[:, lanes] = (act_x * spread(tailw, 2 * i, 2)).astype(bf16)
    st = tn(act[:, :N].astype(bf16), xw[...])
    last = jnp.exp(logd[T - 8 : T])
    decay = jnp.concatenate([spread(last, 4 * i, 4) for i in range(W // 256)], axis=1)[7:8]
    dec[0] = jnp.broadcast_to(decay, (8, W))

    @pl.when(b == 0)
    def _():
        st0[0] = st
        carry[...] = st

    @pl.when(b == 1)
    def _():
        comb[0] = (decay * carry[...] + st).astype(bf16)


def block_states(xbc, cw, hp, micros):
    blocks = 2 * micros
    rows = blocks * T
    blk = lambda j: (j % 2) * micros + j // 2
    out = lambda *sh: jax.ShapeDtypeStruct(sh, f32)
    whole = lambda a: pl.BlockSpec(a.shape, lambda j: (0, 0))
    return pl.pallas_call(
        states_kernel,
        name="block_states",
        grid=(blocks,),
        in_specs=[
            pl.BlockSpec((T, XP), lambda j: (blk(j), 0)),
            pl.BlockSpec((8 * micros, XP), lambda j: (rows // (8 * micros), 0)),
            whole(cw),
            whole(hp),
        ],
        out_specs=[
            pl.BlockSpec((T, W), lambda j: (blk(j), 0)),
            pl.BlockSpec((T, XC), lambda j: (blk(j), 0)),
            pl.BlockSpec((T, 2 * N), lambda j: (blk(j), 0)),
            pl.BlockSpec((T, T), lambda j: (blk(j), 0)),
            pl.BlockSpec((T, 128), lambda j: (blk(j), 0)),
            pl.BlockSpec((T, 128), lambda j: (blk(j), 0)),
            pl.BlockSpec((1, 32, T), lambda j: (blk(j), 0, 0)),
            pl.BlockSpec((1, N, W), lambda j: (j // 2, 0, 0)),
            pl.BlockSpec((1, N, W), lambda j: (j // 2, 0, 0)),
            pl.BlockSpec((1, 8, W), lambda j: (blk(j), 0, 0)),
        ],
        out_shape=[
            out(rows, W),
            out(rows, XC),
            out(rows, 2 * N),
            out(rows, T),
            out(rows, 128),
            out(rows, 128),
            out(blocks, 32, T),
            out(micros, N, W),
            jax.ShapeDtypeStruct((micros, N, W), bf16),
            out(blocks, 8, W),
        ],
        scratch_shapes=[
            pltpu.VMEM((T + 8, XC), f32),
            pltpu.VMEM((8, XC), f32),
            pltpu.VMEM((N, W), f32),
            pltpu.VMEM((T, W), bf16),
        ],
        compiler_params=params(),
        cost_estimate=cost(blocks * 2 * T * N * W, rows * (XP + W + 800) * 4, rows * XC * 2),
    )(xbc, xbc, cw, hp)


def inner_kernel(s, ld, ldt, dt, x, skip, y):
    g = pl.program_id(1)
    shift = lax.rem(128 - 24 * g, 128)
    logd = pltpu.roll(ld[...], shift, 1) * LOG2E
    step = pltpu.roll(dt[...], shift, 1)
    upper = iota((HT, HT), 0) >= iota((HT, HT), 1)
    lower = iota((HT, T), 0) + HT >= iota((HT, T), 1)
    head = iota((T, 256), 1) // PS
    for q in range(6):
        lanes = slice(256 * q, 256 * q + 256)
        tile = x[:, lanes]
        xdt = tile * spread(step, 4 * q, 4)
        top = skip[0:1, lanes] * tile[:HT]
        bottom = skip[0:1, lanes] * tile[HT:]
        for i in range(4):
            h = 4 * q + i
            row = ldt[0, pl.ds(24 * g + h, 1), :] * LOG2E
            col = logd[:, h : h + 1]
            mine = jnp.where(head == i, xdt, 0.0).astype(bf16)
            decay = jnp.exp2(jnp.where(upper, col[:HT] - row[:, :HT], NEG))
            top = top + nn((decay * s[:HT, :HT]).astype(bf16), mine[:HT])
            decay = jnp.exp2(jnp.where(lower, col[HT:] - row, NEG))
            bottom = bottom + nn((decay * s[HT:, :]).astype(bf16), mine)
        y[:HT, lanes] = top
        y[HT:, lanes] = bottom


def inner_part(s, ld, ldt, dt, x, skip_row):
    rows = x.shape[0]
    blocks, groups = rows // T, W // 1536
    return pl.pallas_call(
        inner_kernel,
        name="inner_part",
        grid=(blocks, groups),
        in_specs=[
            pl.BlockSpec((T, T), lambda j, g: (j, 0)),
            pl.BlockSpec((T, 128), lambda j, g: (j, 0)),
            pl.BlockSpec((1, 32, T), lambda j, g: (j, 0, 0)),
            pl.BlockSpec((T, 128), lambda j, g: (j, 0)),
            pl.BlockSpec((T, 1536), lambda j, g: (j, g)),
            pl.BlockSpec((8, 1536), lambda j, g: (0, g)),
        ],
        out_specs=pl.BlockSpec((T, 1536), lambda j, g: (j, g)),
        out_shape=jax.ShapeDtypeStruct((rows, W), f32),
        compiler_params=params(),
        cost_estimate=cost(
            blocks * HH * 2 * T * T * 256, rows * (2 * W + 1024) * 4, blocks * HH * T * T
        ),
    )(s, ld, ldt, dt, x, skip_row)


def gate_kernel(yin, bc, e, ld, z, y, sums):
    grow = jnp.exp(ld[...])
    cst = bc[:, N:].astype(bf16)
    squares = jnp.zeros((T, 256), f32)
    for i in range(W // 256):
        lanes = slice(256 * i, 256 * i + 256)
        out = yin[:, lanes] + spread(grow, 4 * i, 4) * nn(cst, e[0, :, lanes])
        y[:, lanes] = out
        zt = z[:, lanes]
        g = out * (zt * lax.logistic(zt))
        squares = squares + g * g
    sums[...] = jnp.broadcast_to(jnp.sum(squares, axis=1, keepdims=True), (T, 128))


def gate_part(yin, bc, e, ld, z):
    rows = yin.shape[0]
    blocks = rows // T
    row = lambda c: pl.BlockSpec((T, c), lambda j: (j, 0))
    return pl.pallas_call(
        gate_kernel,
        name="gate_part",
        grid=(blocks,),
        in_specs=[
            row(W),
            row(2 * N),
            pl.BlockSpec((1, N, W), lambda j: (j, 0, 0)),
            row(128),
            row(W),
        ],
        out_specs=[row(W), row(128)],
        out_shape=[
            jax.ShapeDtypeStruct((rows, W), f32),
            jax.ShapeDtypeStruct((rows, 128), f32),
        ],
        input_output_aliases={0: 0},
        compiler_params=params(),
        cost_estimate=cost(2 * rows * N * W, rows * W * 4 * 3, rows * W * 2),
    )(yin, bc, e, ld, z)


def out_back_kernel(cot, w, exact, gfin, dots):
    g = nt(cot[...], w[...])
    gfin[...] = g
    dots[...] = jnp.broadcast_to(jnp.sum(g * exact[...], axis=1, keepdims=True), dots.shape)


def out_back(cot, w, exact):
    rows = cot.shape[0]
    row = lambda c: pl.BlockSpec((T, c), lambda j: (j, 0))
    return pl.pallas_call(
        out_back_kernel,
        name="out_back",
        grid=(rows // T,),
        in_specs=[row(D), pl.BlockSpec((W, D), lambda j: (0, 0)), row(W)],
        out_specs=[row(W), row(128)],
        out_shape=[jax.ShapeDtypeStruct((rows, W), f32), jax.ShapeDtypeStruct((rows, 128), f32)],
        compiler_params=params(),
        cost_estimate=cost(2 * rows * D * W, rows * W * 10 + 2 * D * W),
    )(cot, w, exact)


def gate_back_kernel(
    y, z, gfin, x, sums, dots, bc, e, ld, gain, skip, dec, dz, dy, dc, de1, given, dl, ggain, gskip, dye, keep
):
    j = pl.program_id(0)

    @pl.when(j == 0)
    def _():
        ggain[...] = jnp.zeros_like(ggain)
        gskip[...] = jnp.zeros_like(gskip)

    r = lax.rsqrt(sums[:, 0:1] * (1.0 / DI) + EPS)
    coef = r * r * dots[:, 0:1] * (1.0 / DI)
    grow = jnp.exp(ld[...])
    dlog = jnp.zeros((T, 128), f32)
    dcs = jnp.zeros((T, N), f32)
    for i in range(W // 256):
        lanes = slice(256 * i, 256 * i + 256)
        zt, yt, gf = z[:, lanes], y[:, lanes], gfin[:, lanes]
        sg = lax.logistic(zt)
        silu = zt * sg
        g = yt * silu
        gr = g * r
        ggain[0:1, lanes] += row_sum(gf * gr)
        dg = r * (gf * gain[0:1, lanes]) - g * coef
        dyt = dg * silu
        dz[:, lanes] = (dg * yt * (sg * (1.0 + zt * (1.0 - sg)))).astype(bf16)
        dy[:, lanes] = dyt.astype(bf16)
        xt = x[:, lanes]
        gskip[0:1, lanes] += row_sum(dyt * xt)
        dlog = dlog + per_head(dyt * (yt - skip[0:1, lanes] * xt), 4 * i)
        high, low = halves(dyt * spread(grow, 4 * i, 4))
        dye[:, lanes] = high
        dcs = dcs + (nt(high, e[0, :, lanes]) + nt(low, e[0, :, lanes]))
    dl[...] = dlog
    dc[...] = dcs
    de = tn(bc[:, N:].astype(bf16), dye[...])

    @pl.when(j % 2 == 0)
    def _():
        de1[0] = de
        keep[...] = de

    @pl.when(j % 2 == 1)
    def _():
        given[0] = (de + dec[0, 0:1] * keep[...]).astype(bf16)


def gate_back(y, z, gfin, x, sums, dots, bc, e, ld, gain, skip_row, dec, micros):
    rows = y.shape[0]
    blocks = rows // T
    blk = lambda p: (1 - p % 2) * micros + p // 2
    row = lambda c: pl.BlockSpec((T, c), lambda p: (blk(p), 0))
    fixed = pl.BlockSpec((8, W), lambda p: (0, 0))
    state = pl.BlockSpec((1, N, W), lambda p: (blk(p), 0, 0))
    chip = pl.BlockSpec((1, N, W), lambda p: (p // 2, 0, 0))
    sh = jax.ShapeDtypeStruct
    return pl.pallas_call(
        gate_back_kernel,
        name="gate_back",
        grid=(blocks,),
        in_specs=[
            row(W), row(W), row(W), row(W), row(128), row(128), row(2 * N), state, row(128),
            fixed, fixed, pl.BlockSpec((1, 8, W), lambda p: (blk(p), 0, 0)),
        ],
        out_specs=[row(W), row(W), row(N), chip, chip, row(128), fixed, fixed],
        out_shape=[
            sh((rows, W), bf16),
            sh((rows, W), bf16),
            sh((rows, N), f32),
            sh((micros, N, W), f32),
            sh((micros, N, W), bf16),
            sh((rows, 128), f32),
            sh((8, W), f32),
            sh((8, W), f32),
        ],
        scratch_shapes=[pltpu.VMEM((T, W), bf16), pltpu.VMEM((N, W), f32)],
        compiler_params=params(),
        cost_estimate=cost(8 * rows * N * W, rows * W * 24, rows * W * 2),
    )(y, z, gfin, x, sums, dots, bc, e, ld, gain, skip_row, dec)


def inner_back_kernel(s, bc, ld, ldt, dt, x, dy, skip, dx, xv, dbc, st, dst):
    g = pl.program_id(1)

    @pl.when(g == 0)
    def _():
        st[...] = s[...].T
        dst[...] = jnp.zeros_like(dst)
        xv[...] = jnp.zeros_like(xv)

    shift = lax.rem(128 - 24 * g, 128)
    logd = pltpu.roll(ld[...], shift, 1) * LOG2E
    step = pltpu.roll(dt[...], shift, 1)
    early = iota((HT, T), 1) >= iota((HT, T), 0)
    late = iota((HT, HT), 1) >= iota((HT, HT), 0)
    head = iota((T, 256), 1) // PS
    gtop = jnp.zeros((HT, T), f32)
    gbottom = jnp.zeros((HT, HT), f32)
    sums = jnp.zeros((T, 128), f32)
    for q in range(6):
        lanes = slice(256 * q, 256 * q + 256)
        steps = spread(step, 4 * q, 4)
        tile = x[:, lanes]
        xdt = tile * steps
        dyt = dy[:, lanes]
        top = jnp.zeros((HT, 256), f32)
        bottom = jnp.zeros((HT, 256), f32)
        for i in range(4):
            h = 4 * q + i
            row = ldt[0, pl.ds(24 * g + h, 1), :] * LOG2E
            col = logd[:, h : h + 1]
            dmine = jnp.where(head == i, dyt, jnp.zeros_like(dyt))
            xmine = jnp.where(head == i, xdt, 0.0).astype(bf16)
            decay = jnp.exp2(jnp.where(early, row - col[:HT], NEG))
            top = top + nn((decay * st[:HT, :]).astype(bf16), dmine)
            gtop = gtop + nt(xmine[:HT], dyt) * decay
            decay = jnp.exp2(jnp.where(late, row[:, HT:] - col[HT:], NEG))
            bottom = bottom + nn((decay * st[HT:, HT:]).astype(bf16), dmine[HT:])
            gbottom = gbottom + nt(xmine[HT:], dyt[HT:]) * decay
        total = jnp.concatenate([top, bottom], axis=0)
        dx[:, lanes] = total * steps + skip[0:1, lanes] * dyt.astype(f32)
        sums = sums + per_head(tile * total, 24 * g + 4 * q)
    xv[...] += sums
    dst[:HT, :] += gtop
    dst[HT:, HT:] += gbottom

    @pl.when(g == pl.num_programs(1) - 1)
    def _():
        dbc[:, :N] = fine(nn, dst[...], bc[:, N:])
        dbc[:, N:] = fine(tn, dst[...], bc[:, :N])


def inner_back(s, bc, ld, ldt, dt, x, dy, skip_row):
    rows = x.shape[0]
    blocks, groups = rows // T, W // 1536
    row = lambda c: pl.BlockSpec((T, c), lambda j, g: (j, 0))
    tile = pl.BlockSpec((T, 1536), lambda j, g: (j, g))
    sh = jax.ShapeDtypeStruct
    return pl.pallas_call(
        inner_back_kernel,
        name="inner_back",
        grid=(blocks, groups),
        in_specs=[
            row(T),
            row(2 * N),
            row(128),
            pl.BlockSpec((1, 32, T), lambda j, g: (j, 0, 0)),
            row(128),
            tile,
            tile,
            pl.BlockSpec((8, 1536), lambda j, g: (0, g)),
        ],
        out_specs=[tile, row(128), row(2 * N)],
        out_shape=[sh((rows, W), f32), sh((rows, 128), f32), sh((rows, 2 * N), f32)],
        scratch_shapes=[pltpu.VMEM((T, T), f32), pltpu.VMEM((T, T), f32)],
        compiler_params=params(),
        cost_estimate=cost(
            2 * blocks * HH * 2 * T * T * 256, rows * (2 * W + 1024) * 4, blocks * HH * T * T
        ),
    )(s, bc, ld, ldt, dt, x, dy, skip_row)


def conv_back_kernel(
    micros, xbc, prev, pre, dxi, xv, dbc, bc, dt, ld, later1, de1, dec, e, dc, dla, cw, hp,
    gp, gcw, ghp, pad, dpre, nxt, edge,
):
    p = pl.program_id(0)
    b = 1 - p % 2

    @pl.when(p == 0)
    def _():
        gcw[...] = jnp.zeros_like(gcw)
        ghp[...] = jnp.zeros_like(ghp)

    @pl.when(p == 2 * micros)
    def _():
        gp[0 : 8 * micros] = edge[...].astype(bf16)

    @pl.when(p < 2 * micros)
    def _():
        pad[0:8] = prev[:, :XC]
        pad[8 : 8 + T] = xbc[:, :XC]
        dpre[0:8] = jnp.zeros((8, XC), f32)
        dpre[8 + T : 16 + T] = jnp.where(b == 1, 0.0, nxt[...])
        step, logd = dt[...], ld[...]
        fade = jnp.exp(logd[T - 1 : T] - logd)
        tailw = fade * step
        bst = bc[:, :N].astype(bf16)

        def through_conv(grad, lanes, a, sg):
            d = grad * (sg * (1.0 + a * (1.0 - sg)))
            dpre[8 : 8 + T, lanes] = d
            gcw[4:5, lanes] += row_sum(d)
            for k in range(KC):
                gcw[k : k + 1, lanes] += row_sum(d * pad[pl.ds(5 + k, T), lanes])
            total = cw[0:1, lanes] * dpre[pl.ds(11, T), lanes]
            rim = cw[0:1, lanes] * dpre[pl.ds(3, 8), lanes]
            for k in range(1, KC):
                total = total + cw[k : k + 1, lanes] * dpre[pl.ds(11 - k, T), lanes]
                rim = rim + cw[k : k + 1, lanes] * dpre[pl.ds(3 - k, 8), lanes]
            gp[:, lanes] = total.astype(bf16)
            nxt[:, lanes] = d[0:8]

            @pl.when(b == 0)
            def _():
                edge[pl.ds(pl.multiple_of(8 * (p // 2), 8), 8), lanes] = rim

        dw = jnp.zeros((T, 128), f32)
        dbs = jnp.zeros((T, N), f32)
        ddec = jnp.zeros((8, 128), f32)
        for i in range(W // 256):
            lanes = slice(256 * i, 256 * i + 256)
            lat = later1[0, :, lanes]
            earlier = de1[0, :, lanes] + dec[0, 0:1, lanes] * lat.astype(f32)
            lat = jnp.where(b == 1, lat, earlier.astype(bf16))
            spreadw = spread(tailw, 4 * i, 4)
            a = pre[:, lanes]
            sg = lax.logistic(a)
            xt = a * sg
            bl = nn(bst, lat)
            dw = dw + nn((xt * bl).astype(bf16), head_place(256, 4 * i))
            high, low = halves(xt * spreadw)
            dbs = dbs + (nt(high, lat) + nt(low, lat))
            both = row_sum(lat.astype(f32) * e[0, :, lanes].astype(f32))
            ddec = ddec + per_head(jnp.broadcast_to(both, (8, 256)), 4 * i)
            through_conv(dxi[:, lanes] + bl * spreadw, lanes, a, sg)
        a = pre[:, W:]
        both = jnp.concatenate([dbc[:, :N] + dbs, dbc[:, N:] + dc[...]], axis=1)
        through_conv(both, slice(W, XC), a, lax.logistic(a))
        q = dw * tailw
        dlog = dla[...] - step * xv[...] - q
        dlast = row_sum(q) + ddec[0:1] * jnp.exp(logd[T - 1 : T])
        dlog = dlog + jnp.where(iota((T, 128), 0) == T - 1, dlast, 0.0)
        dcum = masked_sums(iota((T, T), 1) >= iota((T, T), 0), dlog)
        dstep = xv[...] + dw * fade - hp[1:2, :] * dcum
        draw = dstep * lax.logistic(xbc[:, XC:XP] + hp[0:1, :])
        draw = jnp.where(iota((T, 128), 1) < HH, draw, 0.0)
        ghp[0:1] += row_sum(draw)
        ghp[1:2] -= row_sum(dcum * step)
        gp[:, XC:XP] = draw.astype(bf16)

        @pl.when(b == 0)
        def _():
            edge[pl.ds(pl.multiple_of(8 * (p // 2), 8), 8), XC:XP] = jnp.zeros((8, 128), f32)


def conv_back(xbc, pre, dxi, xv, dbc, bc, dt, ld, later1, de1, dec, e, dc, dla, cw, hp, micros):
    blocks = 2 * micros
    rows = blocks * T
    blk = lambda p: jnp.where(p < blocks, (1 - p % 2) * micros + p // 2, micros - 1)
    row = lambda c: pl.BlockSpec((T, c), lambda p: (blk(p), 0))
    whole = lambda a: pl.BlockSpec(a.shape, lambda p: (0, 0))
    state = pl.BlockSpec((1, N, W), lambda p: (blk(p), 0, 0))

    unit = lambda p: jnp.minimum(p // 2, micros - 1)
    chip = pl.BlockSpec((1, N, W), lambda p: (unit(p), 0, 0))

    def before(p):
        k = blk(p)
        return (jnp.where(k >= micros, (k - micros + 1) * (T // 8) - 1, rows // 8 + k), 0)

    return pl.pallas_call(
        functools.partial(conv_back_kernel, micros),
        name="conv_back",
        grid=(blocks + 1,),
        in_specs=[
            row(XP),
            pl.BlockSpec((8, XP), before),
            row(XC), row(W), row(128), row(2 * N), row(2 * N), row(128), row(128),
            chip, chip, pl.BlockSpec((1, 8, W), lambda p: (micros + unit(p), 0, 0)), state,
            row(N), row(128), whole(cw), whole(hp),
        ],
        out_specs=[
            pl.BlockSpec((T, XP), lambda p: (jnp.where(p < blocks, blk(p), blocks), 0)),
            pl.BlockSpec((8, XC), lambda p: (0, 0)),
            pl.BlockSpec((8, 128), lambda p: (0, 0)),
        ],
        out_shape=[
            jax.ShapeDtypeStruct((rows + 8 * micros, XP), bf16),
            jax.ShapeDtypeStruct((8, XC), f32),
            jax.ShapeDtypeStruct((8, 128), f32),
        ],
        scratch_shapes=[
            pltpu.VMEM((T + 8, XC), f32),
            pltpu.VMEM((T + 16, XC), f32),
            pltpu.VMEM((8, XC), f32),
            pltpu.VMEM((8 * micros, XP), f32),
        ],
        compiler_params=pltpu.CompilerParams(vmem_limit_bytes=58 * MB_),
        cost_estimate=cost(6 * rows * N * W, rows * W * 18, rows * XC * 2),
    )(xbc, xbc, pre, dxi, xv, dbc, bc, dt, ld, later1, de1, dec, e, dc, dla, cw, hp)


AXIS = {"z": Z, "l": "zl", "s": "s"}
RING = 4
CHIPS = 16


def hop(value, axis):
    n = RING if axis == "z" else 2
    return lax.ppermute(value, AXIS[axis], [(i, (i + 1) % n) for i in range(n)])


def fence(groups, *values):
    held = [{k: g.live[k] for k in g.live} for g in groups]
    held, values = lax.optimization_barrier((held, values))
    for g, h in zip(groups, held):
        g.live.update(h)
    return values


def after(groups, *values):
    values, _ = lax.optimization_barrier((values, [v for g in groups for v in g.sent]))
    for g in groups:
        g.sent = ()
    return values


def partly(group, names, *values):
    held = {k: group.live[k] for k in group.live if k[:-1] in names}
    held, values = lax.optimization_barrier((held, values))
    group.live.update(held)
    return values


class Moves:
    sent = ()

    def send(self, value, axis):
        self.sent = [*self.sent, value]
        return hop(value, axis)


WAYS = (("s", "l"), ("l", "s"))


def lanes_of(widths):
    return [slice(sum(widths[:c]), sum(widths[: c + 1])) for c in range(len(widths))]


def near(c, kl, ks):
    return (ks, kl) if c == 0 else (kl, ks)


class Gather(Moves):
    def __init__(self, own, widths, turns):
        self.widths, self.turns = widths, turns
        self.live = {"g0": own}
        self.n = 1
        self.parts = []

    def z(self):
        self.live[f"g{self.n}"] = self.send(self.live[f"g{self.n - 1}"], "z")
        self.n += 1

    def first(self, h):
        some = jnp.stack([self.live[f"g{k}"] for k in self.turns[h]], 0)
        for k in self.turns[h]:
            if k < self.n - 1 or self.n == RING:
                self.live.pop(f"g{k}")
        for c, lanes in enumerate(lanes_of(self.widths)):
            self.live[f"p{h}{c}"] = some[:, :, lanes]
            self.live[f"q{h}{c}"] = self.send(some[:, :, lanes], WAYS[c][0])

    def second(self, h):
        for c in range(2):
            more = jnp.concatenate([self.live.pop(f"p{h}{c}"), self.live.pop(f"q{h}{c}")], 0)
            self.parts += [more, self.send(more, WAYS[c][1])]

    def place(self, c, kz, kl, ks):
        ka, kb = near(c, kl, ks)
        h = [kz in t for t in self.turns].index(True)
        turn = self.turns[h]
        return (h * 2 + c) * 2 + kb, ka * len(turn) + turn.index(kz)


class RingLast(Moves):
    def __init__(self, own, widths):
        self.widths = widths
        self.live = {f"p{c}": own[None, :, lanes] for c, lanes in enumerate(lanes_of(widths))}
        self.parts = []

    def step(self, n):
        for c in range(2):
            p = self.live[f"p{c}"]
            self.live[f"p{c}"] = jnp.concatenate([p, self.send(p, WAYS[c][n])], 0)

    def z(self):
        if not self.parts:
            self.live["p"] = jnp.concatenate([self.live.pop("p0"), self.live.pop("p1")], 0)
            self.parts = [self.live["p"]]
        self.live["p"] = self.send(self.live["p"], "z")
        self.parts.append(self.live["p"])

    def place(self, c, kz, kl, ks):
        ka, kb = near(c, kl, ks)
        return kz, c * 4 + kb * 2 + ka


class Scatter(Moves):
    def __init__(self, widths, turns):
        self.widths, self.turns = widths, turns
        self.live = {}
        self.order = [k for t in turns for k in t]

    def load(self, parts):
        parts = iter(parts)
        for h in range(len(self.turns)):
            for c in range(2):
                self.live[f"k{h}{c}"] = next(parts)
                self.live[f"s{h}{c}"] = next(parts)

    def second(self, h):
        for c in range(2):
            self.live[f"r{h}{c}"] = self.send(self.live.pop(f"s{h}{c}"), WAYS[c][1])

    def first(self, h):
        n = len(self.turns[h])
        for c in range(2):
            got, kept = self.live.pop(f"r{h}{c}"), self.live.pop(f"k{h}{c}")
            self.live[f"m{h}{c}"] = got[:n].astype(f32) + kept[:n].astype(f32)
            give = (got[n:].astype(f32) + kept[n:].astype(f32)).astype(bf16)
            self.live[f"n{h}{c}"] = self.send(give, WAYS[c][0])

    def ring(self, k):
        h = [self.order[k] in t for t in self.turns].index(True)
        at = self.turns[h].index(self.order[k])
        if at == 0:
            self.live["w"] = jnp.concatenate(
                [self.live.pop(f"m{h}{c}") + self.live.pop(f"n{h}{c}").astype(f32) for c in range(2)], 2
            )
        total = self.live["w"][at]
        if k:
            total = total + self.live.pop("t").astype(f32)
        if k == RING - 1:
            self.live.pop("w")
            return total
        self.live["t"] = self.send(total.astype(bf16), "z")

    def place(self, c, kz, kl, ks):
        ka, kb = near(c, kl, ks)
        h = [kz in t for t in self.turns].index(True)
        turn = self.turns[h]
        return (h * 2 + c) * 2 + kb, ka * len(turn) + turn.index(kz)

    def shapes(self, r):
        return [
            jax.ShapeDtypeStruct((2 * len(t), r, w), bf16)
            for t in self.turns
            for w in self.widths
            for _ in range(2)
        ]


def move_kernel(table, r, out_of, where, *refs):
    sems = refs[-1]
    refs = refs[:-1]
    whole = refs[-1] if out_of else refs[0]
    arrays = refs[:-1] if out_of else refs[1:]
    copies = []
    for n, (array, entry, k, lanes) in enumerate(table):
        row = pl.multiple_of(where[k] * r, 16)
        place = whole.at[pl.ds(row, r), lanes]
        piece = arrays[array].at[entry]
        pair = (piece, place) if out_of else (place, piece)
        copies.append(pltpu.make_async_copy(*pair, sems.at[n]))
    for c in copies:
        c.start()
    for c in copies:
        c.wait()


def move(group, where, r, given, shapes, out_of):
    table = []
    for c, lanes in enumerate(lanes_of(group.widths)):
        for k in range(CHIPS):
            table.append((*group.place(c, k // 4, k // 2 % 2, k % 2), k, lanes))
    any_ = pl.BlockSpec(memory_space=pl.ANY)
    return pl.pallas_call(
        functools.partial(move_kernel, tuple(table), r, out_of),
        name="join" if out_of else "deal",
        in_specs=[pl.BlockSpec(memory_space=pltpu.SMEM)] + [any_] * len(given),
        out_specs=[any_] * len(shapes),
        out_shape=shapes,
        scratch_shapes=[pltpu.SemaphoreType.DMA((len(table),))],
        compiler_params=pltpu.CompilerParams(vmem_limit_bytes=MB_),
        cost_estimate=cost(0, 4 * CHIPS * r * sum(group.widths)),
    )(where, *given)


def join(group, where, r):
    shape = jax.ShapeDtypeStruct((CHIPS * r, sum(group.widths)), bf16)
    return move(group, where, r, group.parts, [shape], True)[0]


def deal(group, where, r, whole):
    group.load(move(group, where, r, [whole], group.shapes(r), False))


def swap(value, axis="c"):
    return lax.ppermute(value, axis, [(0, 1), (1, 0)])


def two(mine, other, at):
    return jnp.where(at == 0, jnp.stack([mine, other]), jnp.stack([other, mine]))


class Plain:
    def __init__(self, axes):
        self.axes = axes

    def gather(self, piece):
        return lax.all_gather(piece, self.axes, axis=0, tiled=True)

    def reduce(self, grad):
        return lax.psum_scatter(grad, self.axes, scatter_dimension=0, tiled=True).astype(f32)


def body(
    hidden, in_weight, out_weight, conv_weight, conv_bias, norm_gain, gate_gain,
    step_bias, decay_rate, skip_gain, cotangent,
):
    nz, nl, ns = lax.axis_size(Z), lax.axis_size("zl"), lax.axis_size("s")
    core = lax.axis_index("c")
    micros = hidden.shape[0]
    rows = micros * 2 * T
    r_in, r_out = in_weight.shape[0], out_weight.shape[0]
    r = 2 * r_in
    fast = (nz, nl, ns) == (RING, 2, 2) and r % 16 == 0 and r_out == r
    onward = [(i, i + 1) for i in range(ns - 1)]
    backward = [(i + 1, i) for i in range(ns - 1)]
    turn = [(a * 2 + b, b * 2 + a) for a in range(2) for b in range(2)]

    def cut(k):
        part = lambda at, width: lax.dynamic_slice_in_dim(in_weight, at + k * width, width, 1)
        steps = in_weight[:, DI + CONV :]
        steps = jnp.where(k == 0, steps[:, :HH], steps[:, HH:])
        return jnp.concatenate(
            [
                part(DI, W),
                in_weight[:, 2 * DI : 2 * DI + 2 * N],
                jnp.pad(steps, ((0, 0), (0, 128 - HH))),
                part(0, W),
            ],
            axis=1,
        )

    ours, theirs = cut(core), cut(1 - core)
    theirs, out_weight, hidden, cotangent = lax.optimization_barrier(
        (theirs, out_weight, hidden, cotangent)
    )
    chip_rows = two(ours, swap(theirs), core).reshape(r, -1)
    w_own = lax.ppermute(out_weight, ("za", "c"), turn)

    ins = Plain(ALL[:4])
    outs = Plain(("zb", "zl", "s", "za"))

    n_c = conv_bias.shape[0]
    packed = jnp.concatenate([conv_weight.T.reshape(-1), conv_bias, norm_gain, gate_gain])

    def spread_out(small, a, at):
        mine, other = (jnp.expand_dims(v, at) for v in (small, swap(small, a)))
        here = lax.axis_index(a) == 0
        return jnp.where(here, jnp.concatenate([mine, other], at), jnp.concatenate([other, mine], at))

    hid_own = hidden.reshape(micros, T, D)
    cot_own = cotangent.reshape(micros, T, D)
    hid_other, cot_other = swap(hid_own), swap(cot_own)

    def chip_tokens(mine, other):
        return two(mine, other, core).reshape(rows, D)

    def rim_of(tokens):
        return lax.ppermute(tokens.reshape(2, micros, T, D)[1, :, T - 8 :], "s", onward)

    if fast:
        back = jnp.arange(CHIPS)
        kz = (lax.axis_index(Z) - back // 4) % RING
        kl = (lax.axis_index("zl") - back // 2) % 2
        ks = (lax.axis_index("s") - back) % 2
        in_place = ((kz * 2 + kl) * 2 + ks).astype(jnp.int32)
        out_place = ((((kz % 2) * 2 + kl) * 2 + ks) * 2 + kz // 2).astype(jnp.int32)
        x_cols, z_cols, o_cols = (896, 1024), (768, 768), (768, 768)
        small = spread_out(packed, "za", 0)
        small = spread_out(small, "zb", 1)
        chip_rows, small = lax.optimization_barrier((chip_rows, small))
        halves_, ring_ = ((0, 1), (2, 3)), ((0, 1, 2, 3),)
        gx_ = Gather(chip_rows[:, :XP], x_cols, halves_)
        gz_ = Gather(chip_rows[:, XP:], z_cols, ring_)
        go_ = RingLast(w_own, o_cols)
        every = [gx_, gz_, go_]
        small = spread_out(small, "zl", 2)
        gx_.z()
        go_.step(0)
        small, hid_other, cot_other = fence(every, small, hid_other, cot_other)
        small = spread_out(small, "s", 3)
        gx_.z()
        gx_.first(0)
        hid_own_, hid_other = after(every, hid_own, hid_other)
        hid_all = chip_tokens(hid_own_, hid_other)
        rim = rim_of(hid_all)
        small = spread_out(small, "c", 4).reshape(-1, packed.shape[0])
        small, rim, hid_all = fence(every, small, rim, hid_all)
        gx_.z()
        gx_.second(0)
        gz_.z()
        small, rim, hid_all, cot_own_, cot_other = after(
            every, small, rim, hid_all, cot_own, cot_other
        )
        cot_all = chip_tokens(cot_own_, cot_other)
    else:
        small = lax.all_gather(packed, ALL)
        hid_all, cot_all = chip_tokens(hid_own, hid_other), chip_tokens(cot_own, cot_other)
        rim = rim_of(hid_all)
        w_x, w_z = ins.gather(chip_rows[:, :XP]), ins.gather(chip_rows[:, XP:])

    rim = jnp.where(iota(rim.shape, 1) >= 5, rim, jnp.zeros_like(rim)).reshape(8 * micros, D)
    devices = small.shape[0]
    taps = small[:, : KC * n_c].reshape(devices, KC, n_c).transpose(1, 0, 2).reshape(KC, CONV)
    bias = small[:, KC * n_c : (KC + 1) * n_c].reshape(1, CONV)
    norm_vec = small[:, (KC + 1) * n_c : (KC + 1) * n_c + r_in].reshape(D).astype(f32)
    gate_vec = small[:, (KC + 1) * n_c + r_in :].reshape(1, DI)
    conv_all = jnp.concatenate([taps, bias, jnp.zeros((3, CONV), bf16)], 0).astype(f32)
    cw = jnp.concatenate(
        [lax.dynamic_slice_in_dim(conv_all, core * W, W, 1), conv_all[:, DI:]], axis=1
    )
    gain = jnp.broadcast_to(lax.dynamic_slice_in_dim(gate_vec, core * W, W, 1).astype(f32), (8, W))
    heads = jnp.stack([step_bias, decay_rate, skip_gain])
    heads = lax.dynamic_slice_in_dim(heads, core * HH, HH, 1)
    hp = jnp.pad(heads, ((0, 5), (0, 128 - HH)))
    skip_row = jnp.broadcast_to(jnp.repeat(heads[2], PS)[None], (8, W))
    normed = pre_norm(hid_all, rim, norm_vec[None])
    if fast:
        normed, cot_all, cw, hp, gain, skip_row = fence(
            every, normed, cot_all, cw, hp, gain, skip_row
        )
        gx_.first(1)
        go_.step(1)
        gz_.z()
        (normed,) = fence([gx_, gz_], normed)
        gx_.second(1)
        gz_.z()
        (normed,) = after([gx_, gz_], normed)

    if fast:
        (normed,) = fence(every, normed)
        gz_.first(0)
        go_.z()
        (normed,) = after([gz_, go_], normed)
        w_x = join(gx_, in_place, r)
    xbc = nn(normed, w_x)
    if fast:
        (xbc,) = fence([gz_], xbc)
        gz_.second(0)
        (xbc,) = after([gz_], xbc)
        go_.live, xbc = lax.optimization_barrier((go_.live, xbc))
        go_.z()
        (xbc,) = after([go_], xbc)
    else:
        w_o = outs.gather(w_own)
    x, pre, bc, s, dt, ld, ldt, st0, comb, dec8 = block_states(xbc, cw, hp, micros)
    dec = dec8[:, 0].reshape(2, micros, 1, W)
    if fast:
        comb, s = lax.optimization_barrier((comb, s))
    if ns == 2:
        first = lax.ppermute(comb, "s", onward)
    else:
        first = jnp.zeros_like(comb)
        chip_decay = dec[0] * dec[1]
        for _ in range(ns - 1):
            out = (chip_decay * first.astype(f32) + comb.astype(f32)).astype(bf16)
            first = lax.ppermute(out, "s", onward)
    yin = inner_part(s, ld, ldt, dt, x, skip_row)
    if fast:
        (yin,) = fence([gz_, go_], yin)
        go_.z()
        (yin,) = after([go_], yin)
    second = (dec[0] * first.astype(f32) + st0).astype(bf16)
    entering = jnp.stack([first, second], 0).reshape(2 * micros, N, W)
    if fast:
        w_z = join(gz_, in_place, r)
    z = nn(normed[:rows], w_z)
    y, sums = gate_part(yin, bc, entering, ld, z)
    sums = sums + swap(sums)
    root = lax.rsqrt(sums[:, :1] * (1.0 / DI) + EPS)
    exact = y * (z * lax.logistic(z)) * root * gain[:1]
    fin = exact.astype(bf16)
    g_out = tn(fin, cot_all).astype(bf16)
    if fast:
        ring_back = ((1, 2, 3, 0),)
        so_ = Scatter(o_cols, ring_back)
        deal(so_, out_place, r, g_out)
        (cot_all,) = fence([so_], cot_all)
        so_.second(0)
        (cot_all,) = after([so_], cot_all)
        w_o = join(go_, out_place, r)

    gfin, dots = out_back(cot_all, w_o, exact)

    if fast:
        dots, gfin = fence([so_], dots, gfin)
        so_.first(0)
        (y,) = after([so_], y)
    dots = dots + swap(dots)
    dz, dy, dc, de1, given, dla, ggain, gskip = gate_back(
        y, z, gfin, x, sums, dots, bc, entering, ld, gain, skip_row, dec8, micros
    )
    if ns == 2:
        dz, given = lax.optimization_barrier((dz, given))
        later1 = lax.ppermute(given, "s", backward)
    else:
        later1 = jnp.zeros((micros, N, W), bf16)
        for _ in range(ns - 1):
            out = given.astype(f32) + dec[0] * dec[1] * later1.astype(f32)
            later1 = lax.ppermute(out.astype(bf16), "s", backward)
    gz = tn(normed[:rows], dz).astype(bf16)
    if fast:
        sz_ = Scatter(z_cols, ring_back)
        deal(sz_, in_place, r, gz)
        (dy,) = fence([so_, sz_], dy)
        so_.ring(0)
        sz_.second(0)
        (dy,) = after([so_, sz_], dy)

    dxi, xv, dbc = inner_back(s, bc, ld, ldt, dt, x, dy, skip_row)
    if fast:
        dxi, later1 = fence([so_, sz_], dxi, later1)
        so_.ring(1)
        sz_.first(0)
        (dxi,) = after([so_, sz_], dxi)
    gp, gcw, ghp = conv_back(
        xbc, pre, dxi, xv, dbc, bc, dt, ld, later1, de1, dec8, entering, dc, dla, cw, hp, micros
    )
    if fast:
        (gp,) = fence([so_, sz_], gp)
        so_.ring(2)
        sz_.ring(0)
        (gp,) = after([so_, sz_], gp)
    gx = tn(normed, gp).astype(bf16)

    wide = lambda v: jnp.pad(v, ((0, 0), (0, XC - v.shape[1])))
    tiny = jnp.concatenate(
        [gcw[:5], wide(ggain[:1]), wide(gskip[:1]), wide(ghp[:2].reshape(1, 256))], axis=0
    )
    if fast:
        sx_ = Scatter(x_cols, ((1, 2), (3, 0)))
        deal(sx_, in_place, r, gx)
        gp, tiny = fence([so_, sz_, sx_], gp, tiny)
        sx_.second(0)
        sz_.ring(1)
        gp, tiny = after([sx_, sz_], gp, tiny)
        tiny = tiny + swap(tiny, "zb")
        g_out = so_.ring(3)
    else:
        g_out = outs.reduce(g_out)
    g_out = lax.ppermute(g_out, ("za", "c"), turn)

    gn = nt(gp, w_x)
    edge = lax.ppermute(gn[rows:].astype(bf16), "s", backward).reshape(1, micros, 8, D)
    if fast:
        gn, dz, tiny = fence([sz_], gn, dz, tiny)
        tiny = tiny + swap(tiny, "za")
    gn = gn[:rows] + nt(dz, w_z)

    if fast:
        gn, g_out, tiny = fence([sz_, sx_], gn, g_out, tiny)
        sx_.first(0)
        sx_.second(1)
        sz_.ring(2)
        (gn,) = after([sx_, sz_], gn)
    gn = gn.reshape(2, micros, T, D)
    edge = jnp.where(iota(edge.shape, 2) >= 5, edge.astype(f32), 0.0)
    gn = gn + jnp.pad(edge, ((1, 0), (0, 0), (T - 8, 0), (0, 0)))
    give = lax.dynamic_index_in_dim(gn, 1 - core, 0, False).astype(bf16)
    keep = lax.dynamic_index_in_dim(gn, core, 0, False)
    other = swap(give)
    if fast:
        keep, other = partly(sx_, ("m0", "n0"), keep, other)
        sx_.ring(0)
        keep, other = after([sx_], keep, other)
    gn = keep + other.astype(f32)
    hid_f = hid_own.astype(f32)
    own_scale = lax.rsqrt(jnp.mean(hid_f * hid_f, axis=-1, keepdims=True) + EPS)
    unit = hid_f * own_scale
    gq = gn * norm_vec
    g_hid = cot_own.astype(f32) + own_scale * (
        gq - unit * jnp.mean(gq * unit, axis=-1, keepdims=True)
    )

    if fast:
        tiny, g_hid, fin = fence([sz_, sx_], tiny, g_hid, fin)
        sx_.first(1)
        sx_.ring(1)
        tiny, fin = after([sx_], tiny, fin)
        tiny = tiny + swap(tiny, "s")
        gz = sz_.ring(3)

    partial_out = nn(fin, w_o).reshape(2, micros, T, D)
    give = lax.dynamic_index_in_dim(partial_out, 1 - core, 0, False).astype(bf16)
    keep = lax.dynamic_index_in_dim(partial_out, core, 0, False)
    given_out = swap(give)
    block_out = (hid_own.astype(f32) + keep + given_out.astype(f32)).astype(bf16)

    def exchanged(g):
        g = g.reshape(2, r_in, -1)
        mine = lax.dynamic_index_in_dim(g, core, 0, False)
        return two(mine, swap(lax.dynamic_index_in_dim(g, 1 - core, 0, False)), core)

    if fast:
        tiny, gz, give, keep = fence([sx_], tiny, gz, give, keep)
        sx_.ring(2)
        tiny, gz = after([sx_], tiny, gz)
        gz = exchanged(gz)
        tiny = tiny + swap(tiny, "zl")
        tiny, gz = fence([sx_], tiny, gz)
        gx = sx_.ring(3)
    else:
        tiny = lax.psum(tiny, ALL[:4])
        gx, gz = ins.reduce(gx), ins.reduce(gz)
        gz = exchanged(gz)
    gx = exchanged(gx)
    both = two(tiny, swap(tiny), core)
    g_conv = jnp.concatenate([both[0, :5, :W], both[1, :5, :W], both[0, :5, W:] + both[1, :5, W:]], axis=1)
    me = lax.axis_index(ALL)
    g_conv = lax.dynamic_slice_in_dim(g_conv, me * n_c, n_c, 1)
    g_gate = both[:, 5, :W].reshape(-1)
    g_gate = lax.dynamic_slice_in_dim(g_gate, me * r_out, r_out)
    g_skip = both[:, 6, :W].reshape(H, PS).sum(-1)
    g_bias = both[:, 7, :HH].reshape(-1)
    g_rate = both[:, 7, 128 : 128 + HH].reshape(-1)
    g_in = jnp.concatenate(
        [
            gz[0], gz[1],
            gx[0, :, :W], gx[1, :, :W],
            gx[0, :, W:XC] + gx[1, :, W:XC],
            gx[0, :, XC : XC + HH], gx[1, :, XC : XC + HH],
        ],
        axis=1,
    )
    g_norm = jnp.sum(g_in * in_weight.astype(f32), axis=1) / norm_gain.astype(f32)
    return (
        block_out.reshape(hidden.shape),
        g_hid.reshape(hidden.shape),
        g_in,
        g_out,
        g_conv[:KC].T,
        g_conv[KC],
        g_norm,
        g_gate,
        g_bias,
        g_rate,
        g_skip,
    )


def solution(mesh):
    dp, seq = mesh.shape["dp"], mesh.shape["seq"]
    split = Mesh(mesh.devices.reshape(2, dp // 4, 2, seq // 2, 2), ALL)
    token = P(None, ("za", "zb", "zl"), ("s", "c"), None)
    in_specs = (token, P(ALL, None), P(ALL, None), P(ALL, None), P(ALL), P(ALL), P(ALL), P(), P(), P(), token)
    out_specs = (token, token, P(ALL, None), P(ALL, None), P(ALL, None), P(ALL), P(ALL), P(ALL), P(), P(), P())
    return jax.shard_map(body, mesh=split, in_specs=in_specs, out_specs=out_specs, check_vma=False)
```
